32 devices in a mesh: dom: 2 (over y), row: 4 (over z), sub: 2 (over x), rep: 2 (over core).
Axes of the slice: x: 2, y: 2, z: 4, core: 2. Of those that a mesh axis runs over, the one named last changes fastest.
Arguments:
- vectors: bfloat16 [28672, 768], P(('dom', 'row', 'sub', 'rep')), parts along dimension 0, may hold values from -150 to 150
- rotation: bfloat16 [1536, 768], P('dom'), parts along dimension 0, may hold values from -0.21875 to 0.21875
- codebooks: float32 [96, 256, 16], P(('dom', 'sub')), parts along dimension 0, may hold values from -8 to 8
Outputs:
- reconstruction: bfloat16 [28672, 768], P(('dom', 'row', 'sub', 'rep')), parts along dimension 0
- new_codebooks: float32 [96, 256, 16], P(('dom', 'sub')), parts along dimension 0
- cross_cov: float32 [1536, 768], P(('dom', 'sub')), parts along dimension 0
The draws below stay inside these ranges and needn't reach their ends.
There are 2 independent parts, one for each index of `dom`. The reference program is written for one: setup_inputs(seed, part) draws one part's arguments, and reference() takes and returns one part's arrays. A program takes and returns all parts, laid end to end along the dimension named above; each array names one. Nothing has to cross between parts.
All inputs are finite; a program needn't handle non-finite values.
Results may differ from the reference program's by a relative error of at most 0.012.
Values may be sent and summed in bfloat16 or wider, within the bound.
No kernel may reach another device: no remote copies, remote signals or barrier semaphores. Data moves between devices by JAX's collectives and lax.ppermute only.
A program may use at most 64 MiB of HBM per device.

```python
import jax
import jax.numpy as jnp
from jax import lax

SUBS = 48
SUBDIM = 16
CODES = 256
D = 768
TOTAL = 14336


def draw_vectors(key, part):
    first_key, followup_key = jax.random.split(jax.random.fold_in(key, 11))
    normal_part = jnp.clip(jax.random.normal(first_key, (TOTAL, D), jnp.float32), -6.0, 6.0)
    rising = 1.0 + 2.0 * jnp.arange(TOTAL, dtype=jnp.float32) / TOTAL
    row_scale = jnp.exp(jax.random.uniform(followup_key, (TOTAL, 1), jnp.float32, -0.5, 0.5)) * rising[:, None]
    return (normal_part * row_scale).astype(jnp.bfloat16)


def shard_levels(own_key, extent, cuts, smallest, high):
    factor_of, own = 1.0, jax.random.fold_in(own_key, 6)
    for position, parts in cuts:
        heights = jnp.exp(jax.random.uniform(jax.random.fold_in(own, position), (parts,), jnp.float32, smallest / len(cuts), high / len(cuts)))
        factor_of = factor_of * jnp.repeat(heights, extent[position] // parts).reshape([-1 if axis == position else 1 for axis in range(len(extent))])
    return factor_of


def gaussian(rng, dims, scale, most, cuts=(), held_as=jnp.bfloat16):
    result = scale * jax.random.normal(rng, dims, jnp.float32)
    if cuts:
        result = result * shard_levels(rng, dims, cuts, -0.22, 0.18)
    return jnp.clip(result, -most, most).astype(held_as)


def setup_inputs(seed: int = 0, part: int = 0) -> dict:
    keys = jax.random.split(jax.random.key(seed), 4)
    own_keys = jax.random.split(jax.random.fold_in(keys[3], part), 4)
    vectors = draw_vectors(jax.random.fold_in(jax.random.fold_in(keys[3], part), 71), part)
    rotation = gaussian(own_keys[1], (D, D), D ** -0.5, 0.21875)
    codebooks = gaussian(own_keys[2], (SUBS, CODES, SUBDIM), 1.5, 8.0, ((0, 2),), jnp.float32)
    return dict(vectors=vectors, rotation=rotation, codebooks=codebooks)


softness_scale = 4.0


def quantize_rows(block, codebook):
    cross_product = jnp.dot(codebook, block, precision=lax.Precision.HIGHEST)
    squared_norms = jnp.sum(codebook * codebook, axis=1)
    affinity_scores = (2.0 * cross_product - squared_norms[:, None]) / softness_scale
    weights = jax.nn.softmax(affinity_scores, axis=0)
    recon = jnp.dot(codebook.T, weights, precision=lax.Precision.HIGHEST)
    sums = lax.dot_general(weights, block, (((1,), (1,)), ((), ())), precision=lax.Precision.HIGHEST)
    counts = jnp.sum(weights, axis=1)
    return recon, sums, counts


def reference(vectors, rotation, codebooks):
    rotated = jnp.dot(vectors, rotation, preferred_element_type=jnp.float32).astype(jnp.bfloat16)
    blocks = rotated.astype(jnp.float32).reshape(TOTAL, SUBS, SUBDIM).transpose(1, 2, 0)
    recon, sums, counts = lax.map(lambda pair: quantize_rows(pair[0], pair[1]), (blocks, codebooks))
    reconstruction = recon.transpose(2, 0, 1).reshape(TOTAL, D).astype(jnp.bfloat16)
    new_codebooks = (sums + codebooks) / (counts[:, :, None] + 1.0)
    cross_cov = jnp.dot(vectors.T, reconstruction, preferred_element_type=jnp.float32) / TOTAL
    return reconstruction, new_codebooks, cross_cov
```

```python
import functools
import math

import jax
import jax.numpy as jnp
from jax import lax
from jax.experimental import pallas as pl
from jax.experimental.pallas import tpu as pltpu
from jax.sharding import PartitionSpec as P

SUBDIM = 16
SOFTNESS = 4.0
LOG2E = math.log2(math.e)
F32, BF16 = jnp.float32, jnp.bfloat16
GROUP = 4
VMEM_BYTES = 56 * 2**20


def quantize_rows(block, codebook):
    block = block.astype(F32)
    cross_product = jnp.dot(codebook, block, precision=lax.Precision.HIGHEST)
    squared_norms = jnp.sum(codebook * codebook, axis=1)
    affinity_scores = (2.0 * cross_product - squared_norms[:, None]) / SOFTNESS
    weights = jax.nn.softmax(affinity_scores, axis=0)
    recon = jnp.dot(codebook.T, weights, precision=lax.Precision.HIGHEST)
    sums = lax.dot_general(weights, block, (((1,), (1,)), ((), ())), precision=lax.Precision.HIGHEST)
    return recon, sums, jnp.sum(weights, axis=1)


def any_mesh(vectors, rotation, codebooks):
    rows, width = vectors.shape
    groups = lax.axis_size("sub")
    part = width // groups
    rotated_t = lax.dot_general(
        rotation, vectors, (((0,), (1,)), ((), ())), preferred_element_type=F32
    ).astype(BF16)
    received = lax.all_to_all(rotated_t.reshape(groups, part, rows), "sub", split_axis=0, concat_axis=2, tiled=True)
    columns = received.shape[2]
    blocks = received.reshape(part // SUBDIM, SUBDIM, columns)
    recon, sums, counts = lax.map(lambda pair: quantize_rows(pair[0], pair[1]), (blocks, codebooks))
    sent = recon.astype(BF16).reshape(1, part, columns)
    recon_t = lax.all_to_all(sent, "sub", split_axis=2, concat_axis=0, tiled=True).reshape(width, rows)
    total = rows * lax.axis_size("row") * groups * lax.axis_size("rep")
    sums, counts = lax.psum((sums, counts), ("row", "rep"))
    term = lax.dot_general(vectors, recon_t, (((0,), (1,)), ((), ())), preferred_element_type=F32)
    whole = lax.psum(term, ("row", "sub", "rep"))
    mine = lax.dynamic_slice_in_dim(whole, lax.axis_index("sub") * part, part, 0)
    return recon_t.T, (sums + codebooks) / (counts[:, :, None] + 1.0), mine / total


def rotate_kernel(vec_ref, rot_ref, y_ref, rott_ref):
    s, r = lax.axis_index("sub"), lax.axis_index("rep")
    n, w = y_ref.shape[0], y_ref.shape[1]
    turned = rot_ref[...].T
    for h in range(n):
        for q in range(2):
            @pl.when(r == q)
            def _():
                rott_ref[(h + n - s) % n] = turned[(2 * h + q) * w : (2 * h + q + 1) * w]
    for k in range(n):
        y_ref[k] = lax.dot_general(
            rott_ref[k], vec_ref[...], (((1,), (1,)), ((), ())), preferred_element_type=F32
        ).astype(BF16)


def rotate_more_kernel(vec_ref, rott_ref, y_ref):
    for k in range(y_ref.shape[0]):
        y_ref[k] = lax.dot_general(
            rott_ref[k], vec_ref[...], (((1,), (1,)), ((), ())), preferred_element_type=F32
        ).astype(BF16)


def operands(c):
    codes = c.shape[1]
    scaled = c * (2.0 / SOFTNESS * LOG2E)
    hi = scaled.astype(BF16).astype(F32)
    mid = (scaled - hi).astype(BF16).astype(F32)
    lo = (scaled - hi) - mid
    n = jnp.sum(c * c, axis=0, keepdims=True) * (-LOG2E / SOFTNESS)
    n_hi = n.astype(BF16).astype(F32)
    n_mid = (n - n_hi).astype(BF16).astype(F32)
    n_lo = (n - n_hi) - n_mid
    row = lax.broadcasted_iota(jnp.int32, (SUBDIM, codes), 0)
    norms = jnp.where(row == 0, n_hi, jnp.where(row == 1, n_mid, jnp.where(row == 2, n_lo, 0.0)))
    a = jnp.concatenate([hi, mid, lo, norms], axis=0).T.astype(BF16)
    c_hi = c.astype(BF16)
    c_lo = (c - c_hi.astype(F32)).astype(BF16)
    b = jnp.concatenate([c_hi, c_lo, jnp.ones((SUBDIM, codes), BF16)], axis=0)
    return a, b


def quantize_kernel(cb_ref, y0_ref, y1_ref, v0_hbm, v1_hbm, rec0_ref, rec1_ref, keep_ref, send_ref,
                    v0, v1, cnt, sem0, sem1, *, k, per):
    step, steps = pl.program_id(0), pl.num_programs(0)
    s, r = lax.axis_index("sub"), lax.axis_index("rep")
    codes = cb_ref.shape[2]
    cols = y0_ref.shape[2]
    w = per * SUBDIM
    lanes = 128
    part = v0.shape[1] // 2
    base = r * per if k == 0 else 0
    p_rows = (part // lanes) * w
    sums_ref = keep_ref if k == 0 else send_ref

    @pl.when(step == 0)
    def _():
        pltpu.make_async_copy(v0_hbm, v0, sem0).start()
        pltpu.make_async_copy(v1_hbm, v1, sem1).start()
        cnt[...] = jnp.zeros_like(cnt)

    ab = [operands(cb_ref[base + step * GROUP + j]) for j in range(GROUP)]
    acc = [jnp.zeros((2 * SUBDIM, codes), F32) for _ in range(GROUP)]
    ys, recs = (y0_ref, y1_ref), (rec0_ref, rec1_ref)
    ones = jnp.ones((SUBDIM, cols), BF16)

    def score(j, i):
        y = ys[i][0, SUBDIM * j : SUBDIM * (j + 1), :]
        return y, jnp.dot(ab[j][0], jnp.concatenate([y, y, y, ones], axis=0), preferred_element_type=F32)

    def spread(sc):
        return jnp.exp2(sc - jnp.max(sc, axis=0, keepdims=True)).astype(BF16)

    def finish(j, i, y, e):
        out = jnp.dot(ab[j][1], e, preferred_element_type=F32)
        inv = 1.0 / out[2 * SUBDIM :]
        at = pl.multiple_of(step * (GROUP * SUBDIM), GROUP * SUBDIM) + SUBDIM * j
        recs[i][pl.ds(pl.multiple_of(at, SUBDIM), SUBDIM), :] = (
            (out[:SUBDIM] + out[SUBDIM : 2 * SUBDIM]) * inv
        ).astype(BF16)
        yz = jnp.concatenate([(y.astype(F32) * inv).astype(BF16), inv.astype(BF16)], axis=0)
        acc[j] = acc[j] + lax.dot_general(yz, e, (((1,), (1,)), ((), ())), preferred_element_type=F32)

    work = [(j, i) for j in range(GROUP) for i in range(2)]
    first = second = None
    for item in work + [None, None]:
        new_first = (item, *score(*item)) if item is not None else None
        new_second = (first[0], first[1], spread(first[2])) if first is not None else None
        if second is not None:
            finish(*second[0], second[1], second[2])
        first, second = new_first, new_second

    for j in range(GROUP):
        m = step * GROUP + j
        for half in range(codes // lanes):
            at = p_rows + half * w + m * SUBDIM
            sums_ref[pl.ds(pl.multiple_of(at, SUBDIM), SUBDIM), :] = acc[j][
                :SUBDIM, half * lanes : (half + 1) * lanes
            ].astype(sums_ref.dtype)
            cnt[pl.ds(half * SUBDIM + m, 1), :] = acc[j][SUBDIM : SUBDIM + 1, half * lanes : (half + 1) * lanes]

    @pl.when(step == steps - 1)
    def _():
        at = p_rows + (codes // lanes) * w
        sums_ref[at : at + cnt.shape[0], :] = cnt[...].astype(sums_ref.dtype)
        pltpu.make_async_copy(v0_hbm, v0, sem0).wait()
        pltpu.make_async_copy(v1_hbm, v1, sem1).wait()
        cross = jnp.dot(rec0_ref[...], v0[...], preferred_element_type=F32) + jnp.dot(
            rec1_ref[...], v1[...], preferred_element_type=F32
        )
        for h in range(2):
            @pl.when(s == h)
            def _():
                for g in range(part // lanes):
                    near = h * part + g * lanes
                    far = (1 - h) * part + g * lanes
                    keep_ref[g * w : (g + 1) * w, :] = cross[:, near : near + lanes]
                    send_ref[g * w : (g + 1) * w, :] = cross[:, far : far + lanes].astype(BF16)


def turn_kernel(m0_ref, m1_ref, t0_ref, t1_ref, out_ref, buf):
    s, r = lax.axis_index("sub"), lax.axis_index("rep")
    w = m0_ref.shape[0]
    for k, (mine, theirs) in enumerate(((m0_ref, t0_ref), (m1_ref, t1_ref))):
        h = (s + k) % 2
        buf[pl.ds(pl.multiple_of((2 * h + r) * w, SUBDIM), w), :] = mine[...]
        buf[pl.ds(pl.multiple_of((2 * h + 1 - r) * w, SUBDIM), w), :] = theirs[...]
    out_ref[...] = buf[...].T


def final_kernel(mine_ref, theirs_ref, cb_ref, cross_ref, new_ref, buf, *, per, total):
    s, r, z = lax.axis_index("sub"), lax.axis_index("rep"), lax.axis_index("row")
    n = mine_ref.shape[0]
    piece = mine_ref.shape[1]
    lanes = 128
    w = per * SUBDIM
    codes = cb_ref.shape[2]
    groups = cross_ref.shape[0] // lanes
    halves = codes // lanes
    for side, ref in enumerate((mine_ref, theirs_ref)):
        for d in range(n):
            at = ((z + n - d) % n) * piece
            buf[side, pl.ds(pl.multiple_of(at, SUBDIM), piece), :] = ref[d].astype(F32)
    a_rows = groups * w + halves * (w + SUBDIM)
    for g in range(groups):
        for h in range(2):
            for q in range(2):
                @pl.when((s == h) & (r == q))
                def _():
                    pieces = []
                    for col in range(2):
                        k = col ^ h
                        for rep in range(2):
                            start = k * a_rows + g * w
                            pieces.append(buf[rep ^ q, start : start + w, :])
                    cross_ref[g * lanes : (g + 1) * lanes, :] = jnp.concatenate(pieces, axis=0).T * (1.0 / total)
    first = groups * w
    for side in range(2):
        part = r if side == 0 else 1 - r
        for m in range(per):
            c = cb_ref[part * per + m]
            sums = jnp.concatenate(
                [buf[side, first + hf * w + m * SUBDIM : first + hf * w + (m + 1) * SUBDIM, :] for hf in range(halves)],
                axis=1,
            )
            at = first + halves * w + m
            count = jnp.concatenate([buf[side, at + hf * SUBDIM : at + hf * SUBDIM + 1, :] for hf in range(halves)], axis=1)
            new_ref[part * per + m] = (sums + c) / (count + 1.0)


def shifts(x, n, d):
    return lax.ppermute(x, "row", [(i, (i + d) % n) for i in range(n)])


def on_device(vectors, rotation, codebooks):
    rows, width = vectors.shape
    subs, rows_n = 2, lax.axis_size("row")
    part = width // subs
    per = part // SUBDIM // 2
    w = per * SUBDIM
    codes = codebooks.shape[1]
    lanes = 128
    steps = per // GROUP
    total = rows * rows_n * subs * 2
    swap = [(0, 1), (1, 0)]
    r, z = lax.axis_index("rep"), lax.axis_index("row")
    params = pltpu.CompilerParams(vmem_limit_bytes=VMEM_BYTES)
    vmem = pl.BlockSpec(memory_space=pltpu.VMEM)

    cb = codebooks.transpose(0, 2, 1)
    cb_far = lax.ppermute(lax.dynamic_slice_in_dim(cb, r * per, per, 0), "sub", swap)
    vec_far = lax.ppermute(vectors, "rep", swap)

    y_shape = jax.ShapeDtypeStruct((subs, w, rows), BF16)
    y0, rott = pl.pallas_call(
        rotate_kernel,
        out_shape=(y_shape, jax.ShapeDtypeStruct((subs, w, width), BF16)),
        in_specs=[vmem] * 2,
        out_specs=(vmem, vmem),
        compiler_params=params,
        name="rotate",
    )(vectors, rotation)
    y1 = pl.pallas_call(
        rotate_more_kernel, out_shape=y_shape, in_specs=[vmem] * 2, out_specs=vmem, compiler_params=params, name="rotate_far"
    )(vec_far, rott)

    p_rows = (part // lanes) * w
    s_rows = (codes // lanes) * (w + SUBDIM)
    rec_shape = jax.ShapeDtypeStruct((w, rows), BF16)

    def quantize(k, cb_k):
        n_keep, n_send = (p_rows + s_rows, p_rows) if k == 0 else (p_rows, p_rows + s_rows)
        whole = lambda shape: pl.BlockSpec(shape, lambda m: (0,) * len(shape))
        y_spec = pl.BlockSpec((1, GROUP * SUBDIM, rows), lambda m: (k, m, 0))
        any_spec = pl.BlockSpec(memory_space=pl.ANY)
        return pl.pallas_call(
            functools.partial(quantize_kernel, k=k, per=per),
            grid=(steps,),
            in_specs=[whole(cb_k.shape), y_spec, y_spec, any_spec, any_spec],
            out_specs=[whole((w, rows)), whole((w, rows)), whole((n_keep, lanes)), whole((n_send, lanes))],
            out_shape=[
                rec_shape,
                rec_shape,
                jax.ShapeDtypeStruct((n_keep, lanes), F32),
                jax.ShapeDtypeStruct((n_send, lanes), BF16),
            ],
            scratch_shapes=[
                pltpu.VMEM((rows, width), BF16),
                pltpu.VMEM((rows, width), BF16),
                pltpu.VMEM(((codes // lanes) * SUBDIM, lanes), F32),
                pltpu.SemaphoreType.DMA,
                pltpu.SemaphoreType.DMA,
            ],
            compiler_params=params,
            name="quantize_near" if k == 0 else "quantize_far",
        )(cb_k, y0, y1, vectors, vec_far)

    mine0, other0, keep0, send0 = quantize(0, cb)
    got0 = lax.ppermute(send0, "sub", swap)
    theirs0 = lax.ppermute(other0, "rep", swap)
    mine1, other1, keep1, send1 = quantize(1, cb_far)
    got1 = lax.ppermute(send1, "sub", swap)
    theirs1 = lax.ppermute(other1, "rep", swap)

    reconstruction = pl.pallas_call(
        turn_kernel,
        out_shape=jax.ShapeDtypeStruct((rows, width), BF16),
        in_specs=[vmem] * 4,
        out_specs=vmem,
        scratch_shapes=[pltpu.VMEM((width, rows), BF16)],
        compiler_params=params,
        name="turn",
    )(mine0, mine1, theirs0, theirs1)

    used = 2 * p_rows + s_rows
    piece = -(-used // (rows_n * SUBDIM)) * SUBDIM
    pad = jnp.zeros((piece * rows_n - used, lanes), BF16)
    half = jnp.concatenate(
        [(keep0 + got1.astype(F32)).astype(BF16), (keep1 + got0.astype(F32)).astype(BF16), pad], axis=0
    ).reshape(rows_n, piece, lanes)
    own = lax.dynamic_index_in_dim(half, z, 0, keepdims=False)
    gathered = [
        shifts(lax.dynamic_index_in_dim(half, (z + d) % rows_n, 0, keepdims=False), rows_n, d) for d in range(1, rows_n)
    ]
    summed = functools.reduce(lambda a, b: a + b.astype(F32), gathered, own.astype(F32)).astype(BF16)
    all_mine = jnp.stack([summed] + [shifts(summed, rows_n, d) for d in range(1, rows_n)])
    all_theirs = lax.ppermute(all_mine, "rep", swap)

    cross, new = pl.pallas_call(
        functools.partial(final_kernel, per=per, total=total),
        out_shape=(jax.ShapeDtypeStruct((part, width), F32), jax.ShapeDtypeStruct(cb.shape, F32)),
        in_specs=[vmem] * 3,
        out_specs=(vmem, vmem),
        scratch_shapes=[pltpu.VMEM((2, rows_n * piece, lanes), F32)],
        compiler_params=params,
        name="final",
    )(all_mine, all_theirs, cb)
    return reconstruction, new.transpose(0, 2, 1), cross


def solution(mesh):
    placed = (P(("dom", "row", "sub", "rep"), None), P("dom", None), P(("dom", "sub"), None, None))
    body = on_device if mesh.shape["sub"] == 2 and mesh.shape["row"] <= 8 else any_mesh
    return jax.shard_map(
        body,
        mesh=mesh,
        in_specs=placed,
        out_specs=(
            P(("dom", "row", "sub", "rep"), None),
            P(("dom", "sub"), None, None),
            P(("dom", "sub"), None),
        ),
        check_vma=False,
    )
```

```python
import functools
import math

import jax
import jax.numpy as jnp
from jax import lax
from jax.experimental import pallas as pl
from jax.experimental.pallas import tpu as pltpu
from jax.sharding import PartitionSpec as P

SUBDIM = 16
SOFTNESS = 4.0
LOG2E = math.log2(math.e)
F32, BF16 = jnp.float32, jnp.bfloat16
GROUP = 4
VMEM_BYTES = 28 * 2**20


def quantize_rows(block, codebook):
    block = block.astype(F32)
    cross_product = jnp.dot(codebook, block, precision=lax.Precision.HIGHEST)
    squared_norms = jnp.sum(codebook * codebook, axis=1)
    affinity_scores = (2.0 * cross_product - squared_norms[:, None]) / SOFTNESS
    weights = jax.nn.softmax(affinity_scores, axis=0)
    recon = jnp.dot(codebook.T, weights, precision=lax.Precision.HIGHEST)
    sums = lax.dot_general(weights, block, (((1,), (1,)), ((), ())), precision=lax.Precision.HIGHEST)
    return recon, sums, jnp.sum(weights, axis=1)


def any_mesh(vectors, rotation, codebooks):
    rows, width = vectors.shape
    groups = lax.axis_size("sub")
    part = width // groups
    rotated_t = lax.dot_general(
        rotation, vectors, (((0,), (1,)), ((), ())), preferred_element_type=F32
    ).astype(BF16)
    received = lax.all_to_all(rotated_t.reshape(groups, part, rows), "sub", split_axis=0, concat_axis=2, tiled=True)
    columns = received.shape[2]
    blocks = received.reshape(part // SUBDIM, SUBDIM, columns)
    recon, sums, counts = lax.map(lambda pair: quantize_rows(pair[0], pair[1]), (blocks, codebooks))
    sent = recon.astype(BF16).reshape(1, part, columns)
    recon_t = lax.all_to_all(sent, "sub", split_axis=2, concat_axis=0, tiled=True).reshape(width, rows)
    total = rows * lax.axis_size("row") * groups * lax.axis_size("rep")
    sums, counts = lax.psum((sums, counts), ("row", "rep"))
    term = lax.dot_general(vectors, recon_t, (((0,), (1,)), ((), ())), preferred_element_type=F32)
    whole = lax.psum(term, ("row", "sub", "rep"))
    mine = lax.dynamic_slice_in_dim(whole, lax.axis_index("sub") * part, part, 0)
    return recon_t.T, (sums + codebooks) / (counts[:, :, None] + 1.0), mine / total


def rotate_kernel(vec_ref, rot_ref, y_ref, rott_ref):
    s, r = lax.axis_index("sub"), lax.axis_index("rep")
    n, w = y_ref.shape[0], y_ref.shape[1]
    turned = rot_ref[...].T
    for h in range(n):
        for q in range(2):
            @pl.when(r == q)
            def _():
                rott_ref[(h + n - s) % n] = turned[(2 * h + q) * w : (2 * h + q + 1) * w]
    for k in range(n):
        y_ref[k] = lax.dot_general(
            rott_ref[k], vec_ref[...], (((1,), (1,)), ((), ())), preferred_element_type=F32
        ).astype(BF16)


def operands(c):
    codes = c.shape[1]
    scaled = c * (2.0 / SOFTNESS * LOG2E)
    hi = scaled.astype(BF16).astype(F32)
    mid = (scaled - hi).astype(BF16).astype(F32)
    lo = (scaled - hi) - mid
    n = jnp.sum(c * c, axis=0, keepdims=True) * (-LOG2E / SOFTNESS)
    n_hi = n.astype(BF16).astype(F32)
    n_mid = (n - n_hi).astype(BF16).astype(F32)
    n_lo = (n - n_hi) - n_mid
    row = lax.broadcasted_iota(jnp.int32, (SUBDIM, codes), 0)
    norms = jnp.where(row == 0, n_hi, jnp.where(row == 1, n_mid, jnp.where(row == 2, n_lo, 0.0)))
    a = jnp.concatenate([hi, mid, lo, norms], axis=0).T.astype(BF16)
    c_hi = c.astype(BF16)
    c_lo = (c - c_hi.astype(F32)).astype(BF16)
    b = jnp.concatenate([c_hi, c_lo, jnp.ones((SUBDIM, codes), BF16)], axis=0)
    return a, b


def quantize_kernel(*refs, k, per):
    if k == 1:
        (cb_ref, y0_ref, rott_ref, v0_hbm, v1_hbm,
         rec0_ref, rec1_ref, keep_ref, send_ref, y1_ref, v0, v1, cnt, sem0, sem1) = refs
    else:
        (cb_ref, y0_ref, y1_ref, v0_hbm, v1_hbm,
         rec0_ref, rec1_ref, keep_ref, send_ref, v0, v1, cnt, sem0, sem1) = refs
    step, steps = pl.program_id(0), pl.num_programs(0)
    s, r = lax.axis_index("sub"), lax.axis_index("rep")
    codes = cb_ref.shape[2]
    cols = y0_ref.shape[2]
    w = per * SUBDIM
    lanes = 128
    part = v0.shape[1] // 2
    base = r * per if k == 0 else 0
    p_rows = (part // lanes) * w
    sums_ref = keep_ref if k == 0 else send_ref

    @pl.when(step == 0)
    def _():
        pltpu.make_async_copy(v1_hbm, v1, sem1).start()
        pltpu.make_async_copy(v0_hbm, v0, sem0).start()
        cnt[...] = jnp.zeros_like(cnt)
        pltpu.make_async_copy(v1_hbm, v1, sem1).wait()
        if k == 1:
            for q in range(2):
                y1_ref[q] = lax.dot_general(
                    rott_ref[q], v1[...], (((1,), (1,)), ((), ())), preferred_element_type=F32
                ).astype(BF16)

    ab = [operands(cb_ref[base + step * GROUP + j]) for j in range(GROUP)]
    acc = [jnp.zeros((2 * SUBDIM, codes), F32) for _ in range(GROUP)]
    recs = (rec0_ref, rec1_ref)
    ones = jnp.ones((SUBDIM, cols), BF16)

    def rows_at(j):
        return pl.multiple_of(step * (GROUP * SUBDIM), GROUP * SUBDIM) + SUBDIM * j

    def score(j, i):
        if i == 1 and k == 1:
            y = y1_ref[1, pl.ds(pl.multiple_of(rows_at(j), SUBDIM), SUBDIM), :]
        else:
            y = (y0_ref, y1_ref)[i][0, SUBDIM * j : SUBDIM * (j + 1), :]
        return y, jnp.dot(ab[j][0], jnp.concatenate([y, y, y, ones], axis=0), preferred_element_type=F32)

    def spread(sc):
        return jnp.exp2(sc - jnp.max(sc, axis=0, keepdims=True)).astype(BF16)

    def finish(j, i, y, e):
        out = jnp.dot(ab[j][1], e, preferred_element_type=F32)
        inv = 1.0 / out[2 * SUBDIM :]
        recs[i][pl.ds(pl.multiple_of(rows_at(j), SUBDIM), SUBDIM), :] = (
            (out[:SUBDIM] + out[SUBDIM : 2 * SUBDIM]) * inv
        ).astype(BF16)
        yz = jnp.concatenate([(y.astype(F32) * inv).astype(BF16), inv.astype(BF16)], axis=0)
        acc[j] = acc[j] + lax.dot_general(yz, e, (((1,), (1,)), ((), ())), preferred_element_type=F32)

    work = [(j, i) for j in range(GROUP) for i in range(2)]
    first = second = None
    for item in work + [None, None]:
        new_first = (item, *score(*item)) if item is not None else None
        new_second = (first[0], first[1], spread(first[2])) if first is not None else None
        if second is not None:
            finish(*second[0], second[1], second[2])
        first, second = new_first, new_second

    for j in range(GROUP):
        m = step * GROUP + j
        for half in range(codes // lanes):
            at = p_rows + half * w + m * SUBDIM
            sums_ref[pl.ds(pl.multiple_of(at, SUBDIM), SUBDIM), :] = acc[j][
                :SUBDIM, half * lanes : (half + 1) * lanes
            ].astype(sums_ref.dtype)
            cnt[pl.ds(half * SUBDIM + m, 1), :] = acc[j][SUBDIM : SUBDIM + 1, half * lanes : (half + 1) * lanes]

    @pl.when(step == steps - 1)
    def _():
        at = p_rows + (codes // lanes) * w
        sums_ref[at : at + cnt.shape[0], :] = cnt[...].astype(sums_ref.dtype)
        pltpu.make_async_copy(v0_hbm, v0, sem0).wait()
        cross = jnp.dot(rec0_ref[...], v0[...], preferred_element_type=F32) + jnp.dot(
            rec1_ref[...], v1[...], preferred_element_type=F32
        )
        for h in range(2):
            @pl.when(s == h)
            def _():
                for g in range(part // lanes):
                    near = h * part + g * lanes
                    far = (1 - h) * part + g * lanes
                    keep_ref[g * w : (g + 1) * w, :] = cross[:, near : near + lanes]
                    send_ref[g * w : (g + 1) * w, :] = cross[:, far : far + lanes].astype(BF16)


def turn_kernel(m0_ref, m1_ref, t0_ref, t1_ref, out_ref, buf):
    s, r = lax.axis_index("sub"), lax.axis_index("rep")
    w = m0_ref.shape[0]
    for k, (mine, theirs) in enumerate(((m0_ref, t0_ref), (m1_ref, t1_ref))):
        h = (s + k) % 2
        buf[pl.ds(pl.multiple_of((2 * h + r) * w, SUBDIM), w), :] = mine[...]
        buf[pl.ds(pl.multiple_of((2 * h + 1 - r) * w, SUBDIM), w), :] = theirs[...]
    out_ref[...] = buf[...].T


def final_kernel(mine_ref, theirs_ref, cb_ref, cross_ref, new_ref, buf, *, per, total):
    s, r, z = lax.axis_index("sub"), lax.axis_index("rep"), lax.axis_index("row")
    n = mine_ref.shape[0]
    piece = mine_ref.shape[1]
    lanes = 128
    w = per * SUBDIM
    codes = cb_ref.shape[2]
    groups = cross_ref.shape[0] // lanes
    halves = codes // lanes
    for side, ref in enumerate((mine_ref, theirs_ref)):
        for d in range(n):
            at = ((z + n - d) % n) * piece
            buf[side, pl.ds(pl.multiple_of(at, SUBDIM), piece), :] = ref[d].astype(F32)
    a_rows = groups * w + halves * (w + SUBDIM)
    for g in range(groups):
        for h in range(2):
            for q in range(2):
                @pl.when((s == h) & (r == q))
                def _():
                    pieces = []
                    for col in range(2):
                        k = col ^ h
                        for rep in range(2):
                            start = k * a_rows + g * w
                            pieces.append(buf[rep ^ q, start : start + w, :])
                    cross_ref[g * lanes : (g + 1) * lanes, :] = jnp.concatenate(pieces, axis=0).T * (1.0 / total)
    first = groups * w
    for side in range(2):
        part = r if side == 0 else 1 - r
        for m in range(per):
            c = cb_ref[part * per + m]
            sums = jnp.concatenate(
                [buf[side, first + hf * w + m * SUBDIM : first + hf * w + (m + 1) * SUBDIM, :] for hf in range(halves)],
                axis=1,
            )
            at = first + halves * w + m
            count = jnp.concatenate([buf[side, at + hf * SUBDIM : at + hf * SUBDIM + 1, :] for hf in range(halves)], axis=1)
            new_ref[part * per + m] = (sums + c) / (count + 1.0)


def shifts(x, n, d):
    return lax.ppermute(x, "row", [(i, (i + d) % n) for i in range(n)])


def on_device(vectors, rotation, codebooks):
    rows, width = vectors.shape
    subs, rows_n = 2, lax.axis_size("row")
    part = width // subs
    per = part // SUBDIM // 2
    w = per * SUBDIM
    codes = codebooks.shape[1]
    lanes = 128
    steps = per // GROUP
    total = rows * rows_n * subs * 2
    swap = [(0, 1), (1, 0)]
    r, z = lax.axis_index("rep"), lax.axis_index("row")
    params = pltpu.CompilerParams(vmem_limit_bytes=VMEM_BYTES)
    small = pltpu.CompilerParams(vmem_limit_bytes=VMEM_BYTES // 2)
    vmem = pl.BlockSpec(memory_space=pltpu.VMEM)

    cb = codebooks.transpose(0, 2, 1)
    cb_far = lax.ppermute(lax.dynamic_slice_in_dim(cb, r * per, per, 0), "sub", swap)
    vec_far = lax.ppermute(vectors, "rep", swap)

    y_shape = jax.ShapeDtypeStruct((subs, w, rows), BF16)
    y0, rott = pl.pallas_call(
        rotate_kernel,
        out_shape=(y_shape, jax.ShapeDtypeStruct((subs, w, width), BF16)),
        in_specs=[vmem] * 2,
        out_specs=(vmem, vmem),
        compiler_params=small,
        name="rotate",
    )(vectors, rotation)

    p_rows = (part // lanes) * w
    s_rows = (codes // lanes) * (w + SUBDIM)
    rec_shape = jax.ShapeDtypeStruct((w, rows), BF16)

    def quantize(k, cb_k, extra):
        n_keep, n_send = (p_rows + s_rows, p_rows) if k == 0 else (p_rows, p_rows + s_rows)
        whole = lambda shape: pl.BlockSpec(shape, lambda m: (0,) * len(shape))
        y_spec = pl.BlockSpec((1, GROUP * SUBDIM, rows), lambda m: (k, m, 0))
        any_spec = pl.BlockSpec(memory_space=pl.ANY)
        more = k == 1
        return pl.pallas_call(
            functools.partial(quantize_kernel, k=k, per=per),
            grid=(steps,),
            in_specs=[whole(cb_k.shape), y_spec, whole(extra.shape) if more else y_spec, any_spec, any_spec],
            out_specs=[whole((w, rows)), whole((w, rows)), whole((n_keep, lanes)), whole((n_send, lanes))]
            + [whole(y_shape.shape)] * more,
            out_shape=[
                rec_shape,
                rec_shape,
                jax.ShapeDtypeStruct((n_keep, lanes), F32),
                jax.ShapeDtypeStruct((n_send, lanes), BF16),
            ]
            + [y_shape] * more,
            scratch_shapes=[
                pltpu.VMEM((rows, width), BF16),
                pltpu.VMEM((rows, width), BF16),
                pltpu.VMEM(((codes // lanes) * SUBDIM, lanes), F32),
                pltpu.SemaphoreType.DMA,
                pltpu.SemaphoreType.DMA,
            ],
            compiler_params=params,
            name="quantize_near" if k == 0 else "quantize_far",
        )(cb_k, y0, extra, vectors, vec_far)

    mine1, other1, keep1, send1, y1 = quantize(1, cb_far, rott)
    got1 = lax.ppermute(send1, "sub", swap)
    theirs1 = lax.ppermute(other1, "rep", swap)
    mine0, other0, keep0, send0 = quantize(0, cb, y1)
    got0 = lax.ppermute(send0, "sub", swap)
    theirs0 = lax.ppermute(other0, "rep", swap)
    got0, theirs0, theirs1 = lax.optimization_barrier((got0, theirs0, theirs1))

    reconstruction = pl.pallas_call(
        turn_kernel,
        out_shape=jax.ShapeDtypeStruct((rows, width), BF16),
        in_specs=[vmem] * 4,
        out_specs=vmem,
        scratch_shapes=[pltpu.VMEM((width, rows), BF16)],
        compiler_params=small,
        name="turn",
    )(mine0, mine1, theirs0, theirs1)

    used = 2 * p_rows + s_rows
    piece = -(-used // (rows_n * SUBDIM)) * SUBDIM
    pad = jnp.zeros((piece * rows_n - used, lanes), BF16)
    half = jnp.concatenate(
        [(keep0 + got1.astype(F32)).astype(BF16), (keep1 + got0.astype(F32)).astype(BF16), pad], axis=0
    ).reshape(rows_n, piece, lanes)
    own = lax.dynamic_index_in_dim(half, z, 0, keepdims=False)
    gathered = [
        shifts(lax.dynamic_index_in_dim(half, (z + d) % rows_n, 0, keepdims=False), rows_n, d) for d in range(1, rows_n)
    ]
    summed = functools.reduce(lambda a, b: a + b.astype(F32), gathered, own.astype(F32)).astype(BF16)
    summed, reconstruction = lax.optimization_barrier((summed, reconstruction))
    all_mine = jnp.stack([summed] + [shifts(summed, rows_n, d) for d in range(1, rows_n)])
    all_theirs = lax.ppermute(all_mine, "rep", swap)

    cross, new = pl.pallas_call(
        functools.partial(final_kernel, per=per, total=total),
        out_shape=(jax.ShapeDtypeStruct((part, width), F32), jax.ShapeDtypeStruct(cb.shape, F32)),
        in_specs=[vmem] * 3,
        out_specs=(vmem, vmem),
        scratch_shapes=[pltpu.VMEM((2, rows_n * piece, lanes), F32)],
        compiler_params=small,
        name="final",
    )(all_mine, all_theirs, cb)
    return reconstruction, new.transpose(0, 2, 1), cross


def solution(mesh):
    placed = (P(("dom", "row", "sub", "rep"), None), P("dom", None), P(("dom", "sub"), None, None))
    body = on_device if mesh.shape["sub"] == 2 and mesh.shape["row"] <= 8 else any_mesh
    return jax.shard_map(
        body,
        mesh=mesh,
        in_specs=placed,
        out_specs=(
            P(("dom", "row", "sub", "rep"), None),
            P(("dom", "sub"), None, None),
            P(("dom", "sub"), None),
        ),
        check_vma=False,
    )
```

```python
import functools
import math

import jax
import jax.numpy as jnp
from jax import lax
from jax.experimental import pallas as pl
from jax.experimental.pallas import tpu as pltpu
from jax.sharding import PartitionSpec as P

SUBDIM = 16
SOFTNESS = 4.0
LOG2E = math.log2(math.e)
F32, BF16 = jnp.float32, jnp.bfloat16
VMEM_BYTES = 28 * 2**20


def quantize_rows(block, codebook):
    block = block.astype(F32)
    cross_product = jnp.dot(codebook, block, precision=lax.Precision.HIGHEST)
    squared_norms = jnp.sum(codebook * codebook, axis=1)
    affinity_scores = (2.0 * cross_product - squared_norms[:, None]) / SOFTNESS
    weights = jax.nn.softmax(affinity_scores, axis=0)
    recon = jnp.dot(codebook.T, weights, precision=lax.Precision.HIGHEST)
    sums = lax.dot_general(weights, block, (((1,), (1,)), ((), ())), precision=lax.Precision.HIGHEST)
    return recon, sums, jnp.sum(weights, axis=1)


def any_mesh(vectors, rotation, codebooks):
    rows, width = vectors.shape
    groups = lax.axis_size("sub")
    part = width // groups
    rotated_t = lax.dot_general(
        rotation, vectors, (((0,), (1,)), ((), ())), preferred_element_type=F32
    ).astype(BF16)
    received = lax.all_to_all(rotated_t.reshape(groups, part, rows), "sub", split_axis=0, concat_axis=2, tiled=True)
    columns = received.shape[2]
    blocks = received.reshape(part // SUBDIM, SUBDIM, columns)
    recon, sums, counts = lax.map(lambda pair: quantize_rows(pair[0], pair[1]), (blocks, codebooks))
    sent = recon.astype(BF16).reshape(1, part, columns)
    recon_t = lax.all_to_all(sent, "sub", split_axis=2, concat_axis=0, tiled=True).reshape(width, rows)
    total = rows * lax.axis_size("row") * groups * lax.axis_size("rep")
    sums, counts = lax.psum((sums, counts), ("row", "rep"))
    term = lax.dot_general(vectors, recon_t, (((0,), (1,)), ((), ())), preferred_element_type=F32)
    whole = lax.psum(term, ("row", "sub", "rep"))
    mine = lax.dynamic_slice_in_dim(whole, lax.axis_index("sub") * part, part, 0)
    return recon_t.T, (sums + codebooks) / (counts[:, :, None] + 1.0), mine / total


def rotate_kernel(vec_ref, rot_ref, y_ref, rott_ref):
    s, r = lax.axis_index("sub"), lax.axis_index("rep")
    n, w = y_ref.shape[0], y_ref.shape[1]
    turned = rot_ref[...].T
    for h in range(n):
        for q in range(2):
            @pl.when(r == q)
            def _():
                rott_ref[(h + n - s) % n] = turned[(2 * h + q) * w : (2 * h + q + 1) * w]
    for k in range(n):
        y_ref[k] = lax.dot_general(
            rott_ref[k], vec_ref[...], (((1,), (1,)), ((), ())), preferred_element_type=F32
        ).astype(BF16)


def rotate_more_kernel(vec_ref, rott_ref, y_ref):
    for k in range(y_ref.shape[0]):
        y_ref[k] = lax.dot_general(
            rott_ref[k], vec_ref[...], (((1,), (1,)), ((), ())), preferred_element_type=F32
        ).astype(BF16)


def operands(c):
    codes = c.shape[1]
    scaled = c * (2.0 / SOFTNESS * LOG2E)
    hi = scaled.astype(BF16).astype(F32)
    mid = (scaled - hi).astype(BF16).astype(F32)
    lo = (scaled - hi) - mid
    n = jnp.sum(c * c, axis=0, keepdims=True) * (-LOG2E / SOFTNESS)
    n_hi = n.astype(BF16).astype(F32)
    n_mid = (n - n_hi).astype(BF16).astype(F32)
    n_lo = (n - n_hi) - n_mid
    row = lax.broadcasted_iota(jnp.int32, (SUBDIM, codes), 0)
    norms = jnp.where(row == 0, n_hi, jnp.where(row == 1, n_mid, jnp.where(row == 2, n_lo, 0.0)))
    a = jnp.concatenate([hi, mid, lo, norms], axis=0).T.astype(BF16)
    c_hi = c.astype(BF16)
    c_lo = (c - c_hi.astype(F32)).astype(BF16)
    b = jnp.concatenate([c_hi, c_lo, jnp.ones((SUBDIM, codes), BF16)], axis=0)
    return a, b


def quantize_kernel(cb_ref, y0_ref, y1_ref, v0_ref, v1_ref, rec0_ref, rec1_ref, keep_ref, send_ref, cnt, *, k, per):
    s, r = lax.axis_index("sub"), lax.axis_index("rep")
    codes = cb_ref.shape[2]
    cols = y0_ref.shape[2]
    w = per * SUBDIM
    lanes = 128
    part = v0_ref.shape[1] // 2
    base = r * per if k == 0 else 0
    p_rows = (part // lanes) * w
    sums_ref = keep_ref if k == 0 else send_ref
    ones = jnp.ones((SUBDIM, cols), BF16)
    ys, recs = (y0_ref, y1_ref), (rec0_ref, rec1_ref)
    cnt[...] = jnp.zeros_like(cnt)
    ab, acc = {}, {}

    def score(j, i):
        if j not in ab:
            ab[j] = operands(cb_ref[base + j])
        y = ys[i][k, SUBDIM * j : SUBDIM * (j + 1), :]
        return y, jnp.dot(ab[j][0], jnp.concatenate([y, y, y, ones], axis=0), preferred_element_type=F32)

    def spread(sc):
        return jnp.exp2(sc - jnp.max(sc, axis=0, keepdims=True)).astype(BF16)

    def rebuild(j, i, y, e):
        out = jnp.dot(ab[j][1], e, preferred_element_type=F32)
        inv = 1.0 / out[2 * SUBDIM :]
        recs[i][SUBDIM * j : SUBDIM * (j + 1), :] = ((out[:SUBDIM] + out[SUBDIM : 2 * SUBDIM]) * inv).astype(BF16)
        return jnp.concatenate([(y.astype(F32) * inv).astype(BF16), inv.astype(BF16)], axis=0)

    def gather(j, i, yz, e):
        sums = lax.dot_general(yz, e, (((1,), (1,)), ((), ())), preferred_element_type=F32)
        if i == 0:
            acc[j] = sums
            return
        sums = acc.pop(j) + sums
        for half in range(codes // lanes):
            at = p_rows + half * w + j * SUBDIM
            sums_ref[at : at + SUBDIM, :] = sums[:SUBDIM, half * lanes : (half + 1) * lanes].astype(sums_ref.dtype)
            at = half * SUBDIM + j
            cnt[at : at + 1, :] = sums[SUBDIM : SUBDIM + 1, half * lanes : (half + 1) * lanes]

    first = second = third = None
    for item in [(j, i) for j in range(per) for i in range(2)] + [None] * 3:
        new_first = (item, *score(*item)) if item is not None else None
        new_second = (first[0], first[1], spread(first[2])) if first is not None else None
        new_third = (second[0], rebuild(*second[0], second[1], second[2]), second[2]) if second is not None else None
        if third is not None:
            gather(*third[0], third[1], third[2])
        first, second, third = new_first, new_second, new_third

    at = p_rows + (codes // lanes) * w
    sums_ref[at : at + cnt.shape[0], :] = cnt[...].astype(sums_ref.dtype)
    cross = jnp.dot(rec0_ref[...], v0_ref[...], preferred_element_type=F32) + jnp.dot(
        rec1_ref[...], v1_ref[...], preferred_element_type=F32
    )
    for h in range(2):
        @pl.when(s == h)
        def _():
            for g in range(part // lanes):
                near = h * part + g * lanes
                far = (1 - h) * part + g * lanes
                keep_ref[g * w : (g + 1) * w, :] = cross[:, near : near + lanes]
                send_ref[g * w : (g + 1) * w, :] = cross[:, far : far + lanes].astype(BF16)


def turn_kernel(m0_ref, m1_ref, t0_ref, t1_ref, out_ref, buf):
    s, r = lax.axis_index("sub"), lax.axis_index("rep")
    w = m0_ref.shape[0]
    for k, (mine, theirs) in enumerate(((m0_ref, t0_ref), (m1_ref, t1_ref))):
        h = (s + k) % 2
        buf[pl.ds(pl.multiple_of((2 * h + r) * w, SUBDIM), w), :] = mine[...]
        buf[pl.ds(pl.multiple_of((2 * h + 1 - r) * w, SUBDIM), w), :] = theirs[...]
    out_ref[...] = buf[...].T


def final_kernel(mine_ref, theirs_ref, cb_ref, cross_ref, new_ref, buf, *, per, total):
    s, r, z = lax.axis_index("sub"), lax.axis_index("rep"), lax.axis_index("row")
    n = mine_ref.shape[0]
    piece = mine_ref.shape[1]
    lanes = 128
    w = per * SUBDIM
    codes = cb_ref.shape[2]
    groups = cross_ref.shape[0] // lanes
    halves = codes // lanes
    for side, ref in enumerate((mine_ref, theirs_ref)):
        for i in range(n):
            at = (z ^ ((n - i) % n)) * piece
            buf[side, pl.ds(pl.multiple_of(at, SUBDIM), piece), :] = ref[i].astype(F32)
    a_rows = groups * w + halves * (w + SUBDIM)
    for g in range(groups):
        for h in range(2):
            for q in range(2):
                @pl.when((s == h) & (r == q))
                def _():
                    pieces = []
                    for col in range(2):
                        k = col ^ h
                        for rep in range(2):
                            start = k * a_rows + g * w
                            pieces.append(buf[rep ^ q, start : start + w, :])
                    cross_ref[g * lanes : (g + 1) * lanes, :] = jnp.concatenate(pieces, axis=0).T * (1.0 / total)
    first = groups * w
    for side in range(2):
        part = r if side == 0 else 1 - r
        for m in range(per):
            c = cb_ref[part * per + m]
            sums = jnp.concatenate(
                [buf[side, first + hf * w + m * SUBDIM : first + hf * w + (m + 1) * SUBDIM, :] for hf in range(halves)],
                axis=1,
            )
            at = first + halves * w + m
            count = jnp.concatenate([buf[side, at + hf * SUBDIM : at + hf * SUBDIM + 1, :] for hf in range(halves)], axis=1)
            new_ref[part * per + m] = (sums + c) / (count + 1.0)


def exchange(x, n, d):
    return lax.ppermute(x, "row", [(i, i ^ d) for i in range(n)])


def on_device(vectors, rotation, codebooks):
    rows, width = vectors.shape
    subs, rows_n = 2, lax.axis_size("row")
    part = width // subs
    per = part // SUBDIM // 2
    w = per * SUBDIM
    codes = codebooks.shape[1]
    lanes = 128
    total = rows * rows_n * subs * 2
    swap = [(0, 1), (1, 0)]
    r, z = lax.axis_index("rep"), lax.axis_index("row")
    params = pltpu.CompilerParams(vmem_limit_bytes=VMEM_BYTES)
    small = pltpu.CompilerParams(vmem_limit_bytes=VMEM_BYTES // 2)
    vmem = pl.BlockSpec(memory_space=pltpu.VMEM)

    cb = codebooks.transpose(0, 2, 1)
    cb_sent, vec_sent = lax.optimization_barrier((lax.dynamic_slice_in_dim(cb, r * per, per, 0), vectors))
    cb_far = lax.ppermute(cb_sent, "sub", swap)
    vec_far = lax.ppermute(vec_sent, "rep", swap)

    y_shape = jax.ShapeDtypeStruct((subs, w, rows), BF16)
    y0, rott = pl.pallas_call(
        rotate_kernel,
        out_shape=(y_shape, jax.ShapeDtypeStruct((subs, w, width), BF16)),
        in_specs=[vmem] * 2,
        out_specs=(vmem, vmem),
        compiler_params=small,
        name="rotate",
    )(vectors, rotation)

    y1 = pl.pallas_call(
        rotate_more_kernel, out_shape=y_shape, in_specs=[vmem] * 2, out_specs=vmem, compiler_params=small, name="rotate_far"
    )(vec_far, rott)

    p_rows = (part // lanes) * w
    s_rows = (codes // lanes) * (w + SUBDIM)
    rec_shape = jax.ShapeDtypeStruct((w, rows), BF16)

    def quantize(k, cb_k):
        n_keep, n_send = (p_rows + s_rows, p_rows) if k == 0 else (p_rows, p_rows + s_rows)
        return pl.pallas_call(
            functools.partial(quantize_kernel, k=k, per=per),
            in_specs=[vmem] * 5,
            out_specs=[vmem] * 4,
            out_shape=[
                rec_shape,
                rec_shape,
                jax.ShapeDtypeStruct((n_keep, lanes), F32),
                jax.ShapeDtypeStruct((n_send, lanes), BF16),
            ],
            scratch_shapes=[pltpu.VMEM(((codes // lanes) * SUBDIM, lanes), F32)],
            compiler_params=params,
            name="quantize_near" if k == 0 else "quantize_far",
        )(cb_k, y0, y1, vectors, vec_far)

    mine1, other1, keep1, send1 = quantize(1, cb_far)
    got1 = lax.ppermute(send1, "sub", swap)
    theirs1 = lax.ppermute(other1, "rep", swap)
    mine0, other0, keep0, send0 = quantize(0, cb)
    got0 = lax.ppermute(send0, "sub", swap)
    theirs0 = lax.ppermute(other0, "rep", swap)
    got0, theirs0, theirs1 = lax.optimization_barrier((got0, theirs0, theirs1))

    reconstruction = pl.pallas_call(
        turn_kernel,
        out_shape=jax.ShapeDtypeStruct((rows, width), BF16),
        in_specs=[vmem] * 4,
        out_specs=vmem,
        scratch_shapes=[pltpu.VMEM((width, rows), BF16)],
        compiler_params=small,
        name="turn",
    )(mine0, mine1, theirs0, theirs1)

    used = 2 * p_rows + s_rows
    piece = -(-used // (rows_n * SUBDIM)) * SUBDIM
    pad = jnp.zeros((piece * rows_n - used, lanes), BF16)
    half = jnp.concatenate(
        [(keep0 + got1.astype(F32)).astype(BF16), (keep1 + got0.astype(F32)).astype(BF16), pad], axis=0
    ).reshape(rows_n, piece, lanes)
    own = lax.dynamic_index_in_dim(half, z, 0, keepdims=False)
    apart = range(rows_n - 1, 0, -1)
    gathered = [exchange(lax.dynamic_index_in_dim(half, z ^ d, 0, keepdims=False), rows_n, d) for d in apart]
    summed = functools.reduce(lambda a, b: a + b.astype(F32), gathered, own.astype(F32)).astype(BF16)
    summed, reconstruction = lax.optimization_barrier((summed, reconstruction))
    all_mine = jnp.stack([summed] + [exchange(summed, rows_n, d) for d in apart])
    all_theirs = lax.ppermute(all_mine, "rep", swap)

    cross, new = pl.pallas_call(
        functools.partial(final_kernel, per=per, total=total),
        out_shape=(jax.ShapeDtypeStruct((part, width), F32), jax.ShapeDtypeStruct(cb.shape, F32)),
        in_specs=[vmem] * 3,
        out_specs=(vmem, vmem),
        scratch_shapes=[pltpu.VMEM((2, rows_n * piece, lanes), F32)],
        compiler_params=small,
        name="final",
    )(all_mine, all_theirs, cb)
    return reconstruction, new.transpose(0, 2, 1), cross


def solution(mesh):
    placed = (P(("dom", "row", "sub", "rep"), None), P("dom", None), P(("dom", "sub"), None, None))
    body = on_device if mesh.shape["sub"] == 2 and mesh.shape["row"] in (2, 4, 8) else any_mesh
    return jax.shard_map(
        body,
        mesh=mesh,
        in_specs=placed,
        out_specs=(
            P(("dom", "row", "sub", "rep"), None),
            P(("dom", "sub"), None, None),
            P(("dom", "sub"), None),
        ),
        check_vma=False,
    )
```

```python
import functools
import math

import jax
import jax.numpy as jnp
from jax import lax
from jax.experimental import pallas as pl
from jax.experimental.pallas import tpu as pltpu
from jax.sharding import PartitionSpec as P

SUBDIM = 16
SOFTNESS = 4.0
LOG2E = math.log2(math.e)
F32, BF16 = jnp.float32, jnp.bfloat16
VMEM_BYTES = 24 * 2**20


def quantize_rows(block, codebook):
    block = block.astype(F32)
    cross_product = jnp.dot(codebook, block, precision=lax.Precision.HIGHEST)
    squared_norms = jnp.sum(codebook * codebook, axis=1)
    affinity_scores = (2.0 * cross_product - squared_norms[:, None]) / SOFTNESS
    weights = jax.nn.softmax(affinity_scores, axis=0)
    recon = jnp.dot(codebook.T, weights, precision=lax.Precision.HIGHEST)
    sums = lax.dot_general(weights, block, (((1,), (1,)), ((), ())), precision=lax.Precision.HIGHEST)
    return recon, sums, jnp.sum(weights, axis=1)


def any_mesh(vectors, rotation, codebooks):
    rows, width = vectors.shape
    groups = lax.axis_size("sub")
    part = width // groups
    rotated_t = lax.dot_general(
        rotation, vectors, (((0,), (1,)), ((), ())), preferred_element_type=F32
    ).astype(BF16)
    received = lax.all_to_all(rotated_t.reshape(groups, part, rows), "sub", split_axis=0, concat_axis=2, tiled=True)
    columns = received.shape[2]
    blocks = received.reshape(part // SUBDIM, SUBDIM, columns)
    recon, sums, counts = lax.map(lambda pair: quantize_rows(pair[0], pair[1]), (blocks, codebooks))
    sent = recon.astype(BF16).reshape(1, part, columns)
    recon_t = lax.all_to_all(sent, "sub", split_axis=2, concat_axis=0, tiled=True).reshape(width, rows)
    total = rows * lax.axis_size("row") * groups * lax.axis_size("rep")
    sums, counts = lax.psum((sums, counts), ("row", "rep"))
    term = lax.dot_general(vectors, recon_t, (((0,), (1,)), ((), ())), preferred_element_type=F32)
    whole = lax.psum(term, ("row", "sub", "rep"))
    mine = lax.dynamic_slice_in_dim(whole, lax.axis_index("sub") * part, part, 0)
    return recon_t.T, (sums + codebooks) / (counts[:, :, None] + 1.0), mine / total


def rotate_kernel(vec_ref, rot_ref, y_ref, rott_ref):
    s, r = lax.axis_index("sub"), lax.axis_index("rep")
    n, w = y_ref.shape[0], y_ref.shape[1]
    turned = rot_ref[...].T
    for h in range(n):
        for q in range(2):
            @pl.when(r == q)
            def _():
                rott_ref[(h + n - s) % n] = turned[(2 * h + q) * w : (2 * h + q + 1) * w]
    for k in range(n):
        y_ref[k] = lax.dot_general(
            rott_ref[k], vec_ref[...], (((1,), (1,)), ((), ())), preferred_element_type=F32
        ).astype(BF16)


def rotate_more_kernel(vec_ref, rott_ref, y_ref):
    for k in range(y_ref.shape[0]):
        y_ref[k] = lax.dot_general(
            rott_ref[k], vec_ref[...], (((1,), (1,)), ((), ())), preferred_element_type=F32
        ).astype(BF16)


def operands(c):
    codes = c.shape[1]
    scaled = c * (2.0 / SOFTNESS * LOG2E)
    hi = scaled.astype(BF16).astype(F32)
    mid = (scaled - hi).astype(BF16).astype(F32)
    lo = (scaled - hi) - mid
    n = jnp.sum(c * c, axis=0, keepdims=True) * (-LOG2E / SOFTNESS)
    n_hi = n.astype(BF16).astype(F32)
    n_mid = (n - n_hi).astype(BF16).astype(F32)
    n_lo = (n - n_hi) - n_mid
    row = lax.broadcasted_iota(jnp.int32, (SUBDIM, codes), 0)
    norms = jnp.where(row == 0, n_hi, jnp.where(row == 1, n_mid, jnp.where(row == 2, n_lo, 0.0)))
    a = jnp.concatenate([hi, mid, lo, norms], axis=0).T.astype(BF16)
    c_hi = c.astype(BF16)
    c_lo = (c - c_hi.astype(F32)).astype(BF16)
    b = jnp.concatenate([c_hi, c_lo, jnp.ones((SUBDIM, codes), BF16)], axis=0)
    return a, b


def quantize_kernel(cb_ref, y0_ref, y1_ref, v0_ref, v1_ref, rec0_ref, rec1_ref, keep_ref, send_ref, cnt, *, k, per):
    s, r = lax.axis_index("sub"), lax.axis_index("rep")
    codes = cb_ref.shape[2]
    cols = y0_ref.shape[2]
    w = per * SUBDIM
    lanes = 128
    part = v0_ref.shape[1] // 2
    base = r * per if k == 0 else 0
    p_rows = (part // lanes) * w
    sums_ref = keep_ref if k == 0 else send_ref
    ones = jnp.ones((SUBDIM, cols), BF16)
    ys, recs = (y0_ref, y1_ref), (rec0_ref, rec1_ref)
    cnt[...] = jnp.zeros_like(cnt)
    ab, acc = {}, {}

    def score(j, i):
        if j not in ab:
            ab[j] = operands(cb_ref[base + j])
        y = ys[i][k, SUBDIM * j : SUBDIM * (j + 1), :]
        return y, jnp.dot(ab[j][0], jnp.concatenate([y, y, y, ones], axis=0), preferred_element_type=F32)

    def spread(sc):
        return jnp.exp2(sc - jnp.max(sc, axis=0, keepdims=True)).astype(BF16)

    def rebuild(j, i, y, e):
        out = jnp.dot(ab[j][1], e, preferred_element_type=F32)
        inv = 1.0 / out[2 * SUBDIM :]
        recs[i][SUBDIM * j : SUBDIM * (j + 1), :] = ((out[:SUBDIM] + out[SUBDIM : 2 * SUBDIM]) * inv).astype(BF16)
        return jnp.concatenate([(y.astype(F32) * inv).astype(BF16), inv.astype(BF16)], axis=0)

    def gather(j, i, yz, e):
        sums = lax.dot_general(yz, e, (((1,), (1,)), ((), ())), preferred_element_type=F32)
        if i == 0:
            acc[j] = sums
            return
        sums = acc.pop(j) + sums
        for half in range(codes // lanes):
            at = p_rows + half * w + j * SUBDIM
            sums_ref[at : at + SUBDIM, :] = sums[:SUBDIM, half * lanes : (half + 1) * lanes].astype(sums_ref.dtype)
            at = half * SUBDIM + j
            cnt[at : at + 1, :] = sums[SUBDIM : SUBDIM + 1, half * lanes : (half + 1) * lanes]

    first = second = third = None
    for item in [(j, i) for j in range(per) for i in range(2)] + [None] * 3:
        new_first = (item, *score(*item)) if item is not None else None
        new_second = (first[0], first[1], spread(first[2])) if first is not None else None
        new_third = (second[0], rebuild(*second[0], second[1], second[2]), second[2]) if second is not None else None
        if third is not None:
            gather(*third[0], third[1], third[2])
        first, second, third = new_first, new_second, new_third

    at = p_rows + (codes // lanes) * w
    sums_ref[at : at + cnt.shape[0], :] = cnt[...].astype(sums_ref.dtype)
    cross = jnp.dot(rec0_ref[...], v0_ref[...], preferred_element_type=F32) + jnp.dot(
        rec1_ref[...], v1_ref[...], preferred_element_type=F32
    )
    for h in range(2):
        @pl.when(s == h)
        def _():
            for g in range(part // lanes):
                near = h * part + g * lanes
                far = (1 - h) * part + g * lanes
                keep_ref[g * w : (g + 1) * w, :] = cross[:, near : near + lanes]
                send_ref[g * w : (g + 1) * w, :] = cross[:, far : far + lanes].astype(BF16)


def turn_kernel(m0_ref, m1_ref, t0_ref, t1_ref, out_ref, buf):
    s, r = lax.axis_index("sub"), lax.axis_index("rep")
    w = m0_ref.shape[0]
    for k, (mine, theirs) in enumerate(((m0_ref, t0_ref), (m1_ref, t1_ref))):
        h = (s + k) % 2
        buf[pl.ds(pl.multiple_of((2 * h + r) * w, SUBDIM), w), :] = mine[...]
        buf[pl.ds(pl.multiple_of((2 * h + 1 - r) * w, SUBDIM), w), :] = theirs[...]
    out_ref[...] = buf[...].T


def final_kernel(*refs, n, per, total):
    pieces, (cb_ref, cross_hbm, new_hbm, buf, cross, new, sems) = refs[: 2 * n], refs[2 * n :]
    s, r, z = lax.axis_index("sub"), lax.axis_index("rep"), lax.axis_index("row")
    lanes = 128
    w = per * SUBDIM
    groups = cross.shape[0] // lanes
    halves = cb_ref.shape[2] // lanes
    near_rows = groups * w + halves * (w + SUBDIM)
    near, far = near_rows // n, groups * w // n
    for side in range(2):
        for i in range(n):
            ref = pieces[side * n + i]
            source = z ^ ((n - i) % n)
            buf[side, pl.ds(pl.multiple_of(source * near, 8), near), :] = ref[:near].astype(F32)
            buf[side, pl.ds(pl.multiple_of(near_rows + source * far, 8), far), :] = ref[near:].astype(F32)

    copies = []
    for g in range(groups):
        for h in range(2):
            for q in range(2):
                @pl.when((s == h) & (r == q))
                def _():
                    parts = []
                    for col in range(2):
                        start = (col ^ h) * near_rows + g * w
                        parts += [buf[rep ^ q, start : start + w, :] for rep in range(2)]
                    cross[g * lanes : (g + 1) * lanes, :] = jnp.concatenate(parts, axis=0).T * (1.0 / total)
        block = pl.ds(g * lanes, lanes)
        copies.append(pltpu.make_async_copy(cross.at[block], cross_hbm.at[block], sems.at[g]))
        copies[-1].start()
    first = groups * w
    for side in range(2):
        part = r if side == 0 else 1 - r
        for m in range(per):
            c = cb_ref[part * per + m]
            rows = [first + hf * w + m * SUBDIM for hf in range(halves)]
            sums = jnp.concatenate([buf[side, a : a + SUBDIM, :] for a in rows], axis=1)
            rows = [first + halves * w + hf * SUBDIM + m for hf in range(halves)]
            count = jnp.concatenate([buf[side, a : a + 1, :] for a in rows], axis=1)
            new[part * per + m] = (sums + c) / (count + 1.0)
    copies.append(pltpu.make_async_copy(new, new_hbm, sems.at[groups]))
    copies[-1].start()
    for copy in copies:
        copy.wait()


def pieces_kernel(kept_ref, got_ref, *refs, n):
    outs, total = refs[:n], refs[n]
    z = lax.axis_index("row")
    total[...] = kept_ref[...] + got_ref[...].astype(F32)
    size = outs[0].shape[0]
    for i, out in enumerate(outs):
        at = (z ^ ((n - i) % n)) * size
        out[...] = total[pl.ds(pl.multiple_of(at, 8), size), :].astype(out.dtype)


def exchange(x, n, d):
    return lax.ppermute(x, "row", [(i, i ^ d) for i in range(n)])


def on_device(vectors, rotation, codebooks):
    rows, width = vectors.shape
    subs, rows_n = 2, lax.axis_size("row")
    part = width // subs
    per = part // SUBDIM // 2
    w = per * SUBDIM
    codes = codebooks.shape[1]
    lanes = 128
    total = rows * rows_n * subs * 2
    swap = [(0, 1), (1, 0)]
    r = lax.axis_index("rep")
    params = pltpu.CompilerParams(vmem_limit_bytes=VMEM_BYTES)
    small = pltpu.CompilerParams(vmem_limit_bytes=VMEM_BYTES // 2)
    vmem = pl.BlockSpec(memory_space=pltpu.VMEM)

    cb = codebooks.transpose(0, 2, 1)
    cb_sent = lax.dynamic_slice_in_dim(cb, r * per, per, 0)
    cb_far = lax.ppermute(cb_sent, "sub", swap)
    vec_far = lax.ppermute(vectors, "rep", swap)

    y_shape = jax.ShapeDtypeStruct((subs, w, rows), BF16)
    y0, rott = pl.pallas_call(
        rotate_kernel,
        out_shape=(y_shape, jax.ShapeDtypeStruct((subs, w, width), BF16)),
        in_specs=[vmem] * 2,
        out_specs=(vmem, vmem),
        compiler_params=small,
        name="rotate",
    )(vectors, rotation)

    y1 = pl.pallas_call(
        rotate_more_kernel, out_shape=y_shape, in_specs=[vmem] * 2, out_specs=vmem, compiler_params=small, name="rotate_far"
    )(vec_far, rott)

    p_rows = (part // lanes) * w
    s_rows = (codes // lanes) * (w + SUBDIM)
    rec_shape = jax.ShapeDtypeStruct((w, rows), BF16)

    def quantize(k, cb_k):
        n_keep, n_send = (p_rows + s_rows, p_rows) if k == 0 else (p_rows, p_rows + s_rows)
        return pl.pallas_call(
            functools.partial(quantize_kernel, k=k, per=per),
            in_specs=[vmem] * 5,
            out_specs=[vmem] * 4,
            out_shape=[
                rec_shape,
                rec_shape,
                jax.ShapeDtypeStruct((n_keep, lanes), F32),
                jax.ShapeDtypeStruct((n_send, lanes), BF16),
            ],
            scratch_shapes=[pltpu.VMEM(((codes // lanes) * SUBDIM, lanes), F32)],
            compiler_params=params,
            name="quantize_near" if k == 0 else "quantize_far",
        )(cb_k, y0, y1, vectors, vec_far)

    mine1, other1, keep1, send1 = quantize(1, cb_far)
    got1 = lax.ppermute(send1, "sub", swap)
    theirs1 = lax.ppermute(other1, "rep", swap)
    mine0, other0, keep0, send0 = quantize(0, cb)
    got0 = lax.ppermute(send0, "sub", swap)
    theirs0 = lax.ppermute(other0, "rep", swap)
    theirs0, theirs1, got0 = lax.optimization_barrier((theirs0, theirs1, got0))

    reconstruction = pl.pallas_call(
        turn_kernel,
        out_shape=jax.ShapeDtypeStruct((rows, width), BF16),
        in_specs=[vmem] * 4,
        out_specs=vmem,
        scratch_shapes=[pltpu.VMEM((width, rows), BF16)],
        compiler_params=small,
        name="turn",
    )(mine0, mine1, theirs0, theirs1)

    def scatter(kept, got):
        size = (kept.shape[0] // rows_n, lanes)
        own, *sent = pl.pallas_call(
            functools.partial(pieces_kernel, n=rows_n),
            out_shape=[jax.ShapeDtypeStruct(size, F32)] + [jax.ShapeDtypeStruct(size, BF16)] * (rows_n - 1),
            in_specs=[vmem] * 2,
            out_specs=[vmem] * rows_n,
            scratch_shapes=[pltpu.VMEM(kept.shape, F32)],
            compiler_params=small,
            name="pieces",
        )(kept, got)
        return [own] + [exchange(x, rows_n, d) for x, d in zip(sent, apart)]

    def add_up(parts):
        return functools.reduce(lambda a, b: a + b.astype(F32), parts[1:], parts[0]).astype(BF16)

    apart = range(rows_n - 1, 0, -1)
    summed = jnp.concatenate([add_up(scatter(keep0, got1)), add_up(scatter(keep1, got0))], axis=0)
    summed, reconstruction = lax.optimization_barrier((summed, reconstruction))
    mine = [summed] + [exchange(summed, rows_n, d) for d in apart]
    theirs = [lax.ppermute(x, "rep", swap) for x in mine]

    any_spec = pl.BlockSpec(memory_space=pl.ANY)
    cross, new = pl.pallas_call(
        functools.partial(final_kernel, n=rows_n, per=per, total=total),
        out_shape=(jax.ShapeDtypeStruct((part, width), F32), jax.ShapeDtypeStruct(cb.shape, F32)),
        in_specs=[vmem] * (2 * rows_n + 1),
        out_specs=(any_spec, any_spec),
        scratch_shapes=[
            pltpu.VMEM((2, rows_n * summed.shape[0], lanes), F32),
            pltpu.VMEM((part, width), F32),
            pltpu.VMEM(cb.shape, F32),
            pltpu.SemaphoreType.DMA((part // lanes + 1,)),
        ],
        compiler_params=small,
        name="final",
    )(*mine, *theirs, cb)
    return reconstruction, new.transpose(0, 2, 1), cross


def solution(mesh):
    placed = (P(("dom", "row", "sub", "rep"), None), P("dom", None), P(("dom", "sub"), None, None))
    body = on_device if mesh.shape["sub"] == 2 and mesh.shape["row"] in (2, 4, 8) else any_mesh
    return jax.shard_map(
        body,
        mesh=mesh,
        in_specs=placed,
        out_specs=(
            P(("dom", "row", "sub", "rep"), None),
            P(("dom", "sub"), None, None),
            P(("dom", "sub"), None),
        ),
        check_vma=False,
    )
```

```python
import functools
import math

import jax
import jax.numpy as jnp
from jax import lax
from jax.experimental import pallas as pl
from jax.experimental.pallas import tpu as pltpu
from jax.sharding import PartitionSpec as P

SUBDIM = 16
SOFTNESS = 4.0
LOG2E = math.log2(math.e)
F32, BF16 = jnp.float32, jnp.bfloat16
VMEM_BYTES = 24 * 2**20
COST_BYTES = 2**23


def quantize_rows(block, codebook):
    block = block.astype(F32)
    cross_product = jnp.dot(codebook, block, precision=lax.Precision.HIGHEST)
    squared_norms = jnp.sum(codebook * codebook, axis=1)
    affinity_scores = (2.0 * cross_product - squared_norms[:, None]) / SOFTNESS
    weights = jax.nn.softmax(affinity_scores, axis=0)
    recon = jnp.dot(codebook.T, weights, precision=lax.Precision.HIGHEST)
    sums = lax.dot_general(weights, block, (((1,), (1,)), ((), ())), precision=lax.Precision.HIGHEST)
    return recon, sums, jnp.sum(weights, axis=1)


def any_mesh(vectors, rotation, codebooks):
    rows, width = vectors.shape
    groups = lax.axis_size("sub")
    part = width // groups
    rotated_t = lax.dot_general(
        rotation, vectors, (((0,), (1,)), ((), ())), preferred_element_type=F32
    ).astype(BF16)
    received = lax.all_to_all(rotated_t.reshape(groups, part, rows), "sub", split_axis=0, concat_axis=2, tiled=True)
    columns = received.shape[2]
    blocks = received.reshape(part // SUBDIM, SUBDIM, columns)
    recon, sums, counts = lax.map(lambda pair: quantize_rows(pair[0], pair[1]), (blocks, codebooks))
    sent = recon.astype(BF16).reshape(1, part, columns)
    recon_t = lax.all_to_all(sent, "sub", split_axis=2, concat_axis=0, tiled=True).reshape(width, rows)
    total = rows * lax.axis_size("row") * groups * lax.axis_size("rep")
    sums, counts = lax.psum((sums, counts), ("row", "rep"))
    term = lax.dot_general(vectors, recon_t, (((0,), (1,)), ((), ())), preferred_element_type=F32)
    whole = lax.psum(term, ("row", "sub", "rep"))
    mine = lax.dynamic_slice_in_dim(whole, lax.axis_index("sub") * part, part, 0)
    return recon_t.T, (sums + codebooks) / (counts[:, :, None] + 1.0), mine / total


def rotate_kernel(vec_ref, rot_ref, y_ref, rott_ref):
    s, r = lax.axis_index("sub"), lax.axis_index("rep")
    n, w = y_ref.shape[0], y_ref.shape[1]
    turned = rot_ref[...].T
    for h in range(n):
        for q in range(2):
            @pl.when(r == q)
            def _():
                rott_ref[(h + n - s) % n] = turned[(2 * h + q) * w : (2 * h + q + 1) * w]
    for k in range(n):
        y_ref[k] = lax.dot_general(
            rott_ref[k], vec_ref[...], (((1,), (1,)), ((), ())), preferred_element_type=F32
        ).astype(BF16)


def rotate_more_kernel(vec_ref, rott_ref, y_ref):
    for k in range(y_ref.shape[0]):
        y_ref[k] = lax.dot_general(
            rott_ref[k], vec_ref[...], (((1,), (1,)), ((), ())), preferred_element_type=F32
        ).astype(BF16)


def operands(c):
    codes = c.shape[1]
    scaled = c * (2.0 / SOFTNESS * LOG2E)
    hi = scaled.astype(BF16).astype(F32)
    mid = (scaled - hi).astype(BF16).astype(F32)
    lo = (scaled - hi) - mid
    n = jnp.sum(c * c, axis=0, keepdims=True) * (-LOG2E / SOFTNESS)
    n_hi = n.astype(BF16).astype(F32)
    n_mid = (n - n_hi).astype(BF16).astype(F32)
    n_lo = (n - n_hi) - n_mid
    row = lax.broadcasted_iota(jnp.int32, (SUBDIM, codes), 0)
    norms = jnp.where(row == 0, n_hi, jnp.where(row == 1, n_mid, jnp.where(row == 2, n_lo, 0.0)))
    a = jnp.concatenate([hi, mid, lo, norms], axis=0).T.astype(BF16)
    c_hi = c.astype(BF16)
    c_lo = (c - c_hi.astype(F32)).astype(BF16)
    b = jnp.concatenate([c_hi, c_lo, jnp.ones((SUBDIM, codes), BF16)], axis=0)
    return a, b


def quantize_kernel(cb_ref, y0_ref, y1_ref, v0_ref, v1_ref, rec0_ref, rec1_ref, keep_ref, send_ref, cnt, *, k, per):
    s, r = lax.axis_index("sub"), lax.axis_index("rep")
    codes = cb_ref.shape[2]
    cols = y0_ref.shape[2]
    w = per * SUBDIM
    lanes = 128
    part = v0_ref.shape[1] // 2
    base = r * per if k == 0 else 0
    p_rows = (part // lanes) * w
    sums_ref = keep_ref if k == 0 else send_ref
    ones = jnp.ones((SUBDIM, cols), BF16)
    ys, recs = (y0_ref, y1_ref), (rec0_ref, rec1_ref)
    cnt[...] = jnp.zeros_like(cnt)
    ab, acc = {}, {}

    def score(j, i):
        if j not in ab:
            ab[j] = operands(cb_ref[base + j])
        y = ys[i][k, SUBDIM * j : SUBDIM * (j + 1), :]
        return y, jnp.dot(ab[j][0], jnp.concatenate([y, y, y, ones], axis=0), preferred_element_type=F32)

    def spread(sc):
        return jnp.exp2(sc - jnp.max(sc, axis=0, keepdims=True)).astype(BF16)

    def rebuild(j, i, y, e):
        out = jnp.dot(ab[j][1], e, preferred_element_type=F32)
        inv = 1.0 / out[2 * SUBDIM :]
        recs[i][SUBDIM * j : SUBDIM * (j + 1), :] = ((out[:SUBDIM] + out[SUBDIM : 2 * SUBDIM]) * inv).astype(BF16)
        return jnp.concatenate([(y.astype(F32) * inv).astype(BF16), inv.astype(BF16)], axis=0)

    def gather(j, i, yz, e):
        sums = lax.dot_general(yz, e, (((1,), (1,)), ((), ())), preferred_element_type=F32)
        if i == 0:
            acc[j] = sums
            return
        sums = acc.pop(j) + sums
        for half in range(codes // lanes):
            at = p_rows + half * w + j * SUBDIM
            sums_ref[at : at + SUBDIM, :] = sums[:SUBDIM, half * lanes : (half + 1) * lanes].astype(sums_ref.dtype)
            at = half * SUBDIM + j
            cnt[at : at + 1, :] = sums[SUBDIM : SUBDIM + 1, half * lanes : (half + 1) * lanes]

    first = second = third = None
    for item in [(j, i) for j in range(per) for i in range(2)] + [None] * 3:
        new_first = (item, *score(*item)) if item is not None else None
        new_second = (first[0], first[1], spread(first[2])) if first is not None else None
        new_third = (second[0], rebuild(*second[0], second[1], second[2]), second[2]) if second is not None else None
        if third is not None:
            gather(*third[0], third[1], third[2])
        first, second, third = new_first, new_second, new_third

    at = p_rows + (codes // lanes) * w
    sums_ref[at : at + cnt.shape[0], :] = cnt[...].astype(sums_ref.dtype)
    cross = jnp.dot(rec0_ref[...], v0_ref[...], preferred_element_type=F32) + jnp.dot(
        rec1_ref[...], v1_ref[...], preferred_element_type=F32
    )
    for h in range(2):
        @pl.when(s == h)
        def _():
            for g in range(part // lanes):
                near = h * part + g * lanes
                far = (1 - h) * part + g * lanes
                keep_ref[g * w : (g + 1) * w, :] = cross[:, near : near + lanes]
                send_ref[g * w : (g + 1) * w, :] = cross[:, far : far + lanes].astype(BF16)


def turn_kernel(m0_ref, m1_ref, t0_ref, t1_ref, out_ref, buf):
    s, r = lax.axis_index("sub"), lax.axis_index("rep")
    w = m0_ref.shape[0]
    for k, (mine, theirs) in enumerate(((m0_ref, t0_ref), (m1_ref, t1_ref))):
        h = (s + k) % 2
        buf[pl.ds(pl.multiple_of((2 * h + r) * w, SUBDIM), w), :] = mine[...]
        buf[pl.ds(pl.multiple_of((2 * h + 1 - r) * w, SUBDIM), w), :] = theirs[...]
    out_ref[...] = buf[...].T


def final_kernel(*refs, n, per, total):
    pieces, (cb_ref, cross_hbm, new_hbm, buf, cross, new, sems) = refs[: 2 * n], refs[2 * n :]
    s, r, z = lax.axis_index("sub"), lax.axis_index("rep"), lax.axis_index("row")
    lanes = 128
    w = per * SUBDIM
    groups = cross.shape[0] // lanes
    halves = cb_ref.shape[2] // lanes
    near_rows = groups * w + halves * (w + SUBDIM)
    near, far = near_rows // n, groups * w // n
    for side in range(2):
        for i in range(n):
            ref = pieces[side * n + i]
            source = z ^ ((n - i) % n)
            buf[side, pl.ds(pl.multiple_of(source * near, 8), near), :] = ref[:near].astype(F32)
            buf[side, pl.ds(pl.multiple_of(near_rows + source * far, 8), far), :] = ref[near:].astype(F32)

    copies = []
    for g in range(groups):
        for h in range(2):
            for q in range(2):
                @pl.when((s == h) & (r == q))
                def _():
                    parts = []
                    for col in range(2):
                        start = (col ^ h) * near_rows + g * w
                        parts += [buf[rep ^ q, start : start + w, :] for rep in range(2)]
                    cross[g * lanes : (g + 1) * lanes, :] = jnp.concatenate(parts, axis=0).T * (1.0 / total)
        block = pl.ds(g * lanes, lanes)
        copies.append(pltpu.make_async_copy(cross.at[block], cross_hbm.at[block], sems.at[g]))
        copies[-1].start()
    first = groups * w
    for side in range(2):
        part = r if side == 0 else 1 - r
        for m in range(per):
            c = cb_ref[part * per + m]
            rows = [first + hf * w + m * SUBDIM for hf in range(halves)]
            sums = jnp.concatenate([buf[side, a : a + SUBDIM, :] for a in rows], axis=1)
            rows = [first + halves * w + hf * SUBDIM + m for hf in range(halves)]
            count = jnp.concatenate([buf[side, a : a + 1, :] for a in rows], axis=1)
            new[part * per + m] = (sums + c) / (count + 1.0)
    copies.append(pltpu.make_async_copy(new, new_hbm, sems.at[groups]))
    copies[-1].start()
    for copy in copies:
        copy.wait()


def pieces_kernel(kept_ref, got_ref, *refs, n):
    outs, total = refs[:n], refs[n]
    z = lax.axis_index("row")
    total[...] = kept_ref[...] + got_ref[...].astype(F32)
    size = outs[0].shape[0]
    for i, out in enumerate(outs):
        at = (z ^ ((n - i) % n)) * size
        out[...] = total[pl.ds(pl.multiple_of(at, 8), size), :].astype(out.dtype)


def exchange(x, n, d):
    return lax.ppermute(x, "row", [(i, i ^ d) for i in range(n)])


def on_device(vectors, rotation, codebooks):
    rows, width = vectors.shape
    subs, rows_n = 2, lax.axis_size("row")
    part = width // subs
    per = part // SUBDIM // 2
    w = per * SUBDIM
    codes = codebooks.shape[1]
    lanes = 128
    total = rows * rows_n * subs * 2
    swap = [(0, 1), (1, 0)]
    r = lax.axis_index("rep")
    params = pltpu.CompilerParams(vmem_limit_bytes=VMEM_BYTES)
    small = pltpu.CompilerParams(vmem_limit_bytes=VMEM_BYTES // 2)
    vmem = pl.BlockSpec(memory_space=pltpu.VMEM)

    cb = codebooks.transpose(0, 2, 1)
    cb_sent = lax.dynamic_slice_in_dim(cb, r * per, per, 0)
    cb_far = lax.ppermute(cb_sent, "sub", swap)
    vec_far = lax.ppermute(vectors, "rep", swap)

    y_shape = jax.ShapeDtypeStruct((subs, w, rows), BF16)
    y0, rott = pl.pallas_call(
        rotate_kernel,
        out_shape=(y_shape, jax.ShapeDtypeStruct((subs, w, width), BF16)),
        in_specs=[vmem] * 2,
        out_specs=(vmem, vmem),
        compiler_params=small,
        name="rotate",
    )(vectors, rotation)

    y1 = pl.pallas_call(
        rotate_more_kernel, out_shape=y_shape, in_specs=[vmem] * 2, out_specs=vmem, compiler_params=small, name="rotate_far"
    )(vec_far, rott)

    p_rows = (part // lanes) * w
    s_rows = (codes // lanes) * (w + SUBDIM)
    rec_shape = jax.ShapeDtypeStruct((w, rows), BF16)

    def quantize(k, cb_k):
        n_keep, n_send = (p_rows + s_rows, p_rows) if k == 0 else (p_rows, p_rows + s_rows)
        return pl.pallas_call(
            functools.partial(quantize_kernel, k=k, per=per),
            in_specs=[vmem] * 5,
            out_specs=[vmem] * 4,
            out_shape=[
                rec_shape,
                rec_shape,
                jax.ShapeDtypeStruct((n_keep, lanes), F32),
                jax.ShapeDtypeStruct((n_send, lanes), BF16),
            ],
            scratch_shapes=[pltpu.VMEM(((codes // lanes) * SUBDIM, lanes), F32)],
            compiler_params=params,
            cost_estimate=pl.CostEstimate(
                flops=per * codes * rows * 2 * 2 * (9 * SUBDIM) + 2 * w * 2 * rows * width,
                transcendentals=per * codes * rows * 2,
                bytes_accessed=COST_BYTES,
            ),
            name="quantize_near" if k == 0 else "quantize_far",
        )(cb_k, y0, y1, vectors, vec_far)

    mine1, other1, keep1, send1 = quantize(1, cb_far)
    got1 = lax.ppermute(send1, "sub", swap)
    theirs1 = lax.ppermute(other1, "rep", swap)
    mine0, other0, keep0, send0 = quantize(0, cb)
    got0 = lax.ppermute(send0, "sub", swap)
    theirs0 = lax.ppermute(other0, "rep", swap)

    reconstruction = pl.pallas_call(
        turn_kernel,
        out_shape=jax.ShapeDtypeStruct((rows, width), BF16),
        in_specs=[vmem] * 4,
        out_specs=vmem,
        scratch_shapes=[pltpu.VMEM((width, rows), BF16)],
        compiler_params=small,
        name="turn",
    )(mine0, mine1, theirs0, theirs1)

    def scatter(kept, got):
        size = (kept.shape[0] // rows_n, lanes)
        own, *sent = pl.pallas_call(
            functools.partial(pieces_kernel, n=rows_n),
            out_shape=[jax.ShapeDtypeStruct(size, F32)] + [jax.ShapeDtypeStruct(size, BF16)] * (rows_n - 1),
            in_specs=[vmem] * 2,
            out_specs=[vmem] * rows_n,
            scratch_shapes=[pltpu.VMEM(kept.shape, F32)],
            compiler_params=small,
            name="pieces",
        )(kept, got)
        return [own] + [exchange(x, rows_n, d) for x, d in zip(sent, apart)]

    def add_up(parts):
        return functools.reduce(lambda a, b: a + b.astype(F32), parts[1:], parts[0]).astype(BF16)

    apart = range(rows_n - 1, 0, -1)
    near = scatter(keep0, got1)
    near[0], got0, theirs1 = lax.optimization_barrier((near[0], got0, theirs1))
    summed = jnp.concatenate([add_up(near), add_up(scatter(keep1, got0))], axis=0)
    summed, reconstruction = lax.optimization_barrier((summed, reconstruction))
    mine = [summed] + [exchange(summed, rows_n, d) for d in apart]
    theirs = [lax.ppermute(x, "rep", swap) for x in mine]

    any_spec = pl.BlockSpec(memory_space=pl.ANY)
    cross, new = pl.pallas_call(
        functools.partial(final_kernel, n=rows_n, per=per, total=total),
        out_shape=(jax.ShapeDtypeStruct((part, width), F32), jax.ShapeDtypeStruct(cb.shape, F32)),
        in_specs=[vmem] * (2 * rows_n + 1),
        out_specs=(any_spec, any_spec),
        scratch_shapes=[
            pltpu.VMEM((2, rows_n * summed.shape[0], lanes), F32),
            pltpu.VMEM((part, width), F32),
            pltpu.VMEM(cb.shape, F32),
            pltpu.SemaphoreType.DMA((part // lanes + 1,)),
        ],
        compiler_params=small,
        name="final",
    )(*mine, *theirs, cb)
    return reconstruction, new.transpose(0, 2, 1), cross


def solution(mesh):
    placed = (P(("dom", "row", "sub", "rep"), None), P("dom", None), P(("dom", "sub"), None, None))
    body = on_device if mesh.shape["sub"] == 2 and mesh.shape["row"] in (2, 4, 8) else any_mesh
    return jax.shard_map(
        body,
        mesh=mesh,
        in_specs=placed,
        out_specs=(
            P(("dom", "row", "sub", "rep"), None),
            P(("dom", "sub"), None, None),
            P(("dom", "sub"), None),
        ),
        check_vma=False,
    )
```

```python
import functools
import math

import jax
import jax.numpy as jnp
from jax import lax
from jax.experimental import pallas as pl
from jax.experimental.pallas import tpu as pltpu
from jax.sharding import PartitionSpec as P

SUBDIM = 16
SOFTNESS = 4.0
LOG2E = math.log2(math.e)
F32, BF16 = jnp.float32, jnp.bfloat16
VMEM_BYTES = 24 * 2**20
HEAD = 3


def quantize_rows(block, codebook):
    block = block.astype(F32)
    cross_product = jnp.dot(codebook, block, precision=lax.Precision.HIGHEST)
    squared_norms = jnp.sum(codebook * codebook, axis=1)
    affinity_scores = (2.0 * cross_product - squared_norms[:, None]) / SOFTNESS
    weights = jax.nn.softmax(affinity_scores, axis=0)
    recon = jnp.dot(codebook.T, weights, precision=lax.Precision.HIGHEST)
    sums = lax.dot_general(weights, block, (((1,), (1,)), ((), ())), precision=lax.Precision.HIGHEST)
    return recon, sums, jnp.sum(weights, axis=1)


def any_mesh(vectors, rotation, codebooks):
    rows, width = vectors.shape
    groups = lax.axis_size("sub")
    part = width // groups
    rotated_t = lax.dot_general(
        rotation, vectors, (((0,), (1,)), ((), ())), preferred_element_type=F32
    ).astype(BF16)
    received = lax.all_to_all(rotated_t.reshape(groups, part, rows), "sub", split_axis=0, concat_axis=2, tiled=True)
    columns = received.shape[2]
    blocks = received.reshape(part // SUBDIM, SUBDIM, columns)
    recon, sums, counts = lax.map(lambda pair: quantize_rows(pair[0], pair[1]), (blocks, codebooks))
    sent = recon.astype(BF16).reshape(1, part, columns)
    recon_t = lax.all_to_all(sent, "sub", split_axis=2, concat_axis=0, tiled=True).reshape(width, rows)
    total = rows * lax.axis_size("row") * groups * lax.axis_size("rep")
    sums, counts = lax.psum((sums, counts), ("row", "rep"))
    term = lax.dot_general(vectors, recon_t, (((0,), (1,)), ((), ())), preferred_element_type=F32)
    whole = lax.psum(term, ("row", "sub", "rep"))
    mine = lax.dynamic_slice_in_dim(whole, lax.axis_index("sub") * part, part, 0)
    return recon_t.T, (sums + codebooks) / (counts[:, :, None] + 1.0), mine / total


def rotate_kernel(vec_ref, rot_ref, y_ref, rott_ref):
    s, r = lax.axis_index("sub"), lax.axis_index("rep")
    n, w = y_ref.shape[0], y_ref.shape[1]
    turned = rot_ref[...].T
    for h in range(n):
        for q in range(2):
            @pl.when(r == q)
            def _():
                rott_ref[(h + n - s) % n] = turned[(2 * h + q) * w : (2 * h + q + 1) * w]
    for k in range(n):
        y_ref[k] = lax.dot_general(
            rott_ref[k], vec_ref[...], (((1,), (1,)), ((), ())), preferred_element_type=F32
        ).astype(BF16)


def rotate_more_kernel(vec_ref, rott_ref, y_ref):
    for k in range(y_ref.shape[0]):
        y_ref[k] = lax.dot_general(
            rott_ref[k], vec_ref[...], (((1,), (1,)), ((), ())), preferred_element_type=F32
        ).astype(BF16)


def operands(c):
    codes = c.shape[1]
    scaled = c * (2.0 / SOFTNESS * LOG2E)
    hi = scaled.astype(BF16).astype(F32)
    mid = (scaled - hi).astype(BF16).astype(F32)
    lo = (scaled - hi) - mid
    n = jnp.sum(c * c, axis=0, keepdims=True) * (-LOG2E / SOFTNESS)
    n_hi = n.astype(BF16).astype(F32)
    n_mid = (n - n_hi).astype(BF16).astype(F32)
    n_lo = (n - n_hi) - n_mid
    row = lax.broadcasted_iota(jnp.int32, (SUBDIM, codes), 0)
    norms = jnp.where(row == 0, n_hi, jnp.where(row == 1, n_mid, jnp.where(row == 2, n_lo, 0.0)))
    a = jnp.concatenate([hi, mid, lo, norms], axis=0).T.astype(BF16)
    c_hi = c.astype(BF16)
    c_lo = (c - c_hi.astype(F32)).astype(BF16)
    b = jnp.concatenate([c_hi, c_lo, jnp.ones((SUBDIM, codes), BF16)], axis=0)
    return a, b


def quantize_kernel(*refs, k, per, first, last):
    cb_ref, y0_ref, y1_ref = refs[:3]
    refs = refs[3:]
    s, r = lax.axis_index("sub"), lax.axis_index("rep")
    codes = cb_ref.shape[2]
    cols = y0_ref.shape[2]
    w = per * SUBDIM
    lanes = 128
    halves = codes // lanes
    whole = last == per
    base = r * per if k == 0 else 0
    if whole:
        v0_ref, v1_ref, *refs = refs
        part = v0_ref.shape[1] // 2
        p_rows = (part // lanes) * w
        if first:
            *head, rec0_ref, rec1_ref, keep_ref, send_ref, cnt = refs
        else:
            rec0_ref, rec1_ref, keep_ref, send_ref, cnt = refs
        sums_ref = keep_ref if k == 0 else send_ref
    else:
        rec0_ref, rec1_ref, sums_ref, cnt = refs
        p_rows = 0
    stride = w if whole else last * SUBDIM
    ones = jnp.ones((SUBDIM, cols), BF16)
    ys, recs = (y0_ref, y1_ref), (rec0_ref, rec1_ref)
    if first:
        done = first * SUBDIM
        rec0_ref[:done, :] = head[0][...]
        rec1_ref[:done, :] = head[1][...]
        for half in range(halves):
            at = p_rows + half * stride
            sums_ref[at : at + done, :] = head[2][half * done : (half + 1) * done, :].astype(sums_ref.dtype)
        cnt[...] = head[3][...]
    else:
        cnt[...] = jnp.zeros_like(cnt)
    ab, acc = {}, {}

    def score(j, i):
        if j not in ab:
            ab[j] = operands(cb_ref[base + j])
        y = ys[i][k, SUBDIM * j : SUBDIM * (j + 1), :]
        return y, jnp.dot(ab[j][0], jnp.concatenate([y, y, y, ones], axis=0), preferred_element_type=F32)

    def spread(sc):
        return jnp.exp2(sc - jnp.max(sc, axis=0, keepdims=True)).astype(BF16)

    def rebuild(j, i, y, e):
        out = jnp.dot(ab[j][1], e, preferred_element_type=F32)
        inv = 1.0 / out[2 * SUBDIM :]
        recs[i][SUBDIM * j : SUBDIM * (j + 1), :] = ((out[:SUBDIM] + out[SUBDIM : 2 * SUBDIM]) * inv).astype(BF16)
        return jnp.concatenate([(y.astype(F32) * inv).astype(BF16), inv.astype(BF16)], axis=0)

    def gather(j, i, yz, e):
        sums = lax.dot_general(yz, e, (((1,), (1,)), ((), ())), preferred_element_type=F32)
        if i == 0:
            acc[j] = sums
            return
        sums = acc.pop(j) + sums
        for half in range(halves):
            at = p_rows + half * stride + j * SUBDIM
            sums_ref[at : at + SUBDIM, :] = sums[:SUBDIM, half * lanes : (half + 1) * lanes].astype(sums_ref.dtype)
            at = half * SUBDIM + j
            cnt[at : at + 1, :] = sums[SUBDIM : SUBDIM + 1, half * lanes : (half + 1) * lanes]

    one = two = three = None
    for item in [(j, i) for j in range(first, last) for i in range(2)] + [None] * 3:
        new_one = (item, *score(*item)) if item is not None else None
        new_two = (one[0], one[1], spread(one[2])) if one is not None else None
        new_three = (two[0], rebuild(*two[0], two[1], two[2]), two[2]) if two is not None else None
        if three is not None:
            gather(*three[0], three[1], three[2])
        one, two, three = new_one, new_two, new_three
    if not whole:
        return

    at = p_rows + halves * w
    sums_ref[at : at + cnt.shape[0], :] = cnt[...].astype(sums_ref.dtype)
    cross = jnp.dot(rec0_ref[...], v0_ref[...], preferred_element_type=F32) + jnp.dot(
        rec1_ref[...], v1_ref[...], preferred_element_type=F32
    )
    for h in range(2):
        @pl.when(s == h)
        def _():
            for g in range(part // lanes):
                near = h * part + g * lanes
                far = (1 - h) * part + g * lanes
                keep_ref[g * w : (g + 1) * w, :] = cross[:, near : near + lanes]
                send_ref[g * w : (g + 1) * w, :] = cross[:, far : far + lanes].astype(BF16)


def turn_kernel(m0_ref, m1_ref, t0_ref, t1_ref, out_ref, buf):
    s, r = lax.axis_index("sub"), lax.axis_index("rep")
    w = m0_ref.shape[0]
    for k, (mine, theirs) in enumerate(((m0_ref, t0_ref), (m1_ref, t1_ref))):
        h = (s + k) % 2
        buf[pl.ds(pl.multiple_of((2 * h + r) * w, SUBDIM), w), :] = mine[...]
        buf[pl.ds(pl.multiple_of((2 * h + 1 - r) * w, SUBDIM), w), :] = theirs[...]
    out_ref[...] = buf[...].T


def final_kernel(*refs, n, per, total):
    held, (cb_ref, cross_hbm, new_hbm, buf, cross, new, sems) = refs[:4], refs[4:]
    s, r, z = lax.axis_index("sub"), lax.axis_index("rep"), lax.axis_index("row")
    lanes = 128
    w = per * SUBDIM
    groups = cross.shape[0] // lanes
    halves = cb_ref.shape[2] // lanes
    near_rows = groups * w + halves * (w + SUBDIM)
    near, far = near_rows // n, groups * w // n
    for side in range(2):
        near_ref, far_ref = held[2 * side : 2 * side + 2]
        for i in range(n):
            source = z ^ ((n - i) % n)
            buf[side, pl.ds(pl.multiple_of(source * near, 8), near), :] = near_ref[i].astype(F32)
            buf[side, pl.ds(pl.multiple_of(near_rows + source * far, 8), far), :] = far_ref[i].astype(F32)

    copies = []
    for g in range(groups):
        for h in range(2):
            for q in range(2):
                @pl.when((s == h) & (r == q))
                def _():
                    parts = []
                    for col in range(2):
                        start = (col ^ h) * near_rows + g * w
                        parts += [buf[rep ^ q, start : start + w, :] for rep in range(2)]
                    cross[g * lanes : (g + 1) * lanes, :] = jnp.concatenate(parts, axis=0).T * (1.0 / total)
        block = pl.ds(g * lanes, lanes)
        copies.append(pltpu.make_async_copy(cross.at[block], cross_hbm.at[block], sems.at[g]))
        copies[-1].start()
    first = groups * w
    for side in range(2):
        part = r if side == 0 else 1 - r
        for m in range(per):
            c = cb_ref[part * per + m]
            rows = [first + hf * w + m * SUBDIM for hf in range(halves)]
            sums = jnp.concatenate([buf[side, a : a + SUBDIM, :] for a in rows], axis=1)
            rows = [first + halves * w + hf * SUBDIM + m for hf in range(halves)]
            count = jnp.concatenate([buf[side, a : a + 1, :] for a in rows], axis=1)
            new[part * per + m] = (sums + c) / (count + 1.0)
    copies.append(pltpu.make_async_copy(new, new_hbm, sems.at[groups]))
    copies[-1].start()
    for copy in copies:
        copy.wait()


def pieces_kernel(kept_ref, got_ref, *refs, n):
    outs, total = refs[:n], refs[n]
    z = lax.axis_index("row")
    total[...] = kept_ref[...] + got_ref[...].astype(F32)
    size = outs[0].shape[0]
    for i, out in enumerate(outs):
        at = (z ^ ((n - i) % n)) * size
        out[...] = total[pl.ds(pl.multiple_of(at, 8), size), :].astype(out.dtype)


def exchange(x, n, d):
    return lax.ppermute(x, "row", [(i, i ^ d) for i in range(n)])


def on_device(vectors, rotation, codebooks):
    rows, width = vectors.shape
    subs, rows_n = 2, lax.axis_size("row")
    part = width // subs
    per = part // SUBDIM // 2
    w = per * SUBDIM
    codes = codebooks.shape[1]
    lanes = 128
    total = rows * rows_n * subs * 2
    swap = [(0, 1), (1, 0)]
    params = pltpu.CompilerParams(vmem_limit_bytes=VMEM_BYTES)
    small = pltpu.CompilerParams(vmem_limit_bytes=VMEM_BYTES // 2)
    vmem = pl.BlockSpec(memory_space=pltpu.VMEM)

    cb = codebooks.transpose(0, 2, 1)
    cb_sent = lax.dynamic_slice_in_dim(cb, lax.axis_index("rep") * per, per, 0)
    cb_far = lax.ppermute(cb_sent, "sub", swap)
    vec_far = lax.ppermute(vectors, "rep", swap)

    y_shape = jax.ShapeDtypeStruct((subs, w, rows), BF16)
    y0, rott = pl.pallas_call(
        rotate_kernel,
        out_shape=(y_shape, jax.ShapeDtypeStruct((subs, w, width), BF16)),
        in_specs=[vmem] * 2,
        out_specs=(vmem, vmem),
        compiler_params=small,
        name="rotate",
    )(vectors, rotation)

    y1 = pl.pallas_call(
        rotate_more_kernel, out_shape=y_shape, in_specs=[vmem] * 2, out_specs=vmem, compiler_params=small, name="rotate_far"
    )(vec_far, rott)

    p_rows = (part // lanes) * w
    s_rows = (codes // lanes) * (w + SUBDIM)
    rec_shape = jax.ShapeDtypeStruct((w, rows), BF16)

    cnt_shape = ((codes // lanes) * SUBDIM, lanes)

    def cost(count, cross):
        return pl.CostEstimate(
            flops=count * codes * rows * 2 * 2 * (9 * SUBDIM) + cross * 2 * w * 2 * rows * width,
            transcendentals=count * codes * rows * 2,
            bytes_accessed=2**23,
        )

    def quantize(k, cb_k, first=0, head=()):
        n_keep, n_send = (p_rows + s_rows, p_rows) if k == 0 else (p_rows, p_rows + s_rows)
        return pl.pallas_call(
            functools.partial(quantize_kernel, k=k, per=per, first=first, last=per),
            in_specs=[vmem] * (5 + len(head)),
            out_specs=[vmem] * 4,
            out_shape=[
                rec_shape,
                rec_shape,
                jax.ShapeDtypeStruct((n_keep, lanes), F32),
                jax.ShapeDtypeStruct((n_send, lanes), BF16),
            ],
            scratch_shapes=[pltpu.VMEM(cnt_shape, F32)],
            compiler_params=params,
            cost_estimate=cost(per - first, 1),
            name="quantize_near" if k == 0 else "quantize_far",
        )(cb_k, y0, y1, vectors, vec_far, *head)

    head = ()
    if HEAD:
        early = jax.ShapeDtypeStruct((HEAD * SUBDIM, rows), BF16)
        head = pl.pallas_call(
            functools.partial(quantize_kernel, k=0, per=per, first=0, last=HEAD),
            in_specs=[vmem] * 3,
            out_specs=[vmem] * 4,
            out_shape=[
                early,
                early,
                jax.ShapeDtypeStruct(((codes // lanes) * HEAD * SUBDIM, lanes), F32),
                jax.ShapeDtypeStruct(cnt_shape, F32),
            ],
            compiler_params=params,
            cost_estimate=cost(HEAD, 0),
            name="quantize_head",
        )(cb, y0, y1)
        cb_far, *head = lax.optimization_barrier((cb_far, *head))
    mine1, other1, keep1, send1 = quantize(1, cb_far)
    got1 = lax.ppermute(send1, "sub", swap)
    theirs1 = lax.ppermute(other1, "rep", swap)
    mine0, other0, keep0, send0 = quantize(0, cb, HEAD, head)
    got0 = lax.ppermute(send0, "sub", swap)
    theirs0 = lax.ppermute(other0, "rep", swap)

    def scatter(kept, got):
        size = (kept.shape[0] // rows_n, lanes)
        own, *sent = pl.pallas_call(
            functools.partial(pieces_kernel, n=rows_n),
            out_shape=[jax.ShapeDtypeStruct(size, F32)] + [jax.ShapeDtypeStruct(size, BF16)] * (rows_n - 1),
            in_specs=[vmem] * 2,
            out_specs=[vmem] * rows_n,
            scratch_shapes=[pltpu.VMEM(kept.shape, F32)],
            compiler_params=small,
            name="pieces",
        )(kept, got)
        return [own] + [exchange(x, rows_n, d) for x, d in zip(sent, apart)]

    def add_up(parts):
        return functools.reduce(lambda a, b: a + b.astype(F32), parts[1:], parts[0]).astype(BF16)

    apart = range(rows_n - 1, 0, -1)
    near = scatter(keep0, got1)
    near[0], got0, theirs1 = lax.optimization_barrier((near[0], got0, theirs1))
    far = scatter(keep1, got0)

    def spread_out(x):
        return [x] + [exchange(x, rows_n, d) for d in apart]

    near_held = jnp.stack(spread_out(add_up(near)))
    near_theirs = lax.ppermute(near_held, "rep", swap)
    near_held, theirs0 = lax.optimization_barrier((near_held, theirs0))

    reconstruction = pl.pallas_call(
        turn_kernel,
        out_shape=jax.ShapeDtypeStruct((rows, width), BF16),
        in_specs=[vmem] * 4,
        out_specs=vmem,
        scratch_shapes=[pltpu.VMEM((width, rows), BF16)],
        compiler_params=small,
        name="turn",
    )(mine0, mine1, theirs0, theirs1)

    far_held = spread_out(add_up(far))
    *far_held, reconstruction = lax.optimization_barrier((*far_held, reconstruction))
    far_held = jnp.stack(far_held)
    far_theirs = lax.ppermute(far_held, "rep", swap)

    any_spec = pl.BlockSpec(memory_space=pl.ANY)
    cross, new = pl.pallas_call(
        functools.partial(final_kernel, n=rows_n, per=per, total=total),
        out_shape=(jax.ShapeDtypeStruct((part, width), F32), jax.ShapeDtypeStruct(cb.shape, F32)),
        in_specs=[vmem] * 5,
        out_specs=(any_spec, any_spec),
        scratch_shapes=[
            pltpu.VMEM((2, 2 * p_rows + s_rows, lanes), F32),
            pltpu.VMEM((part, width), F32),
            pltpu.VMEM(cb.shape, F32),
            pltpu.SemaphoreType.DMA((part // lanes + 1,)),
        ],
        compiler_params=small,
        name="final",
    )(near_held, far_held, near_theirs, far_theirs, cb)
    return reconstruction, new.transpose(0, 2, 1), cross


def solution(mesh):
    placed = (P(("dom", "row", "sub", "rep"), None), P("dom", None), P(("dom", "sub"), None, None))
    body = on_device if mesh.shape["sub"] == 2 and mesh.shape["row"] in (2, 4, 8) else any_mesh
    return jax.shard_map(
        body,
        mesh=mesh,
        in_specs=placed,
        out_specs=(
            P(("dom", "row", "sub", "rep"), None),
            P(("dom", "sub"), None, None),
            P(("dom", "sub"), None),
        ),
        check_vma=False,
    )
```

```python
import functools
import math

import jax
import jax.numpy as jnp
from jax import lax
from jax.experimental import pallas as pl
from jax.experimental.pallas import tpu as pltpu
from jax.sharding import PartitionSpec as P

SUBDIM = 16
SOFTNESS = 4.0
LOG2E = math.log2(math.e)
F32, BF16 = jnp.float32, jnp.bfloat16
VMEM_BYTES = 24 * 2**20
HEAD = 3


def quantize_rows(block, codebook):
    block = block.astype(F32)
    cross_product = jnp.dot(codebook, block, precision=lax.Precision.HIGHEST)
    squared_norms = jnp.sum(codebook * codebook, axis=1)
    affinity_scores = (2.0 * cross_product - squared_norms[:, None]) / SOFTNESS
    weights = jax.nn.softmax(affinity_scores, axis=0)
    recon = jnp.dot(codebook.T, weights, precision=lax.Precision.HIGHEST)
    sums = lax.dot_general(weights, block, (((1,), (1,)), ((), ())), precision=lax.Precision.HIGHEST)
    return recon, sums, jnp.sum(weights, axis=1)


def any_mesh(vectors, rotation, codebooks):
    rows, width = vectors.shape
    groups = lax.axis_size("sub")
    part = width // groups
    rotated_t = lax.dot_general(
        rotation, vectors, (((0,), (1,)), ((), ())), preferred_element_type=F32
    ).astype(BF16)
    received = lax.all_to_all(rotated_t.reshape(groups, part, rows), "sub", split_axis=0, concat_axis=2, tiled=True)
    columns = received.shape[2]
    blocks = received.reshape(part // SUBDIM, SUBDIM, columns)
    recon, sums, counts = lax.map(lambda pair: quantize_rows(pair[0], pair[1]), (blocks, codebooks))
    sent = recon.astype(BF16).reshape(1, part, columns)
    recon_t = lax.all_to_all(sent, "sub", split_axis=2, concat_axis=0, tiled=True).reshape(width, rows)
    total = rows * lax.axis_size("row") * groups * lax.axis_size("rep")
    sums, counts = lax.psum((sums, counts), ("row", "rep"))
    term = lax.dot_general(vectors, recon_t, (((0,), (1,)), ((), ())), preferred_element_type=F32)
    whole = lax.psum(term, ("row", "sub", "rep"))
    mine = lax.dynamic_slice_in_dim(whole, lax.axis_index("sub") * part, part, 0)
    return recon_t.T, (sums + codebooks) / (counts[:, :, None] + 1.0), mine / total


def rotate_kernel(vec_ref, rot_ref, y_ref, rott_ref):
    s, r = lax.axis_index("sub"), lax.axis_index("rep")
    n, w = y_ref.shape[0], y_ref.shape[1]
    turned = rot_ref[...].T
    for h in range(n):
        for q in range(2):
            @pl.when(r == q)
            def _():
                rott_ref[(h + n - s) % n] = turned[(2 * h + q) * w : (2 * h + q + 1) * w]
    for k in range(n):
        y_ref[k] = lax.dot_general(
            rott_ref[k], vec_ref[...], (((1,), (1,)), ((), ())), preferred_element_type=F32
        ).astype(BF16)


def rotate_more_kernel(vec_ref, rott_ref, y_ref):
    for k in range(y_ref.shape[0]):
        y_ref[k] = lax.dot_general(
            rott_ref[k], vec_ref[...], (((1,), (1,)), ((), ())), preferred_element_type=F32
        ).astype(BF16)


def operands(c):
    codes = c.shape[1]
    scaled = c * (2.0 / SOFTNESS * LOG2E)
    hi = scaled.astype(BF16).astype(F32)
    mid = (scaled - hi).astype(BF16).astype(F32)
    lo = (scaled - hi) - mid
    n = jnp.sum(c * c, axis=0, keepdims=True) * (-LOG2E / SOFTNESS)
    n_hi = n.astype(BF16).astype(F32)
    n_mid = (n - n_hi).astype(BF16).astype(F32)
    n_lo = (n - n_hi) - n_mid
    row = lax.broadcasted_iota(jnp.int32, (SUBDIM, codes), 0)
    norms = jnp.where(row == 0, n_hi, jnp.where(row == 1, n_mid, jnp.where(row == 2, n_lo, 0.0)))
    a = jnp.concatenate([hi, mid, lo, norms], axis=0).T.astype(BF16)
    c_hi = c.astype(BF16)
    c_lo = (c - c_hi.astype(F32)).astype(BF16)
    b = jnp.concatenate([c_hi, c_lo, jnp.ones((SUBDIM, codes), BF16)], axis=0)
    return a, b


def quantize_kernel(*refs, k, per, first, last):
    cb_ref, y0_ref, y1_ref = refs[:3]
    refs = refs[3:]
    s, r = lax.axis_index("sub"), lax.axis_index("rep")
    codes = cb_ref.shape[2]
    cols = y0_ref.shape[2]
    w = per * SUBDIM
    lanes = 128
    halves = codes // lanes
    whole = last == per
    base = r * per if k == 0 else 0
    if whole:
        v0_ref, v1_ref, *refs = refs
        part = v0_ref.shape[1] // 2
        p_rows = (part // lanes) * w
        if first:
            *head, rec0_ref, rec1_ref, keep_ref, send_ref, cnt = refs
        else:
            rec0_ref, rec1_ref, keep_ref, send_ref, cnt = refs
        sums_ref = keep_ref if k == 0 else send_ref
    else:
        rec0_ref, rec1_ref, sums_ref, cnt = refs
        p_rows = 0
    stride = w if whole else last * SUBDIM
    ones = jnp.ones((SUBDIM, cols), BF16)
    ys, recs = (y0_ref, y1_ref), (rec0_ref, rec1_ref)
    if first:
        done = first * SUBDIM
        rec0_ref[:done, :] = head[0][...]
        rec1_ref[:done, :] = head[1][...]
        for half in range(halves):
            at = p_rows + half * stride
            sums_ref[at : at + done, :] = head[2][half * done : (half + 1) * done, :].astype(sums_ref.dtype)
        cnt[...] = head[3][...]
    else:
        cnt[...] = jnp.zeros_like(cnt)
    ab, acc = {}, {}

    def score(j, i):
        if j not in ab:
            ab[j] = operands(cb_ref[base + j])
        y = ys[i][k, SUBDIM * j : SUBDIM * (j + 1), :]
        return y, jnp.dot(ab[j][0], jnp.concatenate([y, y, y, ones], axis=0), preferred_element_type=F32)

    def spread(sc):
        return jnp.exp2(sc - jnp.max(sc, axis=0, keepdims=True)).astype(BF16)

    def rebuild(j, i, y, e):
        out = jnp.dot(ab[j][1], e, preferred_element_type=F32)
        inv = 1.0 / out[2 * SUBDIM :]
        recs[i][SUBDIM * j : SUBDIM * (j + 1), :] = ((out[:SUBDIM] + out[SUBDIM : 2 * SUBDIM]) * inv).astype(BF16)
        return jnp.concatenate([(y.astype(F32) * inv).astype(BF16), inv.astype(BF16)], axis=0)

    def gather(j, i, yz, e):
        sums = lax.dot_general(yz, e, (((1,), (1,)), ((), ())), preferred_element_type=F32)
        if i == 0:
            acc[j] = sums
            return
        sums = acc.pop(j) + sums
        for half in range(halves):
            at = p_rows + half * stride + j * SUBDIM
            sums_ref[at : at + SUBDIM, :] = sums[:SUBDIM, half * lanes : (half + 1) * lanes].astype(sums_ref.dtype)
            at = half * SUBDIM + j
            cnt[at : at + 1, :] = sums[SUBDIM : SUBDIM + 1, half * lanes : (half + 1) * lanes]

    one = two = three = None
    for item in [(j, i) for j in range(first, last) for i in range(2)] + [None] * 3:
        new_one = (item, *score(*item)) if item is not None else None
        new_two = (one[0], one[1], spread(one[2])) if one is not None else None
        new_three = (two[0], rebuild(*two[0], two[1], two[2]), two[2]) if two is not None else None
        if three is not None:
            gather(*three[0], three[1], three[2])
        one, two, three = new_one, new_two, new_three
    if not whole:
        return

    at = p_rows + halves * w
    sums_ref[at : at + cnt.shape[0], :] = cnt[...].astype(sums_ref.dtype)
    cross = jnp.dot(rec0_ref[...], v0_ref[...], preferred_element_type=F32) + jnp.dot(
        rec1_ref[...], v1_ref[...], preferred_element_type=F32
    )
    for h in range(2):
        @pl.when(s == h)
        def _():
            for g in range(part // lanes):
                near = h * part + g * lanes
                far = (1 - h) * part + g * lanes
                keep_ref[g * w : (g + 1) * w, :] = cross[:, near : near + lanes]
                send_ref[g * w : (g + 1) * w, :] = cross[:, far : far + lanes].astype(BF16)


def turn_kernel(m0_ref, m1_ref, t0_ref, t1_ref, out_ref, buf):
    s, r = lax.axis_index("sub"), lax.axis_index("rep")
    w = m0_ref.shape[0]
    for k, (mine, theirs) in enumerate(((m0_ref, t0_ref), (m1_ref, t1_ref))):
        h = (s + k) % 2
        buf[pl.ds(pl.multiple_of((2 * h + r) * w, SUBDIM), w), :] = mine[...]
        buf[pl.ds(pl.multiple_of((2 * h + 1 - r) * w, SUBDIM), w), :] = theirs[...]
    out_ref[...] = buf[...].T


def final_kernel(*refs, n, per, total):
    pieces, (cb_ref, cross_hbm, new_hbm, buf, cross, new, sems) = refs[: 2 * n], refs[2 * n :]
    s, r, z = lax.axis_index("sub"), lax.axis_index("rep"), lax.axis_index("row")
    lanes = 128
    w = per * SUBDIM
    groups = cross.shape[0] // lanes
    halves = cb_ref.shape[2] // lanes
    near_rows = groups * w + halves * (w + SUBDIM)
    near, far = near_rows // n, groups * w // n
    for side in range(2):
        for i in range(n):
            ref = pieces[side * n + i]
            source = z ^ ((n - i) % n)
            buf[side, pl.ds(pl.multiple_of(source * near, 8), near), :] = ref[:near].astype(F32)
            buf[side, pl.ds(pl.multiple_of(near_rows + source * far, 8), far), :] = ref[near:].astype(F32)

    copies = []
    for g in range(groups):
        for h in range(2):
            for q in range(2):
                @pl.when((s == h) & (r == q))
                def _():
                    parts = []
                    for col in range(2):
                        start = (col ^ h) * near_rows + g * w
                        parts += [buf[rep ^ q, start : start + w, :] for rep in range(2)]
                    cross[g * lanes : (g + 1) * lanes, :] = jnp.concatenate(parts, axis=0).T * (1.0 / total)
        block = pl.ds(g * lanes, lanes)
        copies.append(pltpu.make_async_copy(cross.at[block], cross_hbm.at[block], sems.at[g]))
        copies[-1].start()
    first = groups * w
    for side in range(2):
        part = r if side == 0 else 1 - r
        for m in range(per):
            c = cb_ref[part * per + m]
            rows = [first + hf * w + m * SUBDIM for hf in range(halves)]
            sums = jnp.concatenate([buf[side, a : a + SUBDIM, :] for a in rows], axis=1)
            rows = [first + halves * w + hf * SUBDIM + m for hf in range(halves)]
            count = jnp.concatenate([buf[side, a : a + 1, :] for a in rows], axis=1)
            new[part * per + m] = (sums + c) / (count + 1.0)
    copies.append(pltpu.make_async_copy(new, new_hbm, sems.at[groups]))
    copies[-1].start()
    for copy in copies:
        copy.wait()


def pieces_kernel(kept_ref, got_ref, own_ref, sent_ref, total):
    z = lax.axis_index("row")
    total[...] = kept_ref[...] + got_ref[...].astype(F32)
    size = own_ref.shape[1]
    for i in range(2):
        own_ref[i] = total[pl.ds(pl.multiple_of((z ^ (2 * i)) * size, 8), size), :]
        sent_ref[i] = total[pl.ds(pl.multiple_of((z ^ (2 * i + 1)) * size, 8), size), :].astype(BF16)


def exchange(x, n, d):
    return lax.ppermute(x, "row", [(i, i ^ d) for i in range(n)])


def on_device(vectors, rotation, codebooks):
    rows, width = vectors.shape
    subs, rows_n = 2, lax.axis_size("row")
    part = width // subs
    per = part // SUBDIM // 2
    w = per * SUBDIM
    codes = codebooks.shape[1]
    lanes = 128
    total = rows * rows_n * subs * 2
    swap = [(0, 1), (1, 0)]
    params = pltpu.CompilerParams(vmem_limit_bytes=VMEM_BYTES)
    small = pltpu.CompilerParams(vmem_limit_bytes=VMEM_BYTES // 2)
    vmem = pl.BlockSpec(memory_space=pltpu.VMEM)

    cb = codebooks.transpose(0, 2, 1)
    cb_sent = lax.dynamic_slice_in_dim(cb, lax.axis_index("rep") * per, per, 0)
    cb_far = lax.ppermute(cb_sent, "sub", swap)
    vec_far = lax.ppermute(vectors, "rep", swap)

    y_shape = jax.ShapeDtypeStruct((subs, w, rows), BF16)
    y0, rott = pl.pallas_call(
        rotate_kernel,
        out_shape=(y_shape, jax.ShapeDtypeStruct((subs, w, width), BF16)),
        in_specs=[vmem] * 2,
        out_specs=(vmem, vmem),
        compiler_params=small,
        name="rotate",
    )(vectors, rotation)

    y1 = pl.pallas_call(
        rotate_more_kernel, out_shape=y_shape, in_specs=[vmem] * 2, out_specs=vmem, compiler_params=small, name="rotate_far"
    )(vec_far, rott)

    p_rows = (part // lanes) * w
    s_rows = (codes // lanes) * (w + SUBDIM)
    rec_shape = jax.ShapeDtypeStruct((w, rows), BF16)

    cnt_shape = ((codes // lanes) * SUBDIM, lanes)

    def cost(count, cross):
        return pl.CostEstimate(
            flops=count * codes * rows * 2 * 2 * (9 * SUBDIM) + cross * 2 * w * 2 * rows * width,
            transcendentals=count * codes * rows * 2,
            bytes_accessed=2**23,
        )

    def quantize(k, cb_k, first=0, head=()):
        n_keep, n_send = (p_rows + s_rows, p_rows) if k == 0 else (p_rows, p_rows + s_rows)
        return pl.pallas_call(
            functools.partial(quantize_kernel, k=k, per=per, first=first, last=per),
            in_specs=[vmem] * (5 + len(head)),
            out_specs=[vmem] * 4,
            out_shape=[
                rec_shape,
                rec_shape,
                jax.ShapeDtypeStruct((n_keep, lanes), F32),
                jax.ShapeDtypeStruct((n_send, lanes), BF16),
            ],
            scratch_shapes=[pltpu.VMEM(cnt_shape, F32)],
            compiler_params=params,
            cost_estimate=cost(per - first, 1),
            name="quantize_near" if k == 0 else "quantize_far",
        )(cb_k, y0, y1, vectors, vec_far, *head)

    head = ()
    if HEAD:
        early = jax.ShapeDtypeStruct((HEAD * SUBDIM, rows), BF16)
        head = pl.pallas_call(
            functools.partial(quantize_kernel, k=0, per=per, first=0, last=HEAD),
            in_specs=[vmem] * 3,
            out_specs=[vmem] * 4,
            out_shape=[
                early,
                early,
                jax.ShapeDtypeStruct(((codes // lanes) * HEAD * SUBDIM, lanes), F32),
                jax.ShapeDtypeStruct(cnt_shape, F32),
            ],
            compiler_params=params,
            cost_estimate=cost(HEAD, 0),
            name="quantize_head",
        )(cb, y0, y1)
        cb_far, *head = lax.optimization_barrier((cb_far, *head))
    mine1, other1, keep1, send1 = quantize(1, cb_far)
    got1 = lax.ppermute(send1, "sub", swap)
    theirs1 = lax.ppermute(other1, "rep", swap)
    mine0, other0, keep0, send0 = quantize(0, cb, HEAD, head)
    got0 = lax.ppermute(send0, "sub", swap)

    def scatter(kept, got):
        size = (2, kept.shape[0] // rows_n, lanes)
        return pl.pallas_call(
            pieces_kernel,
            out_shape=[jax.ShapeDtypeStruct(size, F32), jax.ShapeDtypeStruct(size, BF16)],
            in_specs=[vmem] * 2,
            out_specs=[vmem] * 2,
            scratch_shapes=[pltpu.VMEM(kept.shape, F32)],
            compiler_params=small,
            name="pieces",
        )(kept, got)

    def pair(own, sent):
        both = own + exchange(sent, rows_n, 1).astype(F32)
        return both[0], both[1].astype(BF16)

    def finish(own, sent):
        return (own + exchange(sent, rows_n, 2).astype(F32)).astype(BF16)

    near_own, near_sent = scatter(keep0, got1)
    near_own, other0, got0, theirs1 = lax.optimization_barrier((near_own, other0, got0, theirs1))
    theirs0 = lax.ppermute(other0, "rep", swap)
    near = pair(near_own, near_sent)
    far_own, far_sent = pair(*scatter(keep1, got0))
    far_sent, theirs0 = lax.optimization_barrier((far_sent, theirs0))
    reconstruction = pl.pallas_call(
        turn_kernel,
        out_shape=jax.ShapeDtypeStruct((rows, width), BF16),
        in_specs=[vmem] * 4,
        out_specs=vmem,
        scratch_shapes=[pltpu.VMEM((width, rows), BF16)],
        compiler_params=small,
        name="turn",
    )(mine0, mine1, theirs0, theirs1)
    summed = jnp.concatenate([finish(*near), finish(far_own, far_sent)], axis=0)
    summed, reconstruction = lax.optimization_barrier((summed, reconstruction))
    apart = range(rows_n - 1, 0, -1)
    mine = [summed] + [exchange(summed, rows_n, d) for d in apart]
    theirs = [lax.ppermute(x, "rep", swap) for x in mine]

    any_spec = pl.BlockSpec(memory_space=pl.ANY)
    cross, new = pl.pallas_call(
        functools.partial(final_kernel, n=rows_n, per=per, total=total),
        out_shape=(jax.ShapeDtypeStruct((part, width), F32), jax.ShapeDtypeStruct(cb.shape, F32)),
        in_specs=[vmem] * (2 * rows_n + 1),
        out_specs=(any_spec, any_spec),
        scratch_shapes=[
            pltpu.VMEM((2, 2 * p_rows + s_rows, lanes), F32),
            pltpu.VMEM((part, width), F32),
            pltpu.VMEM(cb.shape, F32),
            pltpu.SemaphoreType.DMA((part // lanes + 1,)),
        ],
        compiler_params=small,
        name="final",
    )(*mine, *theirs, cb)
    return reconstruction, new.transpose(0, 2, 1), cross


def solution(mesh):
    placed = (P(("dom", "row", "sub", "rep"), None), P("dom", None), P(("dom", "sub"), None, None))
    body = on_device if mesh.shape["sub"] == 2 and mesh.shape["row"] == 4 else any_mesh
    return jax.shard_map(
        body,
        mesh=mesh,
        in_specs=placed,
        out_specs=(
            P(("dom", "row", "sub", "rep"), None),
            P(("dom", "sub"), None, None),
            P(("dom", "sub"), None),
        ),
        check_vma=False,
    )
```

```python
import functools
import math

import jax
import jax.numpy as jnp
from jax import lax
from jax.experimental import pallas as pl
from jax.experimental.pallas import tpu as pltpu
from jax.sharding import PartitionSpec as P

SUBDIM = 16
SOFTNESS = 4.0
LOG2E = math.log2(math.e)
F32, BF16 = jnp.float32, jnp.bfloat16
VMEM_BYTES = 24 * 2**20
HEAD = 3
SCATTER = (3, 2, 1)
GATHER = (1, 3, 2)


def quantize_rows(block, codebook):
    block = block.astype(F32)
    cross_product = jnp.dot(codebook, block, precision=lax.Precision.HIGHEST)
    squared_norms = jnp.sum(codebook * codebook, axis=1)
    affinity_scores = (2.0 * cross_product - squared_norms[:, None]) / SOFTNESS
    weights = jax.nn.softmax(affinity_scores, axis=0)
    recon = jnp.dot(codebook.T, weights, precision=lax.Precision.HIGHEST)
    sums = lax.dot_general(weights, block, (((1,), (1,)), ((), ())), precision=lax.Precision.HIGHEST)
    return recon, sums, jnp.sum(weights, axis=1)


def any_mesh(vectors, rotation, codebooks):
    rows, width = vectors.shape
    groups = lax.axis_size("sub")
    part = width // groups
    rotated_t = lax.dot_general(
        rotation, vectors, (((0,), (1,)), ((), ())), preferred_element_type=F32
    ).astype(BF16)
    received = lax.all_to_all(rotated_t.reshape(groups, part, rows), "sub", split_axis=0, concat_axis=2, tiled=True)
    columns = received.shape[2]
    blocks = received.reshape(part // SUBDIM, SUBDIM, columns)
    recon, sums, counts = lax.map(lambda pair: quantize_rows(pair[0], pair[1]), (blocks, codebooks))
    sent = recon.astype(BF16).reshape(1, part, columns)
    recon_t = lax.all_to_all(sent, "sub", split_axis=2, concat_axis=0, tiled=True).reshape(width, rows)
    total = rows * lax.axis_size("row") * groups * lax.axis_size("rep")
    sums, counts = lax.psum((sums, counts), ("row", "rep"))
    term = lax.dot_general(vectors, recon_t, (((0,), (1,)), ((), ())), preferred_element_type=F32)
    whole = lax.psum(term, ("row", "sub", "rep"))
    mine = lax.dynamic_slice_in_dim(whole, lax.axis_index("sub") * part, part, 0)
    return recon_t.T, (sums + codebooks) / (counts[:, :, None] + 1.0), mine / total


def rotate_kernel(vec_ref, rot_ref, y_ref, rott_ref):
    s, r = lax.axis_index("sub"), lax.axis_index("rep")
    n, w = y_ref.shape[0], y_ref.shape[1]
    turned = rot_ref[...].T
    for h in range(n):
        for q in range(2):
            @pl.when(r == q)
            def _():
                rott_ref[(h + n - s) % n] = turned[(2 * h + q) * w : (2 * h + q + 1) * w]
    for k in range(n):
        y_ref[k] = lax.dot_general(
            rott_ref[k], vec_ref[...], (((1,), (1,)), ((), ())), preferred_element_type=F32
        ).astype(BF16)


def rotate_more_kernel(vec_ref, rott_ref, y_ref):
    for k in range(y_ref.shape[0]):
        y_ref[k] = lax.dot_general(
            rott_ref[k], vec_ref[...], (((1,), (1,)), ((), ())), preferred_element_type=F32
        ).astype(BF16)


def operands(c):
    codes = c.shape[1]
    scaled = c * (2.0 / SOFTNESS * LOG2E)
    hi = scaled.astype(BF16).astype(F32)
    mid = (scaled - hi).astype(BF16).astype(F32)
    lo = (scaled - hi) - mid
    n = jnp.sum(c * c, axis=0, keepdims=True) * (-LOG2E / SOFTNESS)
    n_hi = n.astype(BF16).astype(F32)
    n_mid = (n - n_hi).astype(BF16).astype(F32)
    n_lo = (n - n_hi) - n_mid
    row = lax.broadcasted_iota(jnp.int32, (SUBDIM, codes), 0)
    norms = jnp.where(row == 0, n_hi, jnp.where(row == 1, n_mid, jnp.where(row == 2, n_lo, 0.0)))
    a = jnp.concatenate([hi, mid, lo, norms], axis=0).T.astype(BF16)
    b = jnp.concatenate([c.astype(BF16), jnp.ones((SUBDIM, codes), BF16)], axis=0)
    return a, b


def quantize_kernel(*refs, k, per, first, last):
    cb_ref, y0_ref, y1_ref = refs[:3]
    refs = refs[3:]
    s, r = lax.axis_index("sub"), lax.axis_index("rep")
    codes = cb_ref.shape[2]
    cols = y0_ref.shape[2]
    w = per * SUBDIM
    lanes = 128
    halves = codes // lanes
    whole = last == per
    base = r * per if k == 0 else 0
    if not whole:
        rec0_ref, rec1_ref, sums_ref, cnt = refs
        p_rows = 0
    else:
        v0_ref, v1_ref, *refs = refs
        part = v0_ref.shape[1] // 2
        p_rows = (part // lanes) * w
        if k == 1:
            head0_ref, head1_ref, rec0_ref, rec1_ref, keep_ref, send_ref, also_ref, cnt = refs
        else:
            *head, rec0_ref, rec1_ref, keep_ref, send_ref, cnt = refs
        sums_ref = keep_ref if k == 0 else send_ref
    stride = w if whole else last * SUBDIM
    ones = jnp.ones((SUBDIM, cols), BF16)
    ys, recs = (y0_ref, y1_ref), (rec0_ref, rec1_ref)
    if first:
        done = first * SUBDIM
        rec0_ref[:done, :] = head[0][...]
        rec1_ref[:done, :] = head[1][...]
        for half in range(halves):
            at = p_rows + half * stride
            sums_ref[at : at + done, :] = head[2][half * done : (half + 1) * done, :].astype(sums_ref.dtype)
        cnt[...] = head[3][...]
    else:
        cnt[...] = jnp.zeros_like(cnt)
    ab, acc = {}, {}

    def score(j, i):
        if j not in ab:
            ab[j] = operands(cb_ref[base + j])
        y = ys[i][k, SUBDIM * j : SUBDIM * (j + 1), :]
        return y, jnp.dot(ab[j][0], jnp.concatenate([y, y, y, ones], axis=0), preferred_element_type=F32)

    def spread(sc):
        return jnp.exp2(sc - jnp.max(sc, axis=0, keepdims=True)).astype(BF16)

    def rebuild(j, i, y, e):
        out = jnp.dot(ab[j][1], e, preferred_element_type=F32)
        inv = 1.0 / out[SUBDIM:]
        recs[i][SUBDIM * j : SUBDIM * (j + 1), :] = (out[:SUBDIM] * inv).astype(BF16)
        return jnp.concatenate([(y.astype(F32) * inv).astype(BF16), inv.astype(BF16)], axis=0)

    def gather(j, i, yz, e):
        sums = lax.dot_general(yz, e, (((1,), (1,)), ((), ())), preferred_element_type=F32)
        if i == 0:
            acc[j] = sums
            return
        sums = acc.pop(j) + sums
        for half in range(halves):
            at = p_rows + half * stride + j * SUBDIM
            sums_ref[at : at + SUBDIM, :] = sums[:SUBDIM, half * lanes : (half + 1) * lanes].astype(sums_ref.dtype)
            at = half * SUBDIM + j
            cnt[at : at + 1, :] = sums[SUBDIM : SUBDIM + 1, half * lanes : (half + 1) * lanes]

    one = two = three = None
    for item in [(j, i) for j in range(first, last) for i in range(2)] + [None] * 3:
        new_one = (item, *score(*item)) if item is not None else None
        new_two = (one[0], one[1], spread(one[2])) if one is not None else None
        new_three = (two[0], rebuild(*two[0], two[1], two[2]), two[2]) if two is not None else None
        if three is not None:
            gather(*three[0], three[1], three[2])
        one, two, three = new_one, new_two, new_three
    if not whole:
        return

    at = p_rows + halves * w
    sums_ref[at : at + cnt.shape[0], :] = cnt[...].astype(sums_ref.dtype)
    at_head = at + cnt.shape[0]
    done = first * SUBDIM
    early = HEAD * SUBDIM
    cross = jnp.dot(rec0_ref[done:, :], v0_ref[...], preferred_element_type=F32) + jnp.dot(
        rec1_ref[done:, :], v1_ref[...], preferred_element_type=F32
    )
    if k == 1:
        ahead = jnp.dot(head0_ref[...], v0_ref[...], preferred_element_type=F32) + jnp.dot(
            head1_ref[...], v1_ref[...], preferred_element_type=F32
        )
    size = w - done
    for h in range(2):
        @pl.when(s == h)
        def _():
            for g in range(part // lanes):
                near = slice(h * part + g * lanes, h * part + (g + 1) * lanes)
                away = slice((1 - h) * part + g * lanes, (1 - h) * part + (g + 1) * lanes)
                keep_ref[g * w + done : (g + 1) * w, :] = cross[:, near]
                send_ref[g * size : (g + 1) * size, :] = cross[:, away].astype(BF16)
                if k == 1:
                    at = at_head + g * early
                    also_ref[g * early : (g + 1) * early, :] = ahead[:, near]
                    send_ref[at : at + early, :] = ahead[:, away].astype(BF16)
                elif done:
                    keep_ref[g * w : g * w + done, :] = head[4][g * early : (g + 1) * early, :]


def turn_kernel(m0_ref, m1_ref, t0_ref, t1_ref, out_ref, buf):
    s, r = lax.axis_index("sub"), lax.axis_index("rep")
    w = m0_ref.shape[0]
    for k, (mine, theirs) in enumerate(((m0_ref, t0_ref), (m1_ref, t1_ref))):
        h = (s + k) % 2
        buf[pl.ds(pl.multiple_of((2 * h + r) * w, SUBDIM), w), :] = mine[...]
        buf[pl.ds(pl.multiple_of((2 * h + 1 - r) * w, SUBDIM), w), :] = theirs[...]
    out_ref[...] = buf[...].T


def final_kernel(*refs, n, per, total):
    pieces, (cb_ref, cross_hbm, new_hbm, buf, cross, new, sems) = refs[: 2 * n], refs[2 * n :]
    s, r, z = lax.axis_index("sub"), lax.axis_index("rep"), lax.axis_index("row")
    lanes = 128
    w = per * SUBDIM
    groups = cross.shape[0] // lanes
    halves = cb_ref.shape[2] // lanes
    near_rows = groups * w + halves * (w + SUBDIM)
    near, far = near_rows // n, groups * w // n
    for side in range(2):
        for i in range(n):
            ref = pieces[side * n + i]
            source = z ^ ((0,) + GATHER)[i]
            buf[side, pl.ds(pl.multiple_of(source * near, 8), near), :] = ref[:near].astype(F32)
            buf[side, pl.ds(pl.multiple_of(near_rows + source * far, 8), far), :] = ref[near:].astype(F32)

    copies = []
    for g in range(groups):
        for h in range(2):
            for q in range(2):
                @pl.when((s == h) & (r == q))
                def _():
                    parts = []
                    for col in range(2):
                        start = (col ^ h) * near_rows + g * w
                        parts += [buf[rep ^ q, start : start + w, :] for rep in range(2)]
                    cross[g * lanes : (g + 1) * lanes, :] = jnp.concatenate(parts, axis=0).T * (1.0 / total)
        block = pl.ds(g * lanes, lanes)
        copies.append(pltpu.make_async_copy(cross.at[block], cross_hbm.at[block], sems.at[g]))
        copies[-1].start()
    first = groups * w
    for side in range(2):
        part = r if side == 0 else 1 - r
        for m in range(per):
            c = cb_ref[part * per + m]
            rows = [first + hf * w + m * SUBDIM for hf in range(halves)]
            sums = jnp.concatenate([buf[side, a : a + SUBDIM, :] for a in rows], axis=1)
            rows = [first + halves * w + hf * SUBDIM + m for hf in range(halves)]
            count = jnp.concatenate([buf[side, a : a + 1, :] for a in rows], axis=1)
            new[part * per + m] = (sums + c) / (count + 1.0)
    copies.append(pltpu.make_async_copy(new, new_hbm, sems.at[groups]))
    copies[-1].start()
    for copy in copies:
        copy.wait()


def pieces_kernel(kept_ref, got_ref, *refs, n, late):
    if late:
        first_ref, *refs = refs
    outs, total = refs[:n], refs[n]
    z = lax.axis_index("row")
    rows = kept_ref.shape[0]
    if late:
        early = HEAD * SUBDIM
        groups = (first_ref.shape[0] - late) // early
        w = rows // groups
        for g in range(groups):
            a, b = g * w, g * w + early
            c = late + g * early
            total[a:b, :] = kept_ref[a:b, :] + first_ref[c : c + early, :].astype(F32)
            c = g * (w - early)
            total[b : a + w, :] = kept_ref[b : a + w, :] + got_ref[c : c + w - early, :].astype(F32)
    else:
        total[...] = kept_ref[...] + got_ref[:rows, :].astype(F32)
    size = outs[0].shape[0]
    for out, d in zip(outs, (0,) + SCATTER):
        out[...] = total[pl.ds(pl.multiple_of((z ^ d) * size, 8), size), :].astype(out.dtype)


def exchange(x, n, d):
    return lax.ppermute(x, "row", [(i, i ^ d) for i in range(n)])


def on_device(vectors, rotation, codebooks):
    rows, width = vectors.shape
    subs, rows_n = 2, lax.axis_size("row")
    part = width // subs
    per = part // SUBDIM // 2
    w = per * SUBDIM
    codes = codebooks.shape[1]
    lanes = 128
    total = rows * rows_n * subs * 2
    swap = [(0, 1), (1, 0)]
    params = pltpu.CompilerParams(vmem_limit_bytes=VMEM_BYTES)
    small = pltpu.CompilerParams(vmem_limit_bytes=VMEM_BYTES // 2)
    vmem = pl.BlockSpec(memory_space=pltpu.VMEM)

    cb = codebooks.transpose(0, 2, 1)
    cb_sent = lax.dynamic_slice_in_dim(cb, lax.axis_index("rep") * per, per, 0)
    cb_far = lax.ppermute(cb_sent, "sub", swap)
    vec_far = lax.ppermute(vectors, "rep", swap)

    y_shape = jax.ShapeDtypeStruct((subs, w, rows), BF16)
    y0, rott = pl.pallas_call(
        rotate_kernel,
        out_shape=(y_shape, jax.ShapeDtypeStruct((subs, w, width), BF16)),
        in_specs=[vmem] * 2,
        out_specs=(vmem, vmem),
        compiler_params=small,
        name="rotate",
    )(vectors, rotation)

    y1 = pl.pallas_call(
        rotate_more_kernel, out_shape=y_shape, in_specs=[vmem] * 2, out_specs=vmem, compiler_params=small, name="rotate_far"
    )(vec_far, rott)

    p_rows = (part // lanes) * w
    s_rows = (codes // lanes) * (w + SUBDIM)
    rec_shape = jax.ShapeDtypeStruct((w, rows), BF16)

    cnt_shape = ((codes // lanes) * SUBDIM, lanes)

    def cost(count, cross):
        return pl.CostEstimate(
            flops=count * codes * rows * 2 * 2 * (9 * SUBDIM) + cross * 2 * w * 2 * rows * width,
            transcendentals=count * codes * rows * 2,
            bytes_accessed=2**23,
        )

    groups = part // lanes
    early = HEAD * SUBDIM

    def quantize(k, cb_k, *head):
        n_keep, n_send = (p_rows + s_rows, p_rows - groups * early) if k == 0 else (p_rows, p_rows + s_rows + groups * early)
        out_shape = [
            rec_shape,
            rec_shape,
            jax.ShapeDtypeStruct((n_keep, lanes), F32),
            jax.ShapeDtypeStruct((n_send, lanes), BF16),
        ] + [jax.ShapeDtypeStruct((groups * early, lanes), F32)] * k
        first = 0 if k else HEAD
        return pl.pallas_call(
            functools.partial(quantize_kernel, k=k, per=per, first=first, last=per),
            in_specs=[vmem] * (5 + len(head)),
            out_specs=[vmem] * len(out_shape),
            out_shape=out_shape,
            scratch_shapes=[pltpu.VMEM(cnt_shape, F32)],
            compiler_params=params,
            cost_estimate=cost(per - first, 1),
            name="quantize_far" if k else "quantize_near",
        )(cb_k, y0, y1, vectors, vec_far, *head)

    early_shape = jax.ShapeDtypeStruct((early, rows), BF16)
    head = pl.pallas_call(
        functools.partial(quantize_kernel, k=0, per=per, first=0, last=HEAD),
        in_specs=[vmem] * 3,
        out_specs=[vmem] * 4,
        out_shape=[
            early_shape,
            early_shape,
            jax.ShapeDtypeStruct(((codes // lanes) * early, lanes), F32),
            jax.ShapeDtypeStruct(cnt_shape, F32),
        ],
        compiler_params=params,
        cost_estimate=cost(HEAD, 0),
        name="quantize_head",
    )(cb, y0, y1)

    mine1, other1, keep1, send1, ahead = quantize(1, cb_far, *head[:2])
    got1 = lax.ppermute(send1, "sub", swap)
    theirs1 = lax.ppermute(other1, "rep", swap)
    mine0, other0, keep0, send0 = quantize(0, cb, *head, ahead)
    got0 = lax.ppermute(send0, "sub", swap)
    theirs0 = lax.ppermute(other0, "rep", swap)

    reconstruction = pl.pallas_call(
        turn_kernel,
        out_shape=jax.ShapeDtypeStruct((rows, width), BF16),
        in_specs=[vmem] * 4,
        out_specs=vmem,
        scratch_shapes=[pltpu.VMEM((width, rows), BF16)],
        compiler_params=small,
        name="turn",
    )(mine0, mine1, theirs0, theirs1)

    def scatter(kept, got, *more):
        size = (kept.shape[0] // rows_n, lanes)
        own, *sent = pl.pallas_call(
            functools.partial(pieces_kernel, n=rows_n, late=p_rows + s_rows if more else 0),
            out_shape=[jax.ShapeDtypeStruct(size, F32)] + [jax.ShapeDtypeStruct(size, BF16)] * (rows_n - 1),
            in_specs=[vmem] * (2 + len(more)),
            out_specs=[vmem] * rows_n,
            scratch_shapes=[pltpu.VMEM(kept.shape, F32)],
            compiler_params=small,
            name="pieces",
        )(kept, got, *more)
        return [own] + [exchange(x, rows_n, d) for x, d in zip(sent, SCATTER)]

    def add_up(parts):
        return functools.reduce(lambda a, b: a + b.astype(F32), parts[1:], parts[0]).astype(BF16)

    near = scatter(keep0, got1)
    near[0], got0, theirs1 = lax.optimization_barrier((near[0], got0, theirs1))
    summed = jnp.concatenate([add_up(near), add_up(scatter(keep1, got0, got1))], axis=0)
    summed, reconstruction = lax.optimization_barrier((summed, reconstruction))
    mine = [summed] + [exchange(summed, rows_n, d) for d in GATHER]
    theirs = [lax.ppermute(x, "rep", swap) for x in mine]

    any_spec = pl.BlockSpec(memory_space=pl.ANY)
    cross, new = pl.pallas_call(
        functools.partial(final_kernel, n=rows_n, per=per, total=total),
        out_shape=(jax.ShapeDtypeStruct((part, width), F32), jax.ShapeDtypeStruct(cb.shape, F32)),
        in_specs=[vmem] * (2 * rows_n + 1),
        out_specs=(any_spec, any_spec),
        scratch_shapes=[
            pltpu.VMEM((2, 2 * p_rows + s_rows, lanes), F32),
            pltpu.VMEM((part, width), F32),
            pltpu.VMEM(cb.shape, F32),
            pltpu.SemaphoreType.DMA((part // lanes + 1,)),
        ],
        compiler_params=small,
        name="final",
    )(*mine, *theirs, cb)
    return reconstruction, new.transpose(0, 2, 1), cross


def solution(mesh):
    placed = (P(("dom", "row", "sub", "rep"), None), P("dom", None), P(("dom", "sub"), None, None))
    body = on_device if mesh.shape["sub"] == 2 and mesh.shape["row"] == 4 else any_mesh
    return jax.shard_map(
        body,
        mesh=mesh,
        in_specs=placed,
        out_specs=(
            P(("dom", "row", "sub", "rep"), None),
            P(("dom", "sub"), None, None),
            P(("dom", "sub"), None),
        ),
        check_vma=False,
    )
```

```python
import functools
import math

import jax
import jax.numpy as jnp
from jax import lax
from jax.experimental import pallas as pl
from jax.experimental.pallas import tpu as pltpu
from jax.sharding import PartitionSpec as P

SUBDIM = 16
SOFTNESS = 4.0
LOG2E = math.log2(math.e)
F32, BF16 = jnp.float32, jnp.bfloat16
VMEM_BYTES = 24 * 2**20
HEAD = 3
FETCHES = 4
SCATTER = (3, 2, 1)
GATHER = (1, 3, 2)


def quantize_rows(block, codebook):
    block = block.astype(F32)
    cross_product = jnp.dot(codebook, block, precision=lax.Precision.HIGHEST)
    squared_norms = jnp.sum(codebook * codebook, axis=1)
    affinity_scores = (2.0 * cross_product - squared_norms[:, None]) / SOFTNESS
    weights = jax.nn.softmax(affinity_scores, axis=0)
    recon = jnp.dot(codebook.T, weights, precision=lax.Precision.HIGHEST)
    sums = lax.dot_general(weights, block, (((1,), (1,)), ((), ())), precision=lax.Precision.HIGHEST)
    return recon, sums, jnp.sum(weights, axis=1)


def any_mesh(vectors, rotation, codebooks):
    rows, width = vectors.shape
    groups = lax.axis_size("sub")
    part = width // groups
    rotated_t = lax.dot_general(
        rotation, vectors, (((0,), (1,)), ((), ())), preferred_element_type=F32
    ).astype(BF16)
    received = lax.all_to_all(rotated_t.reshape(groups, part, rows), "sub", split_axis=0, concat_axis=2, tiled=True)
    columns = received.shape[2]
    blocks = received.reshape(part // SUBDIM, SUBDIM, columns)
    recon, sums, counts = lax.map(lambda pair: quantize_rows(pair[0], pair[1]), (blocks, codebooks))
    sent = recon.astype(BF16).reshape(1, part, columns)
    recon_t = lax.all_to_all(sent, "sub", split_axis=2, concat_axis=0, tiled=True).reshape(width, rows)
    total = rows * lax.axis_size("row") * groups * lax.axis_size("rep")
    sums, counts = lax.psum((sums, counts), ("row", "rep"))
    term = lax.dot_general(vectors, recon_t, (((0,), (1,)), ((), ())), preferred_element_type=F32)
    whole = lax.psum(term, ("row", "sub", "rep"))
    mine = lax.dynamic_slice_in_dim(whole, lax.axis_index("sub") * part, part, 0)
    return recon_t.T, (sums + codebooks) / (counts[:, :, None] + 1.0), mine / total


def rotate_kernel(vec_hbm, rot_hbm, y_ref, rott_ref, v_ref, rot, sems):
    s, r = lax.axis_index("sub"), lax.axis_index("rep")
    n, w = y_ref.shape[0], y_ref.shape[1]
    copies = []
    for source, target in ((rot_hbm, rot), (vec_hbm, v_ref)):
        size = source.shape[0] // FETCHES
        for q in range(FETCHES):
            block = pl.ds(q * size, size)
            copies.append(pltpu.make_async_copy(source.at[block], target.at[block], sems.at[len(copies)]))
            copies[-1].start()
    for copy in copies[:FETCHES]:
        copy.wait()
    turned = rot[...].T
    for h in range(n):
        for q in range(2):
            @pl.when(r == q)
            def _():
                rott_ref[(h + n - s) % n] = turned[(2 * h + q) * w : (2 * h + q + 1) * w]
    for copy in copies[FETCHES:]:
        copy.wait()
    for k in range(n):
        y_ref[k] = lax.dot_general(
            rott_ref[k], v_ref[...], (((1,), (1,)), ((), ())), preferred_element_type=F32
        ).astype(BF16)


def rotate_more_kernel(vec_ref, rott_ref, y_ref):
    for k in range(y_ref.shape[0]):
        y_ref[k] = lax.dot_general(
            rott_ref[k], vec_ref[...], (((1,), (1,)), ((), ())), preferred_element_type=F32
        ).astype(BF16)


def operands(c):
    codes = c.shape[1]
    scaled = c * (2.0 / SOFTNESS * LOG2E)
    hi = scaled.astype(BF16).astype(F32)
    mid = (scaled - hi).astype(BF16).astype(F32)
    lo = (scaled - hi) - mid
    n = jnp.sum(c * c, axis=0, keepdims=True) * (-LOG2E / SOFTNESS)
    n_hi = n.astype(BF16).astype(F32)
    n_mid = (n - n_hi).astype(BF16).astype(F32)
    n_lo = (n - n_hi) - n_mid
    row = lax.broadcasted_iota(jnp.int32, (SUBDIM, codes), 0)
    norms = jnp.where(row == 0, n_hi, jnp.where(row == 1, n_mid, jnp.where(row == 2, n_lo, 0.0)))
    a = jnp.concatenate([hi, mid, lo, norms], axis=0).T.astype(BF16)
    b = jnp.concatenate([c.astype(BF16), jnp.ones((SUBDIM, codes), BF16)], axis=0)
    return a, b


def quantize_kernel(*refs, k, per, first, last):
    cb_ref, y0_ref, y1_ref = refs[:3]
    refs = refs[3:]
    s, r = lax.axis_index("sub"), lax.axis_index("rep")
    codes = cb_ref.shape[2]
    cols = y0_ref.shape[2]
    w = per * SUBDIM
    lanes = 128
    halves = codes // lanes
    whole = last == per
    base = r * per if k == 0 else 0
    if not whole:
        rec0_ref, rec1_ref, sums_ref, cnt = refs
        p_rows = 0
    else:
        v0_ref, v1_ref, *refs = refs
        part = v0_ref.shape[1] // 2
        p_rows = (part // lanes) * w
        if k == 1:
            head0_ref, head1_ref, rec0_ref, rec1_ref, keep_ref, send_ref, also_ref, cnt = refs
        else:
            *head, rec0_ref, rec1_ref, keep_ref, send_ref, cnt = refs
        sums_ref = keep_ref if k == 0 else send_ref
    stride = w if whole else last * SUBDIM
    ones = jnp.ones((SUBDIM, cols), BF16)
    ys, recs = (y0_ref, y1_ref), (rec0_ref, rec1_ref)
    if first:
        done = first * SUBDIM
        rec0_ref[:done, :] = head[0][...]
        rec1_ref[:done, :] = head[1][...]
        for half in range(halves):
            at = p_rows + half * stride
            sums_ref[at : at + done, :] = head[2][half * done : (half + 1) * done, :].astype(sums_ref.dtype)
        cnt[...] = head[3][...]
    else:
        cnt[...] = jnp.zeros_like(cnt)
    ab, acc = {}, {}

    def score(j, i):
        if j not in ab:
            ab[j] = operands(cb_ref[base + j])
        y = ys[i][k, SUBDIM * j : SUBDIM * (j + 1), :]
        return y, jnp.dot(ab[j][0], jnp.concatenate([y, y, y, ones], axis=0), preferred_element_type=F32)

    def spread(sc):
        return jnp.exp2(sc - jnp.max(sc, axis=0, keepdims=True)).astype(BF16)

    def rebuild(j, i, y, e):
        out = jnp.dot(ab[j][1], e, preferred_element_type=F32)
        inv = 1.0 / out[SUBDIM:]
        recs[i][SUBDIM * j : SUBDIM * (j + 1), :] = (out[:SUBDIM] * inv).astype(BF16)
        return jnp.concatenate([(y.astype(F32) * inv).astype(BF16), inv.astype(BF16)], axis=0)

    def gather(j, i, yz, e):
        sums = lax.dot_general(yz, e, (((1,), (1,)), ((), ())), preferred_element_type=F32)
        if i == 0:
            acc[j] = sums
            return
        sums = acc.pop(j) + sums
        for half in range(halves):
            at = p_rows + half * stride + j * SUBDIM
            sums_ref[at : at + SUBDIM, :] = sums[:SUBDIM, half * lanes : (half + 1) * lanes].astype(sums_ref.dtype)
            at = half * SUBDIM + j
            cnt[at : at + 1, :] = sums[SUBDIM : SUBDIM + 1, half * lanes : (half + 1) * lanes]

    one = two = three = None
    for item in [(j, i) for j in range(first, last) for i in range(2)] + [None] * 3:
        new_one = (item, *score(*item)) if item is not None else None
        new_two = (one[0], one[1], spread(one[2])) if one is not None else None
        new_three = (two[0], rebuild(*two[0], two[1], two[2]), two[2]) if two is not None else None
        if three is not None:
            gather(*three[0], three[1], three[2])
        one, two, three = new_one, new_two, new_three
    if not whole:
        return

    at = p_rows + halves * w
    sums_ref[at : at + cnt.shape[0], :] = cnt[...].astype(sums_ref.dtype)
    at_head = at + cnt.shape[0]
    done = first * SUBDIM
    early = HEAD * SUBDIM
    cross = jnp.dot(rec0_ref[done:, :], v0_ref[...], preferred_element_type=F32) + jnp.dot(
        rec1_ref[done:, :], v1_ref[...], preferred_element_type=F32
    )
    if k == 1:
        ahead = jnp.dot(head0_ref[...], v0_ref[...], preferred_element_type=F32) + jnp.dot(
            head1_ref[...], v1_ref[...], preferred_element_type=F32
        )
    size = w - done
    for h in range(2):
        @pl.when(s == h)
        def _():
            for g in range(part // lanes):
                near = slice(h * part + g * lanes, h * part + (g + 1) * lanes)
                away = slice((1 - h) * part + g * lanes, (1 - h) * part + (g + 1) * lanes)
                keep_ref[g * w + done : (g + 1) * w, :] = cross[:, near]
                send_ref[g * size : (g + 1) * size, :] = cross[:, away].astype(BF16)
                if k == 1:
                    at = at_head + g * early
                    also_ref[g * early : (g + 1) * early, :] = ahead[:, near]
                    send_ref[at : at + early, :] = ahead[:, away].astype(BF16)
                elif done:
                    keep_ref[g * w : g * w + done, :] = head[4][g * early : (g + 1) * early, :]


def slice_kernel(cb_hbm, out_ref, sems, *, per):
    size = per // FETCHES
    copies = []
    for q in range(FETCHES):
        at = lax.axis_index("rep") * per + q * size
        copies.append(pltpu.make_async_copy(cb_hbm.at[pl.ds(at, size)], out_ref.at[pl.ds(q * size, size)], sems.at[q]))
        copies[-1].start()
    for copy in copies:
        copy.wait()


def turn_kernel(m0_ref, m1_ref, t0_ref, t1_ref, out_ref, buf):
    s, r = lax.axis_index("sub"), lax.axis_index("rep")
    w = m0_ref.shape[0]
    for k, (mine, theirs) in enumerate(((m0_ref, t0_ref), (m1_ref, t1_ref))):
        h = (s + k) % 2
        buf[pl.ds(pl.multiple_of((2 * h + r) * w, SUBDIM), w), :] = mine[...]
        buf[pl.ds(pl.multiple_of((2 * h + 1 - r) * w, SUBDIM), w), :] = theirs[...]
    out_ref[...] = buf[...].T


def final_kernel(*refs, n, per, total):
    pieces, (cb_ref, cross_hbm, new_hbm, buf, cross, new, sems) = refs[: 2 * n], refs[2 * n :]
    s, r, z = lax.axis_index("sub"), lax.axis_index("rep"), lax.axis_index("row")
    lanes = 128
    w = per * SUBDIM
    groups = cross.shape[0] // lanes
    halves = cb_ref.shape[2] // lanes
    near_rows = groups * w + halves * (w + SUBDIM)
    near, far = near_rows // n, groups * w // n
    for side in range(2):
        for i in range(n):
            ref = pieces[side * n + i]
            source = z ^ ((0,) + GATHER)[i]
            buf[side, pl.ds(pl.multiple_of(source * near, 8), near), :] = ref[:near].astype(F32)
            buf[side, pl.ds(pl.multiple_of(near_rows + source * far, 8), far), :] = ref[near:].astype(F32)

    copies = []
    for g in range(groups):
        for h in range(2):
            for q in range(2):
                @pl.when((s == h) & (r == q))
                def _():
                    parts = []
                    for col in range(2):
                        start = (col ^ h) * near_rows + g * w
                        parts += [buf[rep ^ q, start : start + w, :] for rep in range(2)]
                    cross[g * lanes : (g + 1) * lanes, :] = jnp.concatenate(parts, axis=0).T * (1.0 / total)
        block = pl.ds(g * lanes, lanes)
        copies.append(pltpu.make_async_copy(cross.at[block], cross_hbm.at[block], sems.at[g]))
        copies[-1].start()
    first = groups * w
    for side in range(2):
        part = r if side == 0 else 1 - r
        for m in range(per):
            c = cb_ref[part * per + m]
            rows = [first + hf * w + m * SUBDIM for hf in range(halves)]
            sums = jnp.concatenate([buf[side, a : a + SUBDIM, :] for a in rows], axis=1)
            rows = [first + halves * w + hf * SUBDIM + m for hf in range(halves)]
            count = jnp.concatenate([buf[side, a : a + 1, :] for a in rows], axis=1)
            new[part * per + m] = (sums + c) / (count + 1.0)
    copies.append(pltpu.make_async_copy(new, new_hbm, sems.at[groups]))
    copies[-1].start()
    for copy in copies:
        copy.wait()


def pieces_kernel(kept_ref, got_ref, *refs, n, late):
    if late:
        first_ref, *refs = refs
    outs, total = refs[:n], refs[n]
    z = lax.axis_index("row")
    rows = kept_ref.shape[0]
    if late:
        early = HEAD * SUBDIM
        groups = (first_ref.shape[0] - late) // early
        w = rows // groups
        for g in range(groups):
            a, b = g * w, g * w + early
            c = late + g * early
            total[a:b, :] = kept_ref[a:b, :] + first_ref[c : c + early, :].astype(F32)
            c = g * (w - early)
            total[b : a + w, :] = kept_ref[b : a + w, :] + got_ref[c : c + w - early, :].astype(F32)
    else:
        total[...] = kept_ref[...] + got_ref[:rows, :].astype(F32)
    size = outs[0].shape[0]
    for out, d in zip(outs, (0,) + SCATTER):
        out[...] = total[pl.ds(pl.multiple_of((z ^ d) * size, 8), size), :].astype(out.dtype)


def exchange(x, n, d):
    return lax.ppermute(x, "row", [(i, i ^ d) for i in range(n)])


def on_device(vectors, rotation, codebooks):
    rows, width = vectors.shape
    subs, rows_n = 2, lax.axis_size("row")
    part = width // subs
    per = part // SUBDIM // 2
    w = per * SUBDIM
    codes = codebooks.shape[1]
    lanes = 128
    total = rows * rows_n * subs * 2
    swap = [(0, 1), (1, 0)]
    params = pltpu.CompilerParams(vmem_limit_bytes=VMEM_BYTES)
    small = pltpu.CompilerParams(vmem_limit_bytes=VMEM_BYTES // 2)
    vmem = pl.BlockSpec(memory_space=pltpu.VMEM)

    cb = codebooks.transpose(0, 2, 1)
    hbm = pl.BlockSpec(memory_space=pltpu.HBM)
    cb_sent = pl.pallas_call(
        functools.partial(slice_kernel, per=per),
        out_shape=jax.ShapeDtypeStruct((per,) + cb.shape[1:], F32),
        in_specs=[hbm],
        out_specs=vmem,
        scratch_shapes=[pltpu.SemaphoreType.DMA((FETCHES,))],
        compiler_params=small,
        name="slice",
    )(pltpu.with_memory_space_constraint(cb, pltpu.HBM))
    cb_far = lax.ppermute(cb_sent, "sub", swap)
    vec_far = lax.ppermute(vectors, "rep", swap)

    y_shape = jax.ShapeDtypeStruct((subs, w, rows), BF16)
    y0, rott, v0 = pl.pallas_call(
        rotate_kernel,
        out_shape=(
            y_shape,
            jax.ShapeDtypeStruct((subs, w, width), BF16),
            jax.ShapeDtypeStruct(vectors.shape, BF16),
        ),
        in_specs=[hbm] * 2,
        out_specs=(vmem,) * 3,
        scratch_shapes=[pltpu.VMEM(rotation.shape, BF16), pltpu.SemaphoreType.DMA((2 * FETCHES,))],
        compiler_params=small,
        name="rotate",
    )(*(pltpu.with_memory_space_constraint(x, pltpu.HBM) for x in (vectors, rotation)))
    y1 = pl.pallas_call(
        rotate_more_kernel, out_shape=y_shape, in_specs=[vmem] * 2, out_specs=vmem, compiler_params=small, name="rotate_far"
    )(vec_far, rott)

    p_rows = (part // lanes) * w
    s_rows = (codes // lanes) * (w + SUBDIM)
    rec_shape = jax.ShapeDtypeStruct((w, rows), BF16)

    cnt_shape = ((codes // lanes) * SUBDIM, lanes)

    def cost(count, cross):
        return pl.CostEstimate(
            flops=count * codes * rows * 2 * 2 * (9 * SUBDIM) + cross * 2 * w * 2 * rows * width,
            transcendentals=count * codes * rows * 2,
            bytes_accessed=2**23,
        )

    groups = part // lanes
    early = HEAD * SUBDIM

    def quantize(k, cb_k, *head):
        n_keep, n_send = (p_rows + s_rows, p_rows - groups * early) if k == 0 else (p_rows, p_rows + s_rows + groups * early)
        out_shape = [
            rec_shape,
            rec_shape,
            jax.ShapeDtypeStruct((n_keep, lanes), F32),
            jax.ShapeDtypeStruct((n_send, lanes), BF16),
        ] + [jax.ShapeDtypeStruct((groups * early, lanes), F32)] * k
        first = 0 if k else HEAD
        return pl.pallas_call(
            functools.partial(quantize_kernel, k=k, per=per, first=first, last=per),
            in_specs=[vmem] * (5 + len(head)),
            out_specs=[vmem] * len(out_shape),
            out_shape=out_shape,
            scratch_shapes=[pltpu.VMEM(cnt_shape, F32)],
            compiler_params=params,
            cost_estimate=cost(per - first, 1),
            name="quantize_far" if k else "quantize_near",
        )(cb_k, y0, y1, v0, vec_far, *head)

    early_shape = jax.ShapeDtypeStruct((early, rows), BF16)
    head = pl.pallas_call(
        functools.partial(quantize_kernel, k=0, per=per, first=0, last=HEAD),
        in_specs=[vmem] * 3,
        out_specs=[vmem] * 4,
        out_shape=[
            early_shape,
            early_shape,
            jax.ShapeDtypeStruct(((codes // lanes) * early, lanes), F32),
            jax.ShapeDtypeStruct(cnt_shape, F32),
        ],
        compiler_params=params,
        cost_estimate=cost(HEAD, 0),
        name="quantize_head",
    )(cb, y0, y1)

    mine1, other1, keep1, send1, ahead = quantize(1, cb_far, *head[:2])
    got1 = lax.ppermute(send1, "sub", swap)
    theirs1 = lax.ppermute(other1, "rep", swap)
    mine0, other0, keep0, send0 = quantize(0, cb, *head, ahead)
    got0 = lax.ppermute(send0, "sub", swap)
    other0, got1 = lax.optimization_barrier((other0, got1))
    theirs0 = lax.ppermute(other0, "rep", swap)

    reconstruction = pl.pallas_call(
        turn_kernel,
        out_shape=jax.ShapeDtypeStruct((rows, width), BF16),
        in_specs=[vmem] * 4,
        out_specs=vmem,
        scratch_shapes=[pltpu.VMEM((width, rows), BF16)],
        compiler_params=small,
        name="turn",
    )(mine0, mine1, theirs0, theirs1)

    def scatter(kept, got, *more):
        size = (kept.shape[0] // rows_n, lanes)
        own, *sent = pl.pallas_call(
            functools.partial(pieces_kernel, n=rows_n, late=p_rows + s_rows if more else 0),
            out_shape=[jax.ShapeDtypeStruct(size, F32)] + [jax.ShapeDtypeStruct(size, BF16)] * (rows_n - 1),
            in_specs=[vmem] * (2 + len(more)),
            out_specs=[vmem] * rows_n,
            scratch_shapes=[pltpu.VMEM(kept.shape, F32)],
            compiler_params=small,
            name="pieces",
        )(kept, got, *more)
        return [own] + [exchange(x, rows_n, d) for x, d in zip(sent, SCATTER)]

    def add_up(parts):
        return functools.reduce(lambda a, b: a + b.astype(F32), parts[1:], parts[0]).astype(BF16)

    near = scatter(keep0, got1)
    near[0], got0, theirs1 = lax.optimization_barrier((near[0], got0, theirs1))
    summed = jnp.concatenate([add_up(near), add_up(scatter(keep1, got0, got1))], axis=0)
    mine = [summed] + [exchange(summed, rows_n, d) for d in GATHER]
    mine[2], mine[3], reconstruction = lax.optimization_barrier((mine[2], mine[3], reconstruction))
    theirs = [lax.ppermute(x, "rep", swap) for x in mine]

    any_spec = pl.BlockSpec(memory_space=pl.ANY)
    cross, new = pl.pallas_call(
        functools.partial(final_kernel, n=rows_n, per=per, total=total),
        out_shape=(jax.ShapeDtypeStruct((part, width), F32), jax.ShapeDtypeStruct(cb.shape, F32)),
        in_specs=[vmem] * (2 * rows_n + 1),
        out_specs=(any_spec, any_spec),
        scratch_shapes=[
            pltpu.VMEM((2, 2 * p_rows + s_rows, lanes), F32),
            pltpu.VMEM((part, width), F32),
            pltpu.VMEM(cb.shape, F32),
            pltpu.SemaphoreType.DMA((part // lanes + 1,)),
        ],
        compiler_params=small,
        name="final",
    )(*mine, *theirs, cb)
    return reconstruction, new.transpose(0, 2, 1), cross


def solution(mesh):
    placed = (P(("dom", "row", "sub", "rep"), None), P("dom", None), P(("dom", "sub"), None, None))
    body = on_device if mesh.shape["sub"] == 2 and mesh.shape["row"] == 4 else any_mesh
    return jax.shard_map(
        body,
        mesh=mesh,
        in_specs=placed,
        out_specs=(
            P(("dom", "row", "sub", "rep"), None),
            P(("dom", "sub"), None, None),
            P(("dom", "sub"), None),
        ),
        check_vma=False,
    )
```

```python
import functools
import math

import jax
import jax.numpy as jnp
from jax import lax
from jax.experimental import pallas as pl
from jax.experimental.pallas import tpu as pltpu
from jax.sharding import PartitionSpec as P

SUBDIM = 16
SOFTNESS = 4.0
LOG2E = math.log2(math.e)
F32, BF16 = jnp.float32, jnp.bfloat16
VMEM_BYTES = 24 * 2**20
HEAD = 4
FETCHES = 4
SCATTER = (3, 2, 1)
GATHER = (1, 3, 2)


def quantize_rows(block, codebook):
    block = block.astype(F32)
    cross_product = jnp.dot(codebook, block, precision=lax.Precision.HIGHEST)
    squared_norms = jnp.sum(codebook * codebook, axis=1)
    affinity_scores = (2.0 * cross_product - squared_norms[:, None]) / SOFTNESS
    weights = jax.nn.softmax(affinity_scores, axis=0)
    recon = jnp.dot(codebook.T, weights, precision=lax.Precision.HIGHEST)
    sums = lax.dot_general(weights, block, (((1,), (1,)), ((), ())), precision=lax.Precision.HIGHEST)
    return recon, sums, jnp.sum(weights, axis=1)


def any_mesh(vectors, rotation, codebooks):
    rows, width = vectors.shape
    groups = lax.axis_size("sub")
    part = width // groups
    rotated_t = lax.dot_general(
        rotation, vectors, (((0,), (1,)), ((), ())), preferred_element_type=F32
    ).astype(BF16)
    received = lax.all_to_all(rotated_t.reshape(groups, part, rows), "sub", split_axis=0, concat_axis=2, tiled=True)
    columns = received.shape[2]
    blocks = received.reshape(part // SUBDIM, SUBDIM, columns)
    recon, sums, counts = lax.map(lambda pair: quantize_rows(pair[0], pair[1]), (blocks, codebooks))
    sent = recon.astype(BF16).reshape(1, part, columns)
    recon_t = lax.all_to_all(sent, "sub", split_axis=2, concat_axis=0, tiled=True).reshape(width, rows)
    total = rows * lax.axis_size("row") * groups * lax.axis_size("rep")
    sums, counts = lax.psum((sums, counts), ("row", "rep"))
    term = lax.dot_general(vectors, recon_t, (((0,), (1,)), ((), ())), preferred_element_type=F32)
    whole = lax.psum(term, ("row", "sub", "rep"))
    mine = lax.dynamic_slice_in_dim(whole, lax.axis_index("sub") * part, part, 0)
    return recon_t.T, (sums + codebooks) / (counts[:, :, None] + 1.0), mine / total


def rotate_kernel(vec_hbm, rot_hbm, y_ref, rott_ref, v_ref, rot, sems):
    s, r = lax.axis_index("sub"), lax.axis_index("rep")
    n, w = y_ref.shape[0], y_ref.shape[1]
    copies = []
    for source, target in ((rot_hbm, rot), (vec_hbm, v_ref)):
        size = source.shape[0] // FETCHES
        for q in range(FETCHES):
            block = pl.ds(q * size, size)
            copies.append(pltpu.make_async_copy(source.at[block], target.at[block], sems.at[len(copies)]))
            copies[-1].start()
    for copy in copies[:FETCHES]:
        copy.wait()
    for h in range(n):
        for q in range(2):
            @pl.when(r == q)
            def _():
                at = (2 * h + q) * w
                start = at // 128 * 128
                turned = rot[:, start : start + 256].T
                rott_ref[(h + n - s) % n] = turned[at - start : at - start + w]
    for copy in copies[FETCHES:]:
        copy.wait()
    for k in range(n):
        y_ref[k] = lax.dot_general(
            rott_ref[k], v_ref[...], (((1,), (1,)), ((), ())), preferred_element_type=F32
        ).astype(BF16)


def rotate_more_kernel(vec_ref, rott_ref, y_ref):
    for k in range(y_ref.shape[0]):
        y_ref[k] = lax.dot_general(
            rott_ref[k], vec_ref[...], (((1,), (1,)), ((), ())), preferred_element_type=F32
        ).astype(BF16)


def operands(c):
    codes = c.shape[1]
    scaled = c * (2.0 / SOFTNESS * LOG2E)
    hi = scaled.astype(BF16).astype(F32)
    mid = (scaled - hi).astype(BF16).astype(F32)
    lo = (scaled - hi) - mid
    n = jnp.sum(c * c, axis=0, keepdims=True) * (-LOG2E / SOFTNESS)
    n_hi = n.astype(BF16).astype(F32)
    n_mid = (n - n_hi).astype(BF16).astype(F32)
    n_lo = (n - n_hi) - n_mid
    row = lax.broadcasted_iota(jnp.int32, (SUBDIM, codes), 0)
    norms = jnp.where(row == 0, n_hi, jnp.where(row == 1, n_mid, jnp.where(row == 2, n_lo, 0.0)))
    a = jnp.concatenate([hi, mid, lo, norms], axis=0).T.astype(BF16)
    b = jnp.concatenate([c.astype(BF16), jnp.ones((SUBDIM, codes), BF16)], axis=0)
    return a, b


def quantize_kernel(*refs, k, per, first, last):
    cb_ref, y0_ref, y1_ref = refs[:3]
    refs = refs[3:]
    s, r = lax.axis_index("sub"), lax.axis_index("rep")
    codes = cb_ref.shape[2]
    cols = y0_ref.shape[2]
    w = per * SUBDIM
    lanes = 128
    halves = codes // lanes
    whole = last == per
    base = r * per if k == 0 else 0
    if not whole:
        rec0_ref, rec1_ref, sums_ref, cnt = refs
        p_rows = 0
    else:
        v0_ref, v1_ref, *refs = refs
        part = v0_ref.shape[1] // 2
        p_rows = (part // lanes) * w
        *head, rec0_ref, rec1_ref, keep_ref, send_ref, cnt = refs
        sums_ref = keep_ref if k == 0 else send_ref
    stride = w if whole else last * SUBDIM
    ones = jnp.ones((SUBDIM, cols), BF16)
    ys, recs = (y0_ref, y1_ref), (rec0_ref, rec1_ref)
    if first:
        done = first * SUBDIM
        rec0_ref[:done, :] = head[0][...]
        rec1_ref[:done, :] = head[1][...]
        for half in range(halves):
            at = p_rows + half * stride
            sums_ref[at : at + done, :] = head[2][half * done : (half + 1) * done, :].astype(sums_ref.dtype)
        cnt[...] = head[3][...]
    else:
        cnt[...] = jnp.zeros_like(cnt)
    ab, acc = {}, {}

    def score(j, i):
        if j not in ab:
            ab[j] = operands(cb_ref[base + j])
        y = ys[i][k, SUBDIM * j : SUBDIM * (j + 1), :]
        return y, jnp.dot(ab[j][0], jnp.concatenate([y, y, y, ones], axis=0), preferred_element_type=F32)

    def spread(sc):
        return jnp.exp2(sc - jnp.max(sc, axis=0, keepdims=True)).astype(BF16)

    def rebuild(j, i, y, e):
        out = jnp.dot(ab[j][1], e, preferred_element_type=F32)
        inv = 1.0 / out[SUBDIM:]
        recs[i][SUBDIM * j : SUBDIM * (j + 1), :] = (out[:SUBDIM] * inv).astype(BF16)
        return jnp.concatenate([(y.astype(F32) * inv).astype(BF16), inv.astype(BF16)], axis=0)

    def gather(j, i, yz, e):
        sums = lax.dot_general(yz, e, (((1,), (1,)), ((), ())), preferred_element_type=F32)
        if i == 0:
            acc[j] = sums
            return
        sums = acc.pop(j) + sums
        for half in range(halves):
            at = p_rows + half * stride + j * SUBDIM
            sums_ref[at : at + SUBDIM, :] = sums[:SUBDIM, half * lanes : (half + 1) * lanes].astype(sums_ref.dtype)
            at = half * SUBDIM + j
            cnt[at : at + 1, :] = sums[SUBDIM : SUBDIM + 1, half * lanes : (half + 1) * lanes]

    one = two = three = None
    for item in [(j, i) for j in range(first, last) for i in range(2)] + [None] * 3:
        new_one = (item, *score(*item)) if item is not None else None
        new_two = (one[0], one[1], spread(one[2])) if one is not None else None
        new_three = (two[0], rebuild(*two[0], two[1], two[2]), two[2]) if two is not None else None
        if three is not None:
            gather(*three[0], three[1], three[2])
        one, two, three = new_one, new_two, new_three
    if not whole:
        return

    at = p_rows + halves * w
    sums_ref[at : at + cnt.shape[0], :] = cnt[...].astype(sums_ref.dtype)
    cross = jnp.dot(rec0_ref[...], v0_ref[...], preferred_element_type=F32) + jnp.dot(
        rec1_ref[...], v1_ref[...], preferred_element_type=F32
    )
    for h in range(2):
        @pl.when(s == h)
        def _():
            for g in range(part // lanes):
                near = h * part + g * lanes
                far = (1 - h) * part + g * lanes
                keep_ref[g * w : (g + 1) * w, :] = cross[:, near : near + lanes]
                send_ref[g * w : (g + 1) * w, :] = cross[:, far : far + lanes].astype(BF16)


def slice_kernel(cb_hbm, out_ref, sems, *, per):
    size = per // FETCHES
    copies = []
    for q in range(FETCHES):
        at = lax.axis_index("rep") * per + q * size
        copies.append(pltpu.make_async_copy(cb_hbm.at[pl.ds(at, size)], out_ref.at[pl.ds(q * size, size)], sems.at[q]))
        copies[-1].start()
    for copy in copies:
        copy.wait()


def turn_kernel(m0_ref, m1_ref, t0_ref, t1_ref, out_ref, buf):
    s, r = lax.axis_index("sub"), lax.axis_index("rep")
    w = m0_ref.shape[0]
    for k, (mine, theirs) in enumerate(((m0_ref, t0_ref), (m1_ref, t1_ref))):
        h = (s + k) % 2
        buf[pl.ds(pl.multiple_of((2 * h + r) * w, SUBDIM), w), :] = mine[...]
        buf[pl.ds(pl.multiple_of((2 * h + 1 - r) * w, SUBDIM), w), :] = theirs[...]
    out_ref[...] = buf[...].T


def final_kernel(*refs, n, per, total):
    pieces, (cb_ref, cross_hbm, new_hbm, buf, cross, new, sems) = refs[: 2 * n], refs[2 * n :]
    s, r, z = lax.axis_index("sub"), lax.axis_index("rep"), lax.axis_index("row")
    lanes = 128
    w = per * SUBDIM
    groups = cross.shape[0] // lanes
    halves = cb_ref.shape[2] // lanes
    near_rows = groups * w + halves * (w + SUBDIM)
    near, far = near_rows // n, groups * w // n
    for side in range(2):
        for i in range(n):
            ref = pieces[side * n + i]
            source = z ^ ((0,) + GATHER)[i]
            buf[side, pl.ds(pl.multiple_of(source * near, 8), near), :] = ref[:near].astype(F32)
            buf[side, pl.ds(pl.multiple_of(near_rows + source * far, 8), far), :] = ref[near:].astype(F32)

    copies = []
    for g in range(groups):
        for h in range(2):
            for q in range(2):
                @pl.when((s == h) & (r == q))
                def _():
                    parts = []
                    for col in range(2):
                        start = (col ^ h) * near_rows + g * w
                        parts += [buf[rep ^ q, start : start + w, :] for rep in range(2)]
                    cross[g * lanes : (g + 1) * lanes, :] = jnp.concatenate(parts, axis=0).T * (1.0 / total)
        block = pl.ds(g * lanes, lanes)
        copies.append(pltpu.make_async_copy(cross.at[block], cross_hbm.at[block], sems.at[g]))
        copies[-1].start()
    first = groups * w
    for side in range(2):
        part = r if side == 0 else 1 - r
        for m in range(per):
            c = cb_ref[part * per + m]
            rows = [first + hf * w + m * SUBDIM for hf in range(halves)]
            sums = jnp.concatenate([buf[side, a : a + SUBDIM, :] for a in rows], axis=1)
            rows = [first + halves * w + hf * SUBDIM + m for hf in range(halves)]
            count = jnp.concatenate([buf[side, a : a + 1, :] for a in rows], axis=1)
            new[part * per + m] = (sums + c) / (count + 1.0)
    copies.append(pltpu.make_async_copy(new, new_hbm, sems.at[groups]))
    copies[-1].start()
    for copy in copies:
        copy.wait()


def pieces_kernel(kept_ref, got_ref, *refs, n):
    outs, total = refs[:n], refs[n]
    z = lax.axis_index("row")
    total[...] = kept_ref[...] + got_ref[...].astype(F32)
    size = outs[0].shape[0]
    for out, d in zip(outs, (0,) + SCATTER):
        out[...] = total[pl.ds(pl.multiple_of((z ^ d) * size, 8), size), :].astype(out.dtype)


def exchange(x, n, d):
    return lax.ppermute(x, "row", [(i, i ^ d) for i in range(n)])


def on_device(vectors, rotation, codebooks):
    rows, width = vectors.shape
    subs, rows_n = 2, lax.axis_size("row")
    part = width // subs
    per = part // SUBDIM // 2
    w = per * SUBDIM
    codes = codebooks.shape[1]
    lanes = 128
    total = rows * rows_n * subs * 2
    swap = [(0, 1), (1, 0)]
    params = pltpu.CompilerParams(vmem_limit_bytes=VMEM_BYTES)
    small = pltpu.CompilerParams(vmem_limit_bytes=VMEM_BYTES // 2)
    vmem = pl.BlockSpec(memory_space=pltpu.VMEM)

    cb = codebooks.transpose(0, 2, 1)
    hbm = pl.BlockSpec(memory_space=pltpu.HBM)
    cb_sent = pl.pallas_call(
        functools.partial(slice_kernel, per=per),
        out_shape=jax.ShapeDtypeStruct((per,) + cb.shape[1:], F32),
        in_specs=[hbm],
        out_specs=vmem,
        scratch_shapes=[pltpu.SemaphoreType.DMA((FETCHES,))],
        compiler_params=small,
        name="slice",
    )(pltpu.with_memory_space_constraint(cb, pltpu.HBM))
    cb_far = lax.ppermute(cb_sent, "sub", swap)
    vec_far = lax.ppermute(vectors, "rep", swap)

    y_shape = jax.ShapeDtypeStruct((subs, w, rows), BF16)
    y0, rott, v0 = pl.pallas_call(
        rotate_kernel,
        out_shape=(
            y_shape,
            jax.ShapeDtypeStruct((subs, w, width), BF16),
            jax.ShapeDtypeStruct(vectors.shape, BF16),
        ),
        in_specs=[hbm] * 2,
        out_specs=(vmem,) * 3,
        scratch_shapes=[pltpu.VMEM(rotation.shape, BF16), pltpu.SemaphoreType.DMA((2 * FETCHES,))],
        compiler_params=small,
        name="rotate",
    )(*(pltpu.with_memory_space_constraint(x, pltpu.HBM) for x in (vectors, rotation)))
    y1 = pl.pallas_call(
        rotate_more_kernel, out_shape=y_shape, in_specs=[vmem] * 2, out_specs=vmem, compiler_params=small, name="rotate_far"
    )(vec_far, rott)

    p_rows = (part // lanes) * w
    s_rows = (codes // lanes) * (w + SUBDIM)
    rec_shape = jax.ShapeDtypeStruct((w, rows), BF16)

    cnt_shape = ((codes // lanes) * SUBDIM, lanes)

    def cost(count, cross):
        return pl.CostEstimate(
            flops=count * codes * rows * 2 * 2 * (9 * SUBDIM) + cross * 2 * w * 2 * rows * width,
            transcendentals=count * codes * rows * 2,
            bytes_accessed=2**23,
        )

    early = HEAD * SUBDIM

    def quantize(k, cb_k, *head):
        n_keep, n_send = (p_rows + s_rows, p_rows) if k == 0 else (p_rows, p_rows + s_rows)
        out_shape = [
            rec_shape,
            rec_shape,
            jax.ShapeDtypeStruct((n_keep, lanes), F32),
            jax.ShapeDtypeStruct((n_send, lanes), BF16),
        ]
        first = 0 if k else HEAD
        return pl.pallas_call(
            functools.partial(quantize_kernel, k=k, per=per, first=first, last=per),
            in_specs=[vmem] * (5 + len(head)),
            out_specs=[vmem] * len(out_shape),
            out_shape=out_shape,
            scratch_shapes=[pltpu.VMEM(cnt_shape, F32)],
            compiler_params=params,
            cost_estimate=cost(per - first, 1),
            name="quantize_far" if k else "quantize_near",
        )(cb_k, y0, y1, v0, vec_far, *head)

    early_shape = jax.ShapeDtypeStruct((early, rows), BF16)
    head = pl.pallas_call(
        functools.partial(quantize_kernel, k=0, per=per, first=0, last=HEAD),
        in_specs=[vmem] * 3,
        out_specs=[vmem] * 4,
        out_shape=[
            early_shape,
            early_shape,
            jax.ShapeDtypeStruct(((codes // lanes) * early, lanes), F32),
            jax.ShapeDtypeStruct(cnt_shape, F32),
        ],
        compiler_params=params,
        cost_estimate=cost(HEAD, 0),
        name="quantize_head",
    )(cb, y0, y1)

    cb_far, *head = lax.optimization_barrier((cb_far, *head))

    mine1, other1, keep1, send1 = quantize(1, cb_far)
    got1 = lax.ppermute(send1, "sub", swap)
    theirs1 = lax.ppermute(other1, "rep", swap)
    mine0, other0, keep0, send0 = quantize(0, cb, *head)
    got0 = lax.ppermute(send0, "sub", swap)
    other0, got1 = lax.optimization_barrier((other0, got1))
    theirs0 = lax.ppermute(other0, "rep", swap)

    reconstruction = pl.pallas_call(
        turn_kernel,
        out_shape=jax.ShapeDtypeStruct((rows, width), BF16),
        in_specs=[vmem] * 4,
        out_specs=vmem,
        scratch_shapes=[pltpu.VMEM((width, rows), BF16)],
        compiler_params=small,
        name="turn",
    )(mine0, mine1, theirs0, theirs1)

    def scatter(kept, got):
        size = (kept.shape[0] // rows_n, lanes)
        own, *sent = pl.pallas_call(
            functools.partial(pieces_kernel, n=rows_n),
            out_shape=[jax.ShapeDtypeStruct(size, F32)] + [jax.ShapeDtypeStruct(size, BF16)] * (rows_n - 1),
            in_specs=[vmem] * 2,
            out_specs=[vmem] * rows_n,
            scratch_shapes=[pltpu.VMEM(kept.shape, F32)],
            compiler_params=small,
            name="pieces",
        )(kept, got)
        return [own] + [exchange(x, rows_n, d) for x, d in zip(sent, SCATTER)]

    def add_up(parts):
        return functools.reduce(lambda a, b: a + b.astype(F32), parts[1:], parts[0]).astype(BF16)

    near = scatter(keep0, got1)
    near[0], got0, theirs1 = lax.optimization_barrier((near[0], got0, theirs1))
    summed = jnp.concatenate([add_up(near), add_up(scatter(keep1, got0))], axis=0)
    mine = [summed] + [exchange(summed, rows_n, d) for d in GATHER]
    mine[2], mine[3], reconstruction = lax.optimization_barrier((mine[2], mine[3], reconstruction))
    theirs = [lax.ppermute(x, "rep", swap) for x in mine]

    any_spec = pl.BlockSpec(memory_space=pl.ANY)
    cross, new = pl.pallas_call(
        functools.partial(final_kernel, n=rows_n, per=per, total=total),
        out_shape=(jax.ShapeDtypeStruct((part, width), F32), jax.ShapeDtypeStruct(cb.shape, F32)),
        in_specs=[vmem] * (2 * rows_n + 1),
        out_specs=(any_spec, any_spec),
        scratch_shapes=[
            pltpu.VMEM((2, 2 * p_rows + s_rows, lanes), F32),
            pltpu.VMEM((part, width), F32),
            pltpu.VMEM(cb.shape, F32),
            pltpu.SemaphoreType.DMA((part // lanes + 1,)),
        ],
        compiler_params=small,
        name="final",
    )(*mine, *theirs, cb)
    return reconstruction, new.transpose(0, 2, 1), cross


def solution(mesh):
    placed = (P(("dom", "row", "sub", "rep"), None), P("dom", None), P(("dom", "sub"), None, None))
    body = on_device if mesh.shape["sub"] == 2 and mesh.shape["row"] == 4 else any_mesh
    return jax.shard_map(
        body,
        mesh=mesh,
        in_specs=placed,
        out_specs=(
            P(("dom", "row", "sub", "rep"), None),
            P(("dom", "sub"), None, None),
            P(("dom", "sub"), None),
        ),
        check_vma=False,
    )
```

```python
import functools
import math

import jax
import jax.numpy as jnp
from jax import lax
from jax.experimental import pallas as pl
from jax.experimental.pallas import tpu as pltpu
from jax.sharding import PartitionSpec as P

SUBDIM = 16
SOFTNESS = 4.0
LOG2E = math.log2(math.e)
F32, BF16 = jnp.float32, jnp.bfloat16
VMEM_BYTES = 24 * 2**20
HEAD = 4
FETCHES = 4
SCATTER = (3, 2, 1)
GATHER = (1, 3, 2)


def quantize_rows(block, codebook):
    block = block.astype(F32)
    cross_product = jnp.dot(codebook, block, precision=lax.Precision.HIGHEST)
    squared_norms = jnp.sum(codebook * codebook, axis=1)
    affinity_scores = (2.0 * cross_product - squared_norms[:, None]) / SOFTNESS
    weights = jax.nn.softmax(affinity_scores, axis=0)
    recon = jnp.dot(codebook.T, weights, precision=lax.Precision.HIGHEST)
    sums = lax.dot_general(weights, block, (((1,), (1,)), ((), ())), precision=lax.Precision.HIGHEST)
    return recon, sums, jnp.sum(weights, axis=1)


def any_mesh(vectors, rotation, codebooks):
    rows, width = vectors.shape
    groups = lax.axis_size("sub")
    part = width // groups
    rotated_t = lax.dot_general(
        rotation, vectors, (((0,), (1,)), ((), ())), preferred_element_type=F32
    ).astype(BF16)
    received = lax.all_to_all(rotated_t.reshape(groups, part, rows), "sub", split_axis=0, concat_axis=2, tiled=True)
    columns = received.shape[2]
    blocks = received.reshape(part // SUBDIM, SUBDIM, columns)
    recon, sums, counts = lax.map(lambda pair: quantize_rows(pair[0], pair[1]), (blocks, codebooks))
    sent = recon.astype(BF16).reshape(1, part, columns)
    recon_t = lax.all_to_all(sent, "sub", split_axis=2, concat_axis=0, tiled=True).reshape(width, rows)
    total = rows * lax.axis_size("row") * groups * lax.axis_size("rep")
    sums, counts = lax.psum((sums, counts), ("row", "rep"))
    term = lax.dot_general(vectors, recon_t, (((0,), (1,)), ((), ())), preferred_element_type=F32)
    whole = lax.psum(term, ("row", "sub", "rep"))
    mine = lax.dynamic_slice_in_dim(whole, lax.axis_index("sub") * part, part, 0)
    return recon_t.T, (sums + codebooks) / (counts[:, :, None] + 1.0), mine / total


def rotate_kernel(vec_hbm, rot_hbm, y_ref, rott_ref, v_ref, rot, sems):
    s, r = lax.axis_index("sub"), lax.axis_index("rep")
    n, w = y_ref.shape[0], y_ref.shape[1]
    copies = []
    for source, target in ((rot_hbm, rot), (vec_hbm, v_ref)):
        size = source.shape[0] // FETCHES
        for q in range(FETCHES):
            block = pl.ds(q * size, size)
            copies.append(pltpu.make_async_copy(source.at[block], target.at[block], sems.at[len(copies)]))
            copies[-1].start()
    for copy in copies[:FETCHES]:
        copy.wait()
    for h in range(n):
        for q in range(2):
            @pl.when(r == q)
            def _():
                at = (2 * h + q) * w
                start = at // 128 * 128
                turned = rot[:, start : start + 256].T
                rott_ref[(h + n - s) % n] = turned[at - start : at - start + w]
    for copy in copies[FETCHES:]:
        copy.wait()
    for k in range(n):
        y_ref[k] = lax.dot_general(
            rott_ref[k], v_ref[...], (((1,), (1,)), ((), ())), preferred_element_type=F32
        ).astype(BF16)


def rotate_more_kernel(vec_ref, rott_ref, y_ref):
    for k in range(y_ref.shape[0]):
        y_ref[k] = lax.dot_general(
            rott_ref[k], vec_ref[...], (((1,), (1,)), ((), ())), preferred_element_type=F32
        ).astype(BF16)


def operands(c):
    codes = c.shape[1]
    scaled = c * (2.0 / SOFTNESS * LOG2E)
    hi = scaled.astype(BF16).astype(F32)
    mid = (scaled - hi).astype(BF16).astype(F32)
    lo = (scaled - hi) - mid
    n = jnp.sum(c * c, axis=0, keepdims=True) * (-LOG2E / SOFTNESS)
    n_hi = n.astype(BF16).astype(F32)
    n_mid = (n - n_hi).astype(BF16).astype(F32)
    n_lo = (n - n_hi) - n_mid
    row = lax.broadcasted_iota(jnp.int32, (SUBDIM, codes), 0)
    norms = jnp.where(row == 0, n_hi, jnp.where(row == 1, n_mid, jnp.where(row == 2, n_lo, 0.0)))
    a = jnp.concatenate([hi, mid, lo, norms], axis=0).T.astype(BF16)
    b = jnp.concatenate([c.astype(BF16), jnp.ones((SUBDIM, codes), BF16)], axis=0)
    return a, b


def quantize_kernel(*refs, k, per, first, last):
    cb_ref, y0_ref, y1_ref = refs[:3]
    refs = refs[3:]
    s, r = lax.axis_index("sub"), lax.axis_index("rep")
    codes = cb_ref.shape[2]
    cols = y0_ref.shape[2]
    w = per * SUBDIM
    lanes = 128
    halves = codes // lanes
    whole = last == per
    base = r * per if k == 0 else 0
    if not whole:
        rec0_ref, rec1_ref, sums_ref, cnt = refs
        p_rows = 0
    else:
        v0_ref, v1_ref, *refs = refs
        part = v0_ref.shape[1] // 2
        p_rows = (part // lanes) * w
        *head, rec0_ref, rec1_ref, keep_ref, send_ref, cnt = refs
        sums_ref = keep_ref if k == 0 else send_ref
    stride = w if whole else last * SUBDIM
    ones = jnp.ones((SUBDIM, cols), BF16)
    ys, recs = (y0_ref, y1_ref), (rec0_ref, rec1_ref)
    if first:
        done = first * SUBDIM
        rec0_ref[:done, :] = head[0][...]
        rec1_ref[:done, :] = head[1][...]
        for half in range(halves):
            at = p_rows + half * stride
            sums_ref[at : at + done, :] = head[2][half * done : (half + 1) * done, :].astype(sums_ref.dtype)
        cnt[...] = head[3][...]
    else:
        cnt[...] = jnp.zeros_like(cnt)
    ab, acc = {}, {}

    def score(j, i):
        if j not in ab:
            ab[j] = operands(cb_ref[base + j])
        y = ys[i][k, SUBDIM * j : SUBDIM * (j + 1), :]
        return y, jnp.dot(ab[j][0], jnp.concatenate([y, y, y, ones], axis=0), preferred_element_type=F32)

    def spread(sc):
        return jnp.exp2(sc - jnp.max(sc, axis=0, keepdims=True)).astype(BF16)

    def rebuild(j, i, y, e):
        out = jnp.dot(ab[j][1], e, preferred_element_type=F32)
        inv = 1.0 / out[SUBDIM:]
        recs[i][SUBDIM * j : SUBDIM * (j + 1), :] = (out[:SUBDIM] * inv).astype(BF16)
        return jnp.concatenate([(y.astype(F32) * inv).astype(BF16), inv.astype(BF16)], axis=0)

    def gather(j, i, yz, e):
        sums = lax.dot_general(yz, e, (((1,), (1,)), ((), ())), preferred_element_type=F32)
        if i == 0:
            acc[j] = sums
            return
        sums = acc.pop(j) + sums
        for half in range(halves):
            at = p_rows + half * stride + j * SUBDIM
            sums_ref[at : at + SUBDIM, :] = sums[:SUBDIM, half * lanes : (half + 1) * lanes].astype(sums_ref.dtype)
            at = half * SUBDIM + j
            cnt[at : at + 1, :] = sums[SUBDIM : SUBDIM + 1, half * lanes : (half + 1) * lanes]

    one = two = three = None
    for item in [(j, i) for j in range(first, last) for i in range(2)] + [None] * 3:
        new_one = (item, *score(*item)) if item is not None else None
        new_two = (one[0], one[1], spread(one[2])) if one is not None else None
        new_three = (two[0], rebuild(*two[0], two[1], two[2]), two[2]) if two is not None else None
        if three is not None:
            gather(*three[0], three[1], three[2])
        one, two, three = new_one, new_two, new_three
    if not whole:
        return

    at = p_rows + halves * w
    sums_ref[at : at + cnt.shape[0], :] = cnt[...].astype(sums_ref.dtype)
    cross = jnp.dot(rec0_ref[...], v0_ref[...], preferred_element_type=F32) + jnp.dot(
        rec1_ref[...], v1_ref[...], preferred_element_type=F32
    )
    for h in range(2):
        @pl.when(s == h)
        def _():
            for g in range(part // lanes):
                near = h * part + g * lanes
                far = (1 - h) * part + g * lanes
                keep_ref[g * w : (g + 1) * w, :] = cross[:, near : near + lanes]
                send_ref[g * w : (g + 1) * w, :] = cross[:, far : far + lanes].astype(BF16)


def slice_kernel(cb_hbm, out_ref, sems, *, per):
    size = per // FETCHES
    copies = []
    for q in range(FETCHES):
        at = lax.axis_index("rep") * per + q * size
        copies.append(pltpu.make_async_copy(cb_hbm.at[pl.ds(at, size)], out_ref.at[pl.ds(q * size, size)], sems.at[q]))
        copies[-1].start()
    for copy in copies:
        copy.wait()


def turn_kernel(m0_ref, m1_ref, t0_ref, t1_ref, out_ref, buf):
    s, r = lax.axis_index("sub"), lax.axis_index("rep")
    w = m0_ref.shape[0]
    for k, (mine, theirs) in enumerate(((m0_ref, t0_ref), (m1_ref, t1_ref))):
        h = (s + k) % 2
        buf[pl.ds(pl.multiple_of((2 * h + r) * w, SUBDIM), w), :] = mine[...]
        buf[pl.ds(pl.multiple_of((2 * h + 1 - r) * w, SUBDIM), w), :] = theirs[...]
    out_ref[...] = buf[...].T


def final_kernel(*refs, n, per, total):
    pieces, (cb_ref, cross_hbm, new_hbm, buf, cross, new, sems) = refs[: 2 * n], refs[2 * n :]
    s, r, z = lax.axis_index("sub"), lax.axis_index("rep"), lax.axis_index("row")
    lanes = 128
    w = per * SUBDIM
    groups = cross.shape[0] // lanes
    halves = cb_ref.shape[2] // lanes
    near_rows = groups * w + halves * (w + SUBDIM)
    near, far = near_rows // n, groups * w // n
    for side in range(2):
        for i in range(n):
            ref = pieces[side * n + i]
            source = z ^ ((0,) + GATHER)[i]
            buf[side, pl.ds(pl.multiple_of(source * near, 8), near), :] = ref[:near].astype(F32)
            buf[side, pl.ds(pl.multiple_of(near_rows + source * far, 8), far), :] = ref[near:].astype(F32)

    copies = []
    first = groups * w
    for side in range(2):
        part = r if side == 0 else 1 - r
        for m in range(per):
            c = cb_ref[part * per + m]
            rows = [first + hf * w + m * SUBDIM for hf in range(halves)]
            sums = jnp.concatenate([buf[side, a : a + SUBDIM, :] for a in rows], axis=1)
            rows = [first + halves * w + hf * SUBDIM + m for hf in range(halves)]
            count = jnp.concatenate([buf[side, a : a + 1, :] for a in rows], axis=1)
            new[part * per + m] = (sums + c) / (count + 1.0)
    copies.append(pltpu.make_async_copy(new, new_hbm, sems.at[groups]))
    copies[-1].start()
    for g in range(groups):
        for h in range(2):
            for q in range(2):
                @pl.when((s == h) & (r == q))
                def _():
                    parts = []
                    for col in range(2):
                        start = (col ^ h) * near_rows + g * w
                        parts += [buf[rep ^ q, start : start + w, :] for rep in range(2)]
                    cross[g * lanes : (g + 1) * lanes, :] = jnp.concatenate(parts, axis=0).T * (1.0 / total)
        block = pl.ds(g * lanes, lanes)
        copies.append(pltpu.make_async_copy(cross.at[block], cross_hbm.at[block], sems.at[g]))
        copies[-1].start()
    for copy in copies:
        copy.wait()


def pieces_kernel(kept_ref, got_ref, *refs, n):
    outs, total = refs[:n], refs[n]
    z = lax.axis_index("row")
    total[...] = kept_ref[...] + got_ref[...].astype(F32)
    size = outs[0].shape[0]
    for out, d in zip(outs, (0,) + SCATTER):
        out[...] = total[pl.ds(pl.multiple_of((z ^ d) * size, 8), size), :].astype(out.dtype)


def exchange(x, n, d):
    return lax.ppermute(x, "row", [(i, i ^ d) for i in range(n)])


def on_device(vectors, rotation, codebooks):
    rows, width = vectors.shape
    subs, rows_n = 2, lax.axis_size("row")
    part = width // subs
    per = part // SUBDIM // 2
    w = per * SUBDIM
    codes = codebooks.shape[1]
    lanes = 128
    total = rows * rows_n * subs * 2
    swap = [(0, 1), (1, 0)]
    params = pltpu.CompilerParams(vmem_limit_bytes=VMEM_BYTES)
    small = pltpu.CompilerParams(vmem_limit_bytes=VMEM_BYTES // 2)
    vmem = pl.BlockSpec(memory_space=pltpu.VMEM)

    cb = codebooks.transpose(0, 2, 1)
    hbm = pl.BlockSpec(memory_space=pltpu.HBM)
    cb_sent = pl.pallas_call(
        functools.partial(slice_kernel, per=per),
        out_shape=jax.ShapeDtypeStruct((per,) + cb.shape[1:], F32),
        in_specs=[hbm],
        out_specs=vmem,
        scratch_shapes=[pltpu.SemaphoreType.DMA((FETCHES,))],
        compiler_params=small,
        name="slice",
    )(pltpu.with_memory_space_constraint(cb, pltpu.HBM))
    cb_far = lax.ppermute(cb_sent, "sub", swap)
    vec_far = lax.ppermute(vectors, "rep", swap)

    y_shape = jax.ShapeDtypeStruct((subs, w, rows), BF16)
    y0, rott, v0 = pl.pallas_call(
        rotate_kernel,
        out_shape=(
            y_shape,
            jax.ShapeDtypeStruct((subs, w, width), BF16),
            jax.ShapeDtypeStruct(vectors.shape, BF16),
        ),
        in_specs=[hbm] * 2,
        out_specs=(vmem,) * 3,
        scratch_shapes=[pltpu.VMEM(rotation.shape, BF16), pltpu.SemaphoreType.DMA((2 * FETCHES,))],
        compiler_params=small,
        name="rotate",
    )(*(pltpu.with_memory_space_constraint(x, pltpu.HBM) for x in (vectors, rotation)))
    y1 = pl.pallas_call(
        rotate_more_kernel, out_shape=y_shape, in_specs=[vmem] * 2, out_specs=vmem, compiler_params=small, name="rotate_far"
    )(vec_far, rott)

    p_rows = (part // lanes) * w
    s_rows = (codes // lanes) * (w + SUBDIM)
    rec_shape = jax.ShapeDtypeStruct((w, rows), BF16)

    cnt_shape = ((codes // lanes) * SUBDIM, lanes)

    def cost(count, cross):
        return pl.CostEstimate(
            flops=count * codes * rows * 2 * 2 * (9 * SUBDIM) + cross * 2 * w * 2 * rows * width,
            transcendentals=count * codes * rows * 2,
            bytes_accessed=2**23,
        )

    early = HEAD * SUBDIM

    def quantize(k, cb_k, *head):
        n_keep, n_send = (p_rows + s_rows, p_rows) if k == 0 else (p_rows, p_rows + s_rows)
        out_shape = [
            rec_shape,
            rec_shape,
            jax.ShapeDtypeStruct((n_keep, lanes), F32),
            jax.ShapeDtypeStruct((n_send, lanes), BF16),
        ]
        first = 0 if k else HEAD
        return pl.pallas_call(
            functools.partial(quantize_kernel, k=k, per=per, first=first, last=per),
            in_specs=[vmem] * (5 + len(head)),
            out_specs=[vmem] * len(out_shape),
            out_shape=out_shape,
            scratch_shapes=[pltpu.VMEM(cnt_shape, F32)],
            compiler_params=params,
            cost_estimate=cost(per - first, 1),
            name="quantize_far" if k else "quantize_near",
        )(cb_k, y0, y1, v0, vec_far, *head)

    early_shape = jax.ShapeDtypeStruct((early, rows), BF16)
    head = pl.pallas_call(
        functools.partial(quantize_kernel, k=0, per=per, first=0, last=HEAD),
        in_specs=[vmem] * 3,
        out_specs=[vmem] * 4,
        out_shape=[
            early_shape,
            early_shape,
            jax.ShapeDtypeStruct(((codes // lanes) * early, lanes), F32),
            jax.ShapeDtypeStruct(cnt_shape, F32),
        ],
        compiler_params=params,
        cost_estimate=cost(HEAD, 0),
        name="quantize_head",
    )(cb, y0, y1)

    cb_far, *head = lax.optimization_barrier((cb_far, *head))

    mine1, other1, keep1, send1 = quantize(1, cb_far)
    got1 = lax.ppermute(send1, "sub", swap)
    theirs1 = lax.ppermute(other1, "rep", swap)
    mine0, other0, keep0, send0 = quantize(0, cb, *head)
    got0 = lax.ppermute(send0, "sub", swap)
    other0, got1 = lax.optimization_barrier((other0, got1))
    theirs0 = lax.ppermute(other0, "rep", swap)

    reconstruction = pl.pallas_call(
        turn_kernel,
        out_shape=jax.ShapeDtypeStruct((rows, width), BF16),
        in_specs=[vmem] * 4,
        out_specs=vmem,
        scratch_shapes=[pltpu.VMEM((width, rows), BF16)],
        compiler_params=small,
        name="turn",
    )(mine0, mine1, theirs0, theirs1)

    def scatter(kept, got):
        size = (kept.shape[0] // rows_n, lanes)
        own, *sent = pl.pallas_call(
            functools.partial(pieces_kernel, n=rows_n),
            out_shape=[jax.ShapeDtypeStruct(size, F32)] + [jax.ShapeDtypeStruct(size, BF16)] * (rows_n - 1),
            in_specs=[vmem] * 2,
            out_specs=[vmem] * rows_n,
            scratch_shapes=[pltpu.VMEM(kept.shape, F32)],
            compiler_params=small,
            name="pieces",
        )(kept, got)
        return [own] + [exchange(x, rows_n, d) for x, d in zip(sent, SCATTER)]

    def add_up(parts):
        return functools.reduce(lambda a, b: a + b.astype(F32), parts[1:], parts[0]).astype(BF16)

    near = scatter(keep0, got1)
    near[0], got0, theirs1 = lax.optimization_barrier((near[0], got0, theirs1))
    summed = jnp.concatenate([add_up(near), add_up(scatter(keep1, got0))], axis=0)
    mine = [summed] + [exchange(summed, rows_n, d) for d in GATHER]
    mine[2], mine[3], reconstruction = lax.optimization_barrier((mine[2], mine[3], reconstruction))
    theirs = [lax.ppermute(x, "rep", swap) for x in mine]

    any_spec = pl.BlockSpec(memory_space=pl.ANY)
    cross, new = pl.pallas_call(
        functools.partial(final_kernel, n=rows_n, per=per, total=total),
        out_shape=(jax.ShapeDtypeStruct((part, width), F32), jax.ShapeDtypeStruct(cb.shape, F32)),
        in_specs=[vmem] * (2 * rows_n + 1),
        out_specs=(any_spec, any_spec),
        scratch_shapes=[
            pltpu.VMEM((2, 2 * p_rows + s_rows, lanes), F32),
            pltpu.VMEM((part, width), F32),
            pltpu.VMEM(cb.shape, F32),
            pltpu.SemaphoreType.DMA((part // lanes + 1,)),
        ],
        compiler_params=small,
        name="final",
    )(*mine, *theirs, cb)
    return reconstruction, new.transpose(0, 2, 1), cross


def solution(mesh):
    placed = (P(("dom", "row", "sub", "rep"), None), P("dom", None), P(("dom", "sub"), None, None))
    body = on_device if mesh.shape["sub"] == 2 and mesh.shape["row"] == 4 else any_mesh
    return jax.shard_map(
        body,
        mesh=mesh,
        in_specs=placed,
        out_specs=(
            P(("dom", "row", "sub", "rep"), None),
            P(("dom", "sub"), None, None),
            P(("dom", "sub"), None),
        ),
        check_vma=False,
    )
```

```python
import functools
import math

import jax
import jax.numpy as jnp
from jax import lax
from jax.experimental import pallas as pl
from jax.experimental.pallas import tpu as pltpu
from jax.sharding import PartitionSpec as P

SUBDIM = 16
SOFTNESS = 4.0
LOG2E = math.log2(math.e)
F32, BF16 = jnp.float32, jnp.bfloat16
VMEM_BYTES = 24 * 2**20
HEAD = 4
FETCHES = 4
SCATTER = (2, 3, 1)
GATHER = (1, 3, 2)


def quantize_rows(block, codebook):
    block = block.astype(F32)
    cross_product = jnp.dot(codebook, block, precision=lax.Precision.HIGHEST)
    squared_norms = jnp.sum(codebook * codebook, axis=1)
    affinity_scores = (2.0 * cross_product - squared_norms[:, None]) / SOFTNESS
    weights = jax.nn.softmax(affinity_scores, axis=0)
    recon = jnp.dot(codebook.T, weights, precision=lax.Precision.HIGHEST)
    sums = lax.dot_general(weights, block, (((1,), (1,)), ((), ())), precision=lax.Precision.HIGHEST)
    return recon, sums, jnp.sum(weights, axis=1)


def any_mesh(vectors, rotation, codebooks):
    rows, width = vectors.shape
    groups = lax.axis_size("sub")
    part = width // groups
    rotated_t = lax.dot_general(
        rotation, vectors, (((0,), (1,)), ((), ())), preferred_element_type=F32
    ).astype(BF16)
    received = lax.all_to_all(rotated_t.reshape(groups, part, rows), "sub", split_axis=0, concat_axis=2, tiled=True)
    columns = received.shape[2]
    blocks = received.reshape(part // SUBDIM, SUBDIM, columns)
    recon, sums, counts = lax.map(lambda pair: quantize_rows(pair[0], pair[1]), (blocks, codebooks))
    sent = recon.astype(BF16).reshape(1, part, columns)
    recon_t = lax.all_to_all(sent, "sub", split_axis=2, concat_axis=0, tiled=True).reshape(width, rows)
    total = rows * lax.axis_size("row") * groups * lax.axis_size("rep")
    sums, counts = lax.psum((sums, counts), ("row", "rep"))
    term = lax.dot_general(vectors, recon_t, (((0,), (1,)), ((), ())), preferred_element_type=F32)
    whole = lax.psum(term, ("row", "sub", "rep"))
    mine = lax.dynamic_slice_in_dim(whole, lax.axis_index("sub") * part, part, 0)
    return recon_t.T, (sums + codebooks) / (counts[:, :, None] + 1.0), mine / total


def rotate_kernel(vec_hbm, rot_hbm, y_ref, rott_ref, v_ref, rot, sems):
    s, r = lax.axis_index("sub"), lax.axis_index("rep")
    n, w = y_ref.shape[0], y_ref.shape[1]
    copies = []
    for source, target in ((rot_hbm, rot), (vec_hbm, v_ref)):
        size = source.shape[0] // FETCHES
        for q in range(FETCHES):
            block = pl.ds(q * size, size)
            copies.append(pltpu.make_async_copy(source.at[block], target.at[block], sems.at[len(copies)]))
            copies[-1].start()
    for copy in copies[:FETCHES]:
        copy.wait()
    for h in range(n):
        for q in range(2):
            @pl.when(r == q)
            def _():
                at = (2 * h + q) * w
                start = at // 128 * 128
                turned = rot[:, start : start + 256].T
                rott_ref[(h + n - s) % n] = turned[at - start : at - start + w]
    for copy in copies[FETCHES:]:
        copy.wait()
    for k in range(n):
        y_ref[k] = lax.dot_general(
            rott_ref[k], v_ref[...], (((1,), (1,)), ((), ())), preferred_element_type=F32
        ).astype(BF16)


def operands(c):
    codes = c.shape[1]
    scaled = c * (2.0 / SOFTNESS * LOG2E)
    hi = scaled.astype(BF16).astype(F32)
    mid = (scaled - hi).astype(BF16).astype(F32)
    lo = (scaled - hi) - mid
    n = jnp.sum(c * c, axis=0, keepdims=True) * (-LOG2E / SOFTNESS)
    n_hi = n.astype(BF16).astype(F32)
    n_mid = (n - n_hi).astype(BF16).astype(F32)
    n_lo = (n - n_hi) - n_mid
    row = lax.broadcasted_iota(jnp.int32, (SUBDIM, codes), 0)
    norms = jnp.where(row == 0, n_hi, jnp.where(row == 1, n_mid, jnp.where(row == 2, n_lo, 0.0)))
    a = jnp.concatenate([hi, mid, lo, norms], axis=0).T.astype(BF16)
    b = jnp.concatenate([c.astype(BF16), jnp.ones((SUBDIM, codes), BF16)], axis=0)
    return a, b


def quantize_kernel(*refs, k, per, first, last):
    cb_ref, y0_ref, y1_ref, *refs = refs
    s, r = lax.axis_index("sub"), lax.axis_index("rep")
    codes = cb_ref.shape[2]
    cols = y0_ref.shape[2]
    w = per * SUBDIM
    lanes = 128
    halves = codes // lanes
    whole = last == per
    base = r * per if k == 0 else 0
    if not whole:
        vec_ref = y1_ref
        rott_ref, rec0_ref, rec1_ref, sums_ref, cnt, y1_ref = refs
        for half in range(y1_ref.shape[0]):
            y1_ref[half] = lax.dot_general(
                rott_ref[half], vec_ref[...], (((1,), (1,)), ((), ())), preferred_element_type=F32
            ).astype(BF16)
        p_rows = 0
    else:
        v0_ref, v1_ref, *refs = refs
        part = v0_ref.shape[1] // 2
        p_rows = (part // lanes) * w
        *head, rec0_ref, rec1_ref, keep_ref, send_ref, cnt = refs
        sums_ref = keep_ref if k == 0 else send_ref
    stride = w if whole else last * SUBDIM
    ones = jnp.ones((SUBDIM, cols), BF16)
    ys, recs = (y0_ref, y1_ref), (rec0_ref, rec1_ref)
    if first:
        done = first * SUBDIM
        rec0_ref[:done, :] = head[0][...]
        rec1_ref[:done, :] = head[1][...]
        for half in range(halves):
            at = p_rows + half * stride
            sums_ref[at : at + done, :] = head[2][half * done : (half + 1) * done, :].astype(sums_ref.dtype)
        cnt[...] = head[3][...]
    else:
        cnt[...] = jnp.zeros_like(cnt)
    ab, acc = {}, {}

    def score(j, i):
        if j not in ab:
            ab[j] = operands(cb_ref[base + j])
        y = ys[i][k, SUBDIM * j : SUBDIM * (j + 1), :]
        return y, jnp.dot(ab[j][0], jnp.concatenate([y, y, y, ones], axis=0), preferred_element_type=F32)

    def spread(sc):
        return jnp.exp2(sc - jnp.max(sc, axis=0, keepdims=True)).astype(BF16)

    def rebuild(j, i, y, e):
        out = jnp.dot(ab[j][1], e, preferred_element_type=F32)
        inv = 1.0 / out[SUBDIM:]
        recs[i][SUBDIM * j : SUBDIM * (j + 1), :] = (out[:SUBDIM] * inv).astype(BF16)
        return jnp.concatenate([(y.astype(F32) * inv).astype(BF16), inv.astype(BF16)], axis=0)

    def gather(j, i, yz, e):
        sums = lax.dot_general(yz, e, (((1,), (1,)), ((), ())), preferred_element_type=F32)
        if i == 0:
            acc[j] = sums
            return
        sums = acc.pop(j) + sums
        for half in range(halves):
            at = p_rows + half * stride + j * SUBDIM
            sums_ref[at : at + SUBDIM, :] = sums[:SUBDIM, half * lanes : (half + 1) * lanes].astype(sums_ref.dtype)
            at = half * SUBDIM + j
            cnt[at : at + 1, :] = sums[SUBDIM : SUBDIM + 1, half * lanes : (half + 1) * lanes]

    one = two = three = None
    for item in [(j, i) for j in range(first, last) for i in range(2)] + [None] * 3:
        new_one = (item, *score(*item)) if item is not None else None
        new_two = (one[0], one[1], spread(one[2])) if one is not None else None
        new_three = (two[0], rebuild(*two[0], two[1], two[2]), two[2]) if two is not None else None
        if three is not None:
            gather(*three[0], three[1], three[2])
        one, two, three = new_one, new_two, new_three
    if not whole:
        return

    at = p_rows + halves * w
    sums_ref[at : at + cnt.shape[0], :] = cnt[...].astype(sums_ref.dtype)
    cross = jnp.dot(rec0_ref[...], v0_ref[...], preferred_element_type=F32) + jnp.dot(
        rec1_ref[...], v1_ref[...], preferred_element_type=F32
    )
    for h in range(2):
        @pl.when(s == h)
        def _():
            for g in range(part // lanes):
                near = h * part + g * lanes
                far = (1 - h) * part + g * lanes
                keep_ref[g * w : (g + 1) * w, :] = cross[:, near : near + lanes]
                send_ref[g * w : (g + 1) * w, :] = cross[:, far : far + lanes].astype(BF16)


def slice_kernel(cb_hbm, out_ref, sems, *, per):
    size = per // FETCHES
    copies = []
    for q in range(FETCHES):
        at = lax.axis_index("rep") * per + q * size
        copies.append(pltpu.make_async_copy(cb_hbm.at[pl.ds(at, size)], out_ref.at[pl.ds(q * size, size)], sems.at[q]))
        copies[-1].start()
    for copy in copies:
        copy.wait()


def turn_kernel(m0_ref, m1_ref, t0_ref, t1_ref, out_ref, buf):
    s, r = lax.axis_index("sub"), lax.axis_index("rep")
    w = m0_ref.shape[0]
    for k, (mine, theirs) in enumerate(((m0_ref, t0_ref), (m1_ref, t1_ref))):
        h = (s + k) % 2
        buf[pl.ds(pl.multiple_of((2 * h + r) * w, SUBDIM), w), :] = mine[...]
        buf[pl.ds(pl.multiple_of((2 * h + 1 - r) * w, SUBDIM), w), :] = theirs[...]
    out_ref[...] = buf[...].T


def final_kernel(*refs, n, per, total):
    pieces, (cb_ref, cross_hbm, new_hbm, buf, cross, new, sems) = refs[: 2 * n], refs[2 * n :]
    s, r, z = lax.axis_index("sub"), lax.axis_index("rep"), lax.axis_index("row")
    lanes = 128
    w = per * SUBDIM
    groups = cross.shape[0] // lanes
    halves = cb_ref.shape[2] // lanes
    near_rows = groups * w + halves * (w + SUBDIM)
    near, far = near_rows // n, groups * w // n
    for side in range(2):
        for i in range(n):
            ref = pieces[side * n + i]
            source = z ^ ((0,) + GATHER)[i]
            buf[side, pl.ds(pl.multiple_of(source * near, 8), near), :] = ref[:near].astype(F32)
            buf[side, pl.ds(pl.multiple_of(near_rows + source * far, 8), far), :] = ref[near:].astype(F32)

    copies = []
    first = groups * w
    for side in range(2):
        part = r if side == 0 else 1 - r
        for m in range(per):
            c = cb_ref[part * per + m]
            rows = [first + hf * w + m * SUBDIM for hf in range(halves)]
            sums = jnp.concatenate([buf[side, a : a + SUBDIM, :] for a in rows], axis=1)
            rows = [first + halves * w + hf * SUBDIM + m for hf in range(halves)]
            count = jnp.concatenate([buf[side, a : a + 1, :] for a in rows], axis=1)
            new[part * per + m] = (sums + c) / (count + 1.0)
    copies.append(pltpu.make_async_copy(new, new_hbm, sems.at[groups]))
    copies[-1].start()
    for g in range(groups):
        for h in range(2):
            for q in range(2):
                @pl.when((s == h) & (r == q))
                def _():
                    parts = []
                    for col in range(2):
                        start = (col ^ h) * near_rows + g * w
                        parts += [buf[rep ^ q, start : start + w, :] for rep in range(2)]
                    cross[g * lanes : (g + 1) * lanes, :] = jnp.concatenate(parts, axis=0).T * (1.0 / total)
        block = pl.ds(g * lanes, lanes)
        copies.append(pltpu.make_async_copy(cross.at[block], cross_hbm.at[block], sems.at[g]))
        copies[-1].start()
    for copy in copies:
        copy.wait()


def pieces_kernel(kept_ref, got_ref, *refs, n):
    outs, total = refs[:n], refs[n]
    z = lax.axis_index("row")
    total[...] = kept_ref[...] + got_ref[...].astype(F32)
    size = outs[0].shape[0]
    for out, d in zip(outs, (0,) + SCATTER):
        out[...] = total[pl.ds(pl.multiple_of((z ^ d) * size, 8), size), :].astype(out.dtype)


def exchange(x, n, d):
    return lax.ppermute(x, "row", [(i, i ^ d) for i in range(n)])


def on_device(vectors, rotation, codebooks):
    rows, width = vectors.shape
    subs, rows_n = 2, lax.axis_size("row")
    part = width // subs
    per = part // SUBDIM // 2
    w = per * SUBDIM
    codes = codebooks.shape[1]
    lanes = 128
    total = rows * rows_n * subs * 2
    swap = [(0, 1), (1, 0)]
    params = pltpu.CompilerParams(vmem_limit_bytes=VMEM_BYTES)
    small = pltpu.CompilerParams(vmem_limit_bytes=VMEM_BYTES // 2)
    vmem = pl.BlockSpec(memory_space=pltpu.VMEM)

    cb = codebooks.transpose(0, 2, 1)
    hbm = pl.BlockSpec(memory_space=pltpu.HBM)
    cb_sent = pl.pallas_call(
        functools.partial(slice_kernel, per=per),
        out_shape=jax.ShapeDtypeStruct((per,) + cb.shape[1:], F32),
        in_specs=[hbm],
        out_specs=vmem,
        scratch_shapes=[pltpu.SemaphoreType.DMA((FETCHES,))],
        compiler_params=small,
        name="slice",
    )(pltpu.with_memory_space_constraint(cb, pltpu.HBM))
    cb_far = lax.ppermute(cb_sent, "sub", swap)
    vec_far = lax.ppermute(vectors, "rep", swap)

    y_shape = jax.ShapeDtypeStruct((subs, w, rows), BF16)
    y0, rott, v0 = pl.pallas_call(
        rotate_kernel,
        out_shape=(
            y_shape,
            jax.ShapeDtypeStruct((subs, w, width), BF16),
            jax.ShapeDtypeStruct(vectors.shape, BF16),
        ),
        in_specs=[hbm] * 2,
        out_specs=(vmem,) * 3,
        scratch_shapes=[pltpu.VMEM(rotation.shape, BF16), pltpu.SemaphoreType.DMA((2 * FETCHES,))],
        compiler_params=small,
        name="rotate",
    )(*(pltpu.with_memory_space_constraint(x, pltpu.HBM) for x in (vectors, rotation)))
    p_rows = (part // lanes) * w
    s_rows = (codes // lanes) * (w + SUBDIM)
    rec_shape = jax.ShapeDtypeStruct((w, rows), BF16)

    cnt_shape = ((codes // lanes) * SUBDIM, lanes)

    def cost(count, cross):
        return pl.CostEstimate(
            flops=count * codes * rows * 2 * 2 * (9 * SUBDIM) + cross * 2 * w * 2 * rows * width,
            transcendentals=count * codes * rows * 2,
            bytes_accessed=2**23,
        )

    early = HEAD * SUBDIM

    def quantize(k, cb_k, y1, *head):
        n_keep, n_send = (p_rows + s_rows, p_rows) if k == 0 else (p_rows, p_rows + s_rows)
        out_shape = [
            rec_shape,
            rec_shape,
            jax.ShapeDtypeStruct((n_keep, lanes), F32),
            jax.ShapeDtypeStruct((n_send, lanes), BF16),
        ]
        first = 0 if k else HEAD
        return pl.pallas_call(
            functools.partial(quantize_kernel, k=k, per=per, first=first, last=per),
            in_specs=[vmem] * (5 + len(head)),
            out_specs=[vmem] * len(out_shape),
            out_shape=out_shape,
            scratch_shapes=[pltpu.VMEM(cnt_shape, F32)],
            compiler_params=params,
            cost_estimate=cost(per - first, 1),
            name="quantize_far" if k else "quantize_near",
        )(cb_k, y0, y1, v0, vec_far, *head)

    early_shape = jax.ShapeDtypeStruct((early, rows), BF16)
    *head, y1 = pl.pallas_call(
        functools.partial(quantize_kernel, k=0, per=per, first=0, last=HEAD),
        in_specs=[vmem] * 4,
        out_specs=[vmem] * 5,
        out_shape=[
            early_shape,
            early_shape,
            jax.ShapeDtypeStruct(((codes // lanes) * early, lanes), F32),
            jax.ShapeDtypeStruct(cnt_shape, F32),
            y_shape,
        ],
        compiler_params=params,
        cost_estimate=cost(HEAD, 0),
        name="quantize_head",
    )(cb, y0, vec_far, rott)

    cb_far, *head = lax.optimization_barrier((cb_far, *head))

    mine1, other1, keep1, send1 = quantize(1, cb_far, y1)
    got1 = lax.ppermute(send1, "sub", swap)
    theirs1 = lax.ppermute(other1, "rep", swap)
    mine0, other0, keep0, send0 = quantize(0, cb, y1, *head)
    got0 = lax.ppermute(send0, "sub", swap)
    other0, got1 = lax.optimization_barrier((other0, got1))
    theirs0 = lax.ppermute(other0, "rep", swap)

    reconstruction = pl.pallas_call(
        turn_kernel,
        out_shape=jax.ShapeDtypeStruct((rows, width), BF16),
        in_specs=[vmem] * 4,
        out_specs=vmem,
        scratch_shapes=[pltpu.VMEM((width, rows), BF16)],
        compiler_params=small,
        name="turn",
    )(mine0, mine1, theirs0, theirs1)

    def scatter(kept, got):
        size = (kept.shape[0] // rows_n, lanes)
        own, *sent = pl.pallas_call(
            functools.partial(pieces_kernel, n=rows_n),
            out_shape=[jax.ShapeDtypeStruct(size, F32)] + [jax.ShapeDtypeStruct(size, BF16)] * (rows_n - 1),
            in_specs=[vmem] * 2,
            out_specs=[vmem] * rows_n,
            scratch_shapes=[pltpu.VMEM(kept.shape, F32)],
            compiler_params=small,
            name="pieces",
        )(kept, got)
        return [own] + [exchange(x, rows_n, d) for x, d in zip(sent, SCATTER)]

    def add_up(parts):
        return functools.reduce(lambda a, b: a + b.astype(F32), parts[1:], parts[0]).astype(BF16)

    near = scatter(keep0, got1)
    near[0], got0, theirs1 = lax.optimization_barrier((near[0], got0, theirs1))
    summed = jnp.concatenate([add_up(near), add_up(scatter(keep1, got0))], axis=0)
    mine = [summed] + [exchange(summed, rows_n, d) for d in GATHER]
    mine[2], mine[3], reconstruction = lax.optimization_barrier((mine[2], mine[3], reconstruction))
    theirs = [lax.ppermute(x, "rep", swap) for x in mine]

    any_spec = pl.BlockSpec(memory_space=pl.ANY)
    cross, new = pl.pallas_call(
        functools.partial(final_kernel, n=rows_n, per=per, total=total),
        out_shape=(jax.ShapeDtypeStruct((part, width), F32), jax.ShapeDtypeStruct(cb.shape, F32)),
        in_specs=[vmem] * (2 * rows_n + 1),
        out_specs=(any_spec, any_spec),
        scratch_shapes=[
            pltpu.VMEM((2, 2 * p_rows + s_rows, lanes), F32),
            pltpu.VMEM((part, width), F32),
            pltpu.VMEM(cb.shape, F32),
            pltpu.SemaphoreType.DMA((part // lanes + 1,)),
        ],
        compiler_params=small,
        name="final",
    )(*mine, *theirs, cb)
    return reconstruction, new.transpose(0, 2, 1), cross


def solution(mesh):
    placed = (P(("dom", "row", "sub", "rep"), None), P("dom", None), P(("dom", "sub"), None, None))
    body = on_device if mesh.shape["sub"] == 2 and mesh.shape["row"] == 4 else any_mesh
    return jax.shard_map(
        body,
        mesh=mesh,
        in_specs=placed,
        out_specs=(
            P(("dom", "row", "sub", "rep"), None),
            P(("dom", "sub"), None, None),
            P(("dom", "sub"), None),
        ),
        check_vma=False,
    )
```

```python
import functools
import math

import jax
import jax.numpy as jnp
from jax import lax
from jax.experimental import pallas as pl
from jax.experimental.pallas import tpu as pltpu
from jax.sharding import PartitionSpec as P

SUBDIM = 16
SOFTNESS = 4.0
LOG2E = math.log2(math.e)
F32, BF16 = jnp.float32, jnp.bfloat16
VMEM_BYTES = 24 * 2**20
HEAD = 4
FETCHES = 4
SCATTER = (2, 3, 1)
GATHER = (1, 3, 2)


def quantize_rows(block, codebook):
    block = block.astype(F32)
    cross_product = jnp.dot(codebook, block, precision=lax.Precision.HIGHEST)
    squared_norms = jnp.sum(codebook * codebook, axis=1)
    affinity_scores = (2.0 * cross_product - squared_norms[:, None]) / SOFTNESS
    weights = jax.nn.softmax(affinity_scores, axis=0)
    recon = jnp.dot(codebook.T, weights, precision=lax.Precision.HIGHEST)
    sums = lax.dot_general(weights, block, (((1,), (1,)), ((), ())), precision=lax.Precision.HIGHEST)
    return recon, sums, jnp.sum(weights, axis=1)


def any_mesh(vectors, rotation, codebooks):
    rows, width = vectors.shape
    groups = lax.axis_size("sub")
    part = width // groups
    rotated_t = lax.dot_general(
        rotation, vectors, (((0,), (1,)), ((), ())), preferred_element_type=F32
    ).astype(BF16)
    received = lax.all_to_all(rotated_t.reshape(groups, part, rows), "sub", split_axis=0, concat_axis=2, tiled=True)
    columns = received.shape[2]
    blocks = received.reshape(part // SUBDIM, SUBDIM, columns)
    recon, sums, counts = lax.map(lambda pair: quantize_rows(pair[0], pair[1]), (blocks, codebooks))
    sent = recon.astype(BF16).reshape(1, part, columns)
    recon_t = lax.all_to_all(sent, "sub", split_axis=2, concat_axis=0, tiled=True).reshape(width, rows)
    total = rows * lax.axis_size("row") * groups * lax.axis_size("rep")
    sums, counts = lax.psum((sums, counts), ("row", "rep"))
    term = lax.dot_general(vectors, recon_t, (((0,), (1,)), ((), ())), preferred_element_type=F32)
    whole = lax.psum(term, ("row", "sub", "rep"))
    mine = lax.dynamic_slice_in_dim(whole, lax.axis_index("sub") * part, part, 0)
    return recon_t.T, (sums + codebooks) / (counts[:, :, None] + 1.0), mine / total


def rotate_kernel(vec_hbm, rot_hbm, y_ref, rott_ref, v_ref, rot, sems):
    s, r = lax.axis_index("sub"), lax.axis_index("rep")
    n, w = y_ref.shape[0], y_ref.shape[1]
    copies = []
    for source, target in ((rot_hbm, rot), (vec_hbm, v_ref)):
        size = source.shape[0] // FETCHES
        for q in range(FETCHES):
            block = pl.ds(q * size, size)
            copies.append(pltpu.make_async_copy(source.at[block], target.at[block], sems.at[len(copies)]))
            copies[-1].start()
    for copy in copies[:FETCHES]:
        copy.wait()
    for h in range(n):
        for q in range(2):
            @pl.when(r == q)
            def _():
                at = (2 * h + q) * w
                start = at // 128 * 128
                turned = rot[:, start : start + 256].T
                rott_ref[(h + n - s) % n] = turned[at - start : at - start + w]
    for copy in copies[FETCHES:]:
        copy.wait()
    for k in range(n):
        y_ref[k] = lax.dot_general(
            rott_ref[k], v_ref[...], (((1,), (1,)), ((), ())), preferred_element_type=F32
        ).astype(BF16)


def operands(c):
    codes = c.shape[1]
    scaled = c * (2.0 / SOFTNESS * LOG2E)
    hi = scaled.astype(BF16).astype(F32)
    mid = (scaled - hi).astype(BF16).astype(F32)
    lo = (scaled - hi) - mid
    n = jnp.sum(c * c, axis=0, keepdims=True) * (-LOG2E / SOFTNESS)
    n_hi = n.astype(BF16).astype(F32)
    n_mid = (n - n_hi).astype(BF16).astype(F32)
    n_lo = (n - n_hi) - n_mid
    row = lax.broadcasted_iota(jnp.int32, (SUBDIM, codes), 0)
    norms = jnp.where(row == 0, n_hi, jnp.where(row == 1, n_mid, jnp.where(row == 2, n_lo, 0.0)))
    a = jnp.concatenate([hi, mid, lo, norms], axis=0).T.astype(BF16)
    b = jnp.concatenate([c.astype(BF16), jnp.ones((SUBDIM, codes), BF16)], axis=0)
    return a, b


def quantize_kernel(*refs, k, per, first, last):
    cb_ref, y0_ref, y1_ref, *refs = refs
    s, r = lax.axis_index("sub"), lax.axis_index("rep")
    codes = cb_ref.shape[2]
    cols = y0_ref.shape[2]
    w = per * SUBDIM
    lanes = 128
    halves = codes // lanes
    whole = last == per
    base = r * per if k == 0 else 0
    if not whole:
        vec_ref = y1_ref
        rott_ref, rec0_ref, rec1_ref, sums_ref, cnt, y1_ref = refs
        for half in range(y1_ref.shape[0]):
            y1_ref[half] = lax.dot_general(
                rott_ref[half], vec_ref[...], (((1,), (1,)), ((), ())), preferred_element_type=F32
            ).astype(BF16)
        p_rows = 0
    else:
        v0_ref, v1_ref, *refs = refs
        part = v0_ref.shape[1] // 2
        p_rows = (part // lanes) * w
        *head, rec0_ref, rec1_ref, keep_ref, send_ref, cnt = refs
        sums_ref = keep_ref if k == 0 else send_ref
    stride = w if whole else last * SUBDIM
    ones = jnp.ones((SUBDIM, cols), BF16)
    ys, recs = (y0_ref, y1_ref), (rec0_ref, rec1_ref)
    if first:
        done = first * SUBDIM
        rec0_ref[:done, :] = head[0][...]
        rec1_ref[:done, :] = head[1][...]
        for half in range(halves):
            at = p_rows + half * stride
            sums_ref[at : at + done, :] = head[2][half * done : (half + 1) * done, :].astype(sums_ref.dtype)
        cnt[...] = head[3][...]
    else:
        cnt[...] = jnp.zeros_like(cnt)
    ab, acc = {}, {}

    def score(j, i):
        if j not in ab:
            ab[j] = operands(cb_ref[base + j])
        y = ys[i][k, SUBDIM * j : SUBDIM * (j + 1), :]
        return y, jnp.dot(ab[j][0], jnp.concatenate([y, y, y, ones], axis=0), preferred_element_type=F32)

    def spread(sc):
        return jnp.exp2(sc - jnp.max(sc, axis=0, keepdims=True)).astype(BF16)

    def rebuild(j, i, y, e):
        out = jnp.dot(ab[j][1], e, preferred_element_type=F32)
        inv = 1.0 / out[SUBDIM:]
        recs[i][SUBDIM * j : SUBDIM * (j + 1), :] = (out[:SUBDIM] * inv).astype(BF16)
        return jnp.concatenate([(y.astype(F32) * inv).astype(BF16), inv.astype(BF16)], axis=0)

    def gather(j, i, yz, e):
        sums = lax.dot_general(yz, e, (((1,), (1,)), ((), ())), preferred_element_type=F32)
        if i == 0:
            acc[j] = sums
            return
        sums = acc.pop(j) + sums
        for half in range(halves):
            at = p_rows + half * stride + j * SUBDIM
            sums_ref[at : at + SUBDIM, :] = sums[:SUBDIM, half * lanes : (half + 1) * lanes].astype(sums_ref.dtype)
            at = half * SUBDIM + j
            cnt[at : at + 1, :] = sums[SUBDIM : SUBDIM + 1, half * lanes : (half + 1) * lanes]

    one = two = three = None
    for item in [(j, i) for j in range(first, last) for i in range(2)] + [None] * 3:
        new_one = (item, *score(*item)) if item is not None else None
        new_two = (one[0], one[1], spread(one[2])) if one is not None else None
        new_three = (two[0], rebuild(*two[0], two[1], two[2]), two[2]) if two is not None else None
        if three is not None:
            gather(*three[0], three[1], three[2])
        one, two, three = new_one, new_two, new_three
    if not whole:
        return

    at = p_rows + halves * w
    sums_ref[at : at + cnt.shape[0], :] = cnt[...].astype(sums_ref.dtype)
    cross = jnp.dot(rec0_ref[...], v0_ref[...], preferred_element_type=F32) + jnp.dot(
        rec1_ref[...], v1_ref[...], preferred_element_type=F32
    )
    for h in range(2):
        @pl.when(s == h)
        def _():
            for g in range(part // lanes):
                near = h * part + g * lanes
                far = (1 - h) * part + g * lanes
                keep_ref[g * w : (g + 1) * w, :] = cross[:, near : near + lanes]
                send_ref[g * w : (g + 1) * w, :] = cross[:, far : far + lanes].astype(BF16)


def slice_kernel(cb_hbm, out_ref, sems, *, per):
    size = per // FETCHES
    copies = []
    for q in range(FETCHES):
        at = lax.axis_index("rep") * per + q * size
        copies.append(pltpu.make_async_copy(cb_hbm.at[pl.ds(at, size)], out_ref.at[pl.ds(q * size, size)], sems.at[q]))
        copies[-1].start()
    for copy in copies:
        copy.wait()


def turn_kernel(m0_ref, m1_ref, t0_ref, t1_ref, out_ref, buf):
    s, r = lax.axis_index("sub"), lax.axis_index("rep")
    w = m0_ref.shape[0]
    for k, (mine, theirs) in enumerate(((m0_ref, t0_ref), (m1_ref, t1_ref))):
        h = (s + k) % 2
        buf[pl.ds(pl.multiple_of((2 * h + r) * w, SUBDIM), w), :] = mine[...]
        buf[pl.ds(pl.multiple_of((2 * h + 1 - r) * w, SUBDIM), w), :] = theirs[...]
    out_ref[...] = buf[...].T


def final_kernel(*refs, n, per, total):
    pieces, (cb_ref, cross_hbm, new_hbm, buf, cross, new, sems) = refs[: 2 * n], refs[2 * n :]
    s, r, z = lax.axis_index("sub"), lax.axis_index("rep"), lax.axis_index("row")
    lanes = 128
    w = per * SUBDIM
    groups = cross.shape[0] // lanes
    halves = cb_ref.shape[2] // lanes
    near_rows = groups * w + halves * (w + SUBDIM)
    near, far = near_rows // n, groups * w // n
    for side in range(2):
        for i in range(n):
            ref = pieces[side * n + i]
            source = z ^ ((0,) + GATHER)[i]
            buf[side, pl.ds(pl.multiple_of(source * near, 8), near), :] = ref[:near].astype(F32)
            buf[side, pl.ds(pl.multiple_of(near_rows + source * far, 8), far), :] = ref[near:].astype(F32)

    copies = []
    first = groups * w
    for side in range(2):
        part = r if side == 0 else 1 - r
        for m in range(per):
            c = cb_ref[part * per + m]
            rows = [first + hf * w + m * SUBDIM for hf in range(halves)]
            sums = jnp.concatenate([buf[side, a : a + SUBDIM, :] for a in rows], axis=1)
            rows = [first + halves * w + hf * SUBDIM + m for hf in range(halves)]
            count = jnp.concatenate([buf[side, a : a + 1, :] for a in rows], axis=1)
            new[part * per + m] = (sums + c) / (count + 1.0)
    for q in range(2):
        block = pl.ds(q * per, per)
        copies.append(pltpu.make_async_copy(new.at[block], new_hbm.at[block], sems.at[2 * groups + q]))
        copies[-1].start()
    for g in range(groups):
        for h in range(2):
            for q in range(2):
                @pl.when((s == h) & (r == q))
                def _():
                    parts = []
                    for col in range(2):
                        start = (col ^ h) * near_rows + g * w
                        parts += [buf[rep ^ q, start : start + w, :] for rep in range(2)]
                    cross[g * lanes : (g + 1) * lanes, :] = jnp.concatenate(parts, axis=0).T * (1.0 / total)
        for q in range(2):
            block = pl.ds(g * lanes + q * (lanes // 2), lanes // 2)
            copies.append(pltpu.make_async_copy(cross.at[block], cross_hbm.at[block], sems.at[2 * g + q]))
            copies[-1].start()
    for copy in copies:
        copy.wait()


def pieces_kernel(kept_ref, got_ref, *refs, n):
    outs, total = refs[:n], refs[n]
    z = lax.axis_index("row")
    total[...] = kept_ref[...] + got_ref[...].astype(F32)
    size = outs[0].shape[0]
    for out, d in zip(outs, (0,) + SCATTER):
        out[...] = total[pl.ds(pl.multiple_of((z ^ d) * size, 8), size), :].astype(out.dtype)


def exchange(x, n, d):
    return lax.ppermute(x, "row", [(i, i ^ d) for i in range(n)])


def on_device(vectors, rotation, codebooks):
    rows, width = vectors.shape
    subs, rows_n = 2, lax.axis_size("row")
    part = width // subs
    per = part // SUBDIM // 2
    w = per * SUBDIM
    codes = codebooks.shape[1]
    lanes = 128
    total = rows * rows_n * subs * 2
    swap = [(0, 1), (1, 0)]
    params = pltpu.CompilerParams(vmem_limit_bytes=VMEM_BYTES)
    small = pltpu.CompilerParams(vmem_limit_bytes=VMEM_BYTES // 2)
    vmem = pl.BlockSpec(memory_space=pltpu.VMEM)

    cb = codebooks.transpose(0, 2, 1)
    hbm = pl.BlockSpec(memory_space=pltpu.HBM)
    cb_sent = pl.pallas_call(
        functools.partial(slice_kernel, per=per),
        out_shape=jax.ShapeDtypeStruct((per,) + cb.shape[1:], F32),
        in_specs=[hbm],
        out_specs=vmem,
        scratch_shapes=[pltpu.SemaphoreType.DMA((FETCHES,))],
        compiler_params=small,
        name="slice",
    )(pltpu.with_memory_space_constraint(cb, pltpu.HBM))
    cb_far = lax.ppermute(cb_sent, "sub", swap)
    vec_far = lax.ppermute(vectors, "rep", swap)

    y_shape = jax.ShapeDtypeStruct((subs, w, rows), BF16)
    y0, rott, v0 = pl.pallas_call(
        rotate_kernel,
        out_shape=(
            y_shape,
            jax.ShapeDtypeStruct((subs, w, width), BF16),
            jax.ShapeDtypeStruct(vectors.shape, BF16),
        ),
        in_specs=[hbm] * 2,
        out_specs=(vmem,) * 3,
        scratch_shapes=[pltpu.VMEM(rotation.shape, BF16), pltpu.SemaphoreType.DMA((2 * FETCHES,))],
        compiler_params=small,
        name="rotate",
    )(*(pltpu.with_memory_space_constraint(x, pltpu.HBM) for x in (vectors, rotation)))
    p_rows = (part // lanes) * w
    s_rows = (codes // lanes) * (w + SUBDIM)
    rec_shape = jax.ShapeDtypeStruct((w, rows), BF16)

    cnt_shape = ((codes // lanes) * SUBDIM, lanes)

    def cost(count, cross):
        return pl.CostEstimate(
            flops=count * codes * rows * 2 * 2 * (9 * SUBDIM) + cross * 2 * w * 2 * rows * width,
            transcendentals=count * codes * rows * 2,
            bytes_accessed=2**23,
        )

    early = HEAD * SUBDIM

    def quantize(k, cb_k, y1, *head):
        n_keep, n_send = (p_rows + s_rows, p_rows) if k == 0 else (p_rows, p_rows + s_rows)
        out_shape = [
            rec_shape,
            rec_shape,
            jax.ShapeDtypeStruct((n_keep, lanes), F32),
            jax.ShapeDtypeStruct((n_send, lanes), BF16),
        ]
        first = 0 if k else HEAD
        return pl.pallas_call(
            functools.partial(quantize_kernel, k=k, per=per, first=first, last=per),
            in_specs=[vmem] * (5 + len(head)),
            out_specs=[vmem] * len(out_shape),
            out_shape=out_shape,
            scratch_shapes=[pltpu.VMEM(cnt_shape, F32)],
            compiler_params=params,
            cost_estimate=cost(per - first, 1),
            name="quantize_far" if k else "quantize_near",
        )(cb_k, y0, y1, v0, vec_far, *head)

    early_shape = jax.ShapeDtypeStruct((early, rows), BF16)
    *head, y1 = pl.pallas_call(
        functools.partial(quantize_kernel, k=0, per=per, first=0, last=HEAD),
        in_specs=[vmem] * 4,
        out_specs=[vmem] * 5,
        out_shape=[
            early_shape,
            early_shape,
            jax.ShapeDtypeStruct(((codes // lanes) * early, lanes), F32),
            jax.ShapeDtypeStruct(cnt_shape, F32),
            y_shape,
        ],
        compiler_params=params,
        cost_estimate=cost(HEAD, 0),
        name="quantize_head",
    )(cb, y0, vec_far, rott)

    cb_far, *head = lax.optimization_barrier((cb_far, *head))

    mine1, other1, keep1, send1 = quantize(1, cb_far, y1)
    got1 = lax.ppermute(send1, "sub", swap)
    theirs1 = lax.ppermute(other1, "rep", swap)
    mine0, other0, keep0, send0 = quantize(0, cb, y1, *head)
    got0 = lax.ppermute(send0, "sub", swap)
    other0, got1 = lax.optimization_barrier((other0, got1))
    theirs0 = lax.ppermute(other0, "rep", swap)

    reconstruction = pl.pallas_call(
        turn_kernel,
        out_shape=jax.ShapeDtypeStruct((rows, width), BF16),
        in_specs=[vmem] * 4,
        out_specs=vmem,
        scratch_shapes=[pltpu.VMEM((width, rows), BF16)],
        compiler_params=small,
        name="turn",
    )(mine0, mine1, theirs0, theirs1)

    def scatter(kept, got):
        size = (kept.shape[0] // rows_n, lanes)
        own, *sent = pl.pallas_call(
            functools.partial(pieces_kernel, n=rows_n),
            out_shape=[jax.ShapeDtypeStruct(size, F32)] + [jax.ShapeDtypeStruct(size, BF16)] * (rows_n - 1),
            in_specs=[vmem] * 2,
            out_specs=[vmem] * rows_n,
            scratch_shapes=[pltpu.VMEM(kept.shape, F32)],
            compiler_params=small,
            name="pieces",
        )(kept, got)
        return [own] + [exchange(x, rows_n, d) for x, d in zip(sent, SCATTER)]

    def add_up(parts):
        return functools.reduce(lambda a, b: a + b.astype(F32), parts[1:], parts[0]).astype(BF16)

    near = scatter(keep0, got1)
    near[0], got0, theirs1 = lax.optimization_barrier((near[0], got0, theirs1))
    summed = jnp.concatenate([add_up(near), add_up(scatter(keep1, got0))], axis=0)
    mine = [summed] + [exchange(summed, rows_n, d) for d in GATHER]
    mine[2], mine[3], reconstruction = lax.optimization_barrier((mine[2], mine[3], reconstruction))
    theirs = [lax.ppermute(x, "rep", swap) for x in mine]

    any_spec = pl.BlockSpec(memory_space=pl.ANY)
    cross, new = pl.pallas_call(
        functools.partial(final_kernel, n=rows_n, per=per, total=total),
        out_shape=(jax.ShapeDtypeStruct((part, width), F32), jax.ShapeDtypeStruct(cb.shape, F32)),
        in_specs=[vmem] * (2 * rows_n + 1),
        out_specs=(any_spec, any_spec),
        scratch_shapes=[
            pltpu.VMEM((2, 2 * p_rows + s_rows, lanes), F32),
            pltpu.VMEM((part, width), F32),
            pltpu.VMEM(cb.shape, F32),
            pltpu.SemaphoreType.DMA((2 * (part // lanes) + 2,)),
        ],
        compiler_params=small,
        name="final",
    )(*mine, *theirs, cb)
    return reconstruction, new.transpose(0, 2, 1), cross


def solution(mesh):
    placed = (P(("dom", "row", "sub", "rep"), None), P("dom", None), P(("dom", "sub"), None, None))
    body = on_device if mesh.shape["sub"] == 2 and mesh.shape["row"] == 4 else any_mesh
    return jax.shard_map(
        body,
        mesh=mesh,
        in_specs=placed,
        out_specs=(
            P(("dom", "row", "sub", "rep"), None),
            P(("dom", "sub"), None, None),
            P(("dom", "sub"), None),
        ),
        check_vma=False,
    )
```

```python
import functools
import math

import jax
import jax.numpy as jnp
from jax import lax
from jax.experimental import pallas as pl
from jax.experimental.pallas import tpu as pltpu
from jax.sharding import PartitionSpec as P

SUBDIM = 16
SOFTNESS = 4.0
LOG2E = math.log2(math.e)
F32, BF16 = jnp.float32, jnp.bfloat16
VMEM_BYTES = 24 * 2**20
HEAD = 4
FETCHES = 4
SCATTER = (2, 3, 1)
LATER = (3, 2, 1)
GATHER = (1, 3, 2)


def quantize_rows(block, codebook):
    block = block.astype(F32)
    cross_product = jnp.dot(codebook, block, precision=lax.Precision.HIGHEST)
    squared_norms = jnp.sum(codebook * codebook, axis=1)
    affinity_scores = (2.0 * cross_product - squared_norms[:, None]) / SOFTNESS
    weights = jax.nn.softmax(affinity_scores, axis=0)
    recon = jnp.dot(codebook.T, weights, precision=lax.Precision.HIGHEST)
    sums = lax.dot_general(weights, block, (((1,), (1,)), ((), ())), precision=lax.Precision.HIGHEST)
    return recon, sums, jnp.sum(weights, axis=1)


def any_mesh(vectors, rotation, codebooks):
    rows, width = vectors.shape
    groups = lax.axis_size("sub")
    part = width // groups
    rotated_t = lax.dot_general(
        rotation, vectors, (((0,), (1,)), ((), ())), preferred_element_type=F32
    ).astype(BF16)
    received = lax.all_to_all(rotated_t.reshape(groups, part, rows), "sub", split_axis=0, concat_axis=2, tiled=True)
    columns = received.shape[2]
    blocks = received.reshape(part // SUBDIM, SUBDIM, columns)
    recon, sums, counts = lax.map(lambda pair: quantize_rows(pair[0], pair[1]), (blocks, codebooks))
    sent = recon.astype(BF16).reshape(1, part, columns)
    recon_t = lax.all_to_all(sent, "sub", split_axis=2, concat_axis=0, tiled=True).reshape(width, rows)
    total = rows * lax.axis_size("row") * groups * lax.axis_size("rep")
    sums, counts = lax.psum((sums, counts), ("row", "rep"))
    term = lax.dot_general(vectors, recon_t, (((0,), (1,)), ((), ())), preferred_element_type=F32)
    whole = lax.psum(term, ("row", "sub", "rep"))
    mine = lax.dynamic_slice_in_dim(whole, lax.axis_index("sub") * part, part, 0)
    return recon_t.T, (sums + codebooks) / (counts[:, :, None] + 1.0), mine / total


def rotate_kernel(vec_hbm, rot_hbm, y_ref, rott_ref, v_ref, rot, sems):
    s, r = lax.axis_index("sub"), lax.axis_index("rep")
    n, w = y_ref.shape[0], y_ref.shape[1]
    copies = []
    for source, target in ((rot_hbm, rot), (vec_hbm, v_ref)):
        size = source.shape[0] // FETCHES
        for q in range(FETCHES):
            block = pl.ds(q * size, size)
            copies.append(pltpu.make_async_copy(source.at[block], target.at[block], sems.at[len(copies)]))
            copies[-1].start()
    for copy in copies[:FETCHES]:
        copy.wait()
    for h in range(n):
        for q in range(2):
            @pl.when(r == q)
            def _():
                at = (2 * h + q) * w
                start = at // 128 * 128
                turned = rot[:, start : start + 256].T
                rott_ref[(h + n - s) % n] = turned[at - start : at - start + w]
    for copy in copies[FETCHES:]:
        copy.wait()
    for k in range(n):
        y_ref[k] = lax.dot_general(
            rott_ref[k], v_ref[...], (((1,), (1,)), ((), ())), preferred_element_type=F32
        ).astype(BF16)


def operands(c):
    codes = c.shape[1]
    scaled = c * (2.0 / SOFTNESS * LOG2E)
    hi = scaled.astype(BF16).astype(F32)
    mid = (scaled - hi).astype(BF16).astype(F32)
    lo = (scaled - hi) - mid
    n = jnp.sum(c * c, axis=0, keepdims=True) * (-LOG2E / SOFTNESS)
    n_hi = n.astype(BF16).astype(F32)
    n_mid = (n - n_hi).astype(BF16).astype(F32)
    n_lo = (n - n_hi) - n_mid
    row = lax.broadcasted_iota(jnp.int32, (SUBDIM, codes), 0)
    norms = jnp.where(row == 0, n_hi, jnp.where(row == 1, n_mid, jnp.where(row == 2, n_lo, 0.0)))
    a = jnp.concatenate([hi, mid, lo, norms], axis=0).T.astype(BF16)
    b = jnp.concatenate([c.astype(BF16), jnp.ones((SUBDIM, codes), BF16)], axis=0)
    return a, b


def quantize_kernel(*refs, k, per, first, last):
    cb_ref, y0_ref, y1_ref, *refs = refs
    s, r = lax.axis_index("sub"), lax.axis_index("rep")
    codes = cb_ref.shape[2]
    cols = y0_ref.shape[2]
    w = per * SUBDIM
    lanes = 128
    halves = codes // lanes
    whole = last == per
    base = r * per if k == 0 else 0
    if not whole:
        vec_ref = y1_ref
        rott_ref, rec0_ref, rec1_ref, sums_ref, cnt, y1_ref = refs
        for half in range(y1_ref.shape[0]):
            y1_ref[half] = lax.dot_general(
                rott_ref[half], vec_ref[...], (((1,), (1,)), ((), ())), preferred_element_type=F32
            ).astype(BF16)
        p_rows = 0
    else:
        v0_ref, v1_ref, *refs = refs
        part = v0_ref.shape[1] // 2
        p_rows = (part // lanes) * w
        *head, rec0_ref, rec1_ref, keep_ref, send_ref, cnt = refs
        sums_ref = keep_ref if k == 0 else send_ref
    stride = w if whole else last * SUBDIM
    ones = jnp.ones((SUBDIM, cols), BF16)
    ys, recs = (y0_ref, y1_ref), (rec0_ref, rec1_ref)
    if first:
        done = first * SUBDIM
        rec0_ref[:done, :] = head[0][...]
        rec1_ref[:done, :] = head[1][...]
        for half in range(halves):
            at = p_rows + half * stride
            sums_ref[at : at + done, :] = head[2][half * done : (half + 1) * done, :].astype(sums_ref.dtype)
        cnt[...] = head[3][...]
    else:
        cnt[...] = jnp.zeros_like(cnt)
    ab, acc = {}, {}

    def score(j, i):
        if j not in ab:
            ab[j] = operands(cb_ref[base + j])
        y = ys[i][k, SUBDIM * j : SUBDIM * (j + 1), :]
        return y, jnp.dot(ab[j][0], jnp.concatenate([y, y, y, ones], axis=0), preferred_element_type=F32)

    def spread(sc):
        return jnp.exp2(sc - jnp.max(sc, axis=0, keepdims=True)).astype(BF16)

    def rebuild(j, i, y, e):
        out = jnp.dot(ab[j][1], e, preferred_element_type=F32)
        inv = 1.0 / out[SUBDIM:]
        recs[i][SUBDIM * j : SUBDIM * (j + 1), :] = (out[:SUBDIM] * inv).astype(BF16)
        return jnp.concatenate([(y.astype(F32) * inv).astype(BF16), inv.astype(BF16)], axis=0)

    def gather(j, i, yz, e):
        sums = lax.dot_general(yz, e, (((1,), (1,)), ((), ())), preferred_element_type=F32)
        if i == 0:
            acc[j] = sums
            return
        sums = acc.pop(j) + sums
        for half in range(halves):
            at = p_rows + half * stride + j * SUBDIM
            sums_ref[at : at + SUBDIM, :] = sums[:SUBDIM, half * lanes : (half + 1) * lanes].astype(sums_ref.dtype)
            at = half * SUBDIM + j
            cnt[at : at + 1, :] = sums[SUBDIM : SUBDIM + 1, half * lanes : (half + 1) * lanes]

    one = two = three = None
    for item in [(j, i) for j in range(first, last) for i in range(2)] + [None] * 3:
        new_one = (item, *score(*item)) if item is not None else None
        new_two = (one[0], one[1], spread(one[2])) if one is not None else None
        new_three = (two[0], rebuild(*two[0], two[1], two[2]), two[2]) if two is not None else None
        if three is not None:
            gather(*three[0], three[1], three[2])
        one, two, three = new_one, new_two, new_three
    if not whole:
        return

    at = p_rows + halves * w
    sums_ref[at : at + cnt.shape[0], :] = cnt[...].astype(sums_ref.dtype)
    cross = jnp.dot(rec0_ref[...], v0_ref[...], preferred_element_type=F32) + jnp.dot(
        rec1_ref[...], v1_ref[...], preferred_element_type=F32
    )
    for h in range(2):
        @pl.when(s == h)
        def _():
            for g in range(part // lanes):
                near = h * part + g * lanes
                far = (1 - h) * part + g * lanes
                keep_ref[g * w : (g + 1) * w, :] = cross[:, near : near + lanes]
                send_ref[g * w : (g + 1) * w, :] = cross[:, far : far + lanes].astype(BF16)


def slice_kernel(cb_hbm, out_ref, sems, *, per):
    size = per // FETCHES
    copies = []
    for q in range(FETCHES):
        at = lax.axis_index("rep") * per + q * size
        copies.append(pltpu.make_async_copy(cb_hbm.at[pl.ds(at, size)], out_ref.at[pl.ds(q * size, size)], sems.at[q]))
        copies[-1].start()
    for copy in copies:
        copy.wait()


def turn_kernel(m0_ref, m1_ref, t0_ref, t1_ref, out_ref, buf):
    s, r = lax.axis_index("sub"), lax.axis_index("rep")
    w = m0_ref.shape[0]
    for k, (mine, theirs) in enumerate(((m0_ref, t0_ref), (m1_ref, t1_ref))):
        h = (s + k) % 2
        buf[pl.ds(pl.multiple_of((2 * h + r) * w, SUBDIM), w), :] = mine[...]
        buf[pl.ds(pl.multiple_of((2 * h + 1 - r) * w, SUBDIM), w), :] = theirs[...]
    out_ref[...] = buf[...].T


def final_kernel(*refs, n, per, total):
    pieces, (cb_ref, cross_hbm, new_hbm, buf, cross, new, sems) = refs[: 2 * n], refs[2 * n :]
    s, r, z = lax.axis_index("sub"), lax.axis_index("rep"), lax.axis_index("row")
    lanes = 128
    w = per * SUBDIM
    groups = cross.shape[0] // lanes
    halves = cb_ref.shape[2] // lanes
    near_rows = groups * w + halves * (w + SUBDIM)
    near, far = near_rows // n, groups * w // n
    for side in range(2):
        for i in range(n):
            ref = pieces[side * n + i]
            source = z ^ ((0,) + GATHER)[i]
            buf[side, pl.ds(pl.multiple_of(source * near, 8), near), :] = ref[:near].astype(F32)
            buf[side, pl.ds(pl.multiple_of(near_rows + source * far, 8), far), :] = ref[near:].astype(F32)

    copies = []
    first = groups * w
    for side in range(2):
        part = r if side == 0 else 1 - r
        for m in range(per):
            c = cb_ref[part * per + m]
            rows = [first + hf * w + m * SUBDIM for hf in range(halves)]
            sums = jnp.concatenate([buf[side, a : a + SUBDIM, :] for a in rows], axis=1)
            rows = [first + halves * w + hf * SUBDIM + m for hf in range(halves)]
            count = jnp.concatenate([buf[side, a : a + 1, :] for a in rows], axis=1)
            new[part * per + m] = (sums + c) / (count + 1.0)
    copies.append(pltpu.make_async_copy(new, new_hbm, sems.at[groups]))
    copies[-1].start()
    for g in range(groups):
        for h in range(2):
            for q in range(2):
                @pl.when((s == h) & (r == q))
                def _():
                    parts = []
                    for col in range(2):
                        start = (col ^ h) * near_rows + g * w
                        parts += [buf[rep ^ q, start : start + w, :] for rep in range(2)]
                    cross[g * lanes : (g + 1) * lanes, :] = jnp.concatenate(parts, axis=0).T * (1.0 / total)
        block = pl.ds(g * lanes, lanes)
        copies.append(pltpu.make_async_copy(cross.at[block], cross_hbm.at[block], sems.at[g]))
        copies[-1].start()
    for copy in copies:
        copy.wait()


def pieces_kernel(kept_ref, got_ref, *refs, n, order):
    outs, total = refs[:n], refs[n]
    z = lax.axis_index("row")
    total[...] = kept_ref[...] + got_ref[...].astype(F32)
    size = outs[0].shape[0]
    for out, d in zip(outs, (0,) + order):
        out[...] = total[pl.ds(pl.multiple_of((z ^ d) * size, 8), size), :].astype(out.dtype)


def exchange(x, n, d):
    return lax.ppermute(x, "row", [(i, i ^ d) for i in range(n)])


def on_device(vectors, rotation, codebooks):
    rows, width = vectors.shape
    subs, rows_n = 2, lax.axis_size("row")
    part = width // subs
    per = part // SUBDIM // 2
    w = per * SUBDIM
    codes = codebooks.shape[1]
    lanes = 128
    total = rows * rows_n * subs * 2
    swap = [(0, 1), (1, 0)]
    params = pltpu.CompilerParams(vmem_limit_bytes=VMEM_BYTES)
    small = pltpu.CompilerParams(vmem_limit_bytes=VMEM_BYTES // 2)
    vmem = pl.BlockSpec(memory_space=pltpu.VMEM)

    cb = codebooks.transpose(0, 2, 1)
    hbm = pl.BlockSpec(memory_space=pltpu.HBM)
    cb_sent = pl.pallas_call(
        functools.partial(slice_kernel, per=per),
        out_shape=jax.ShapeDtypeStruct((per,) + cb.shape[1:], F32),
        in_specs=[hbm],
        out_specs=vmem,
        scratch_shapes=[pltpu.SemaphoreType.DMA((FETCHES,))],
        compiler_params=small,
        name="slice",
    )(pltpu.with_memory_space_constraint(cb, pltpu.HBM))
    cb_far = lax.ppermute(cb_sent, "sub", swap)
    vec_far = lax.ppermute(vectors, "rep", swap)

    y_shape = jax.ShapeDtypeStruct((subs, w, rows), BF16)
    y0, rott, v0 = pl.pallas_call(
        rotate_kernel,
        out_shape=(
            y_shape,
            jax.ShapeDtypeStruct((subs, w, width), BF16),
            jax.ShapeDtypeStruct(vectors.shape, BF16),
        ),
        in_specs=[hbm] * 2,
        out_specs=(vmem,) * 3,
        scratch_shapes=[pltpu.VMEM(rotation.shape, BF16), pltpu.SemaphoreType.DMA((2 * FETCHES,))],
        compiler_params=small,
        name="rotate",
    )(*(pltpu.with_memory_space_constraint(x, pltpu.HBM) for x in (vectors, rotation)))
    p_rows = (part // lanes) * w
    s_rows = (codes // lanes) * (w + SUBDIM)
    rec_shape = jax.ShapeDtypeStruct((w, rows), BF16)

    cnt_shape = ((codes // lanes) * SUBDIM, lanes)

    def cost(count, cross):
        return pl.CostEstimate(
            flops=count * codes * rows * 2 * 2 * (9 * SUBDIM) + cross * 2 * w * 2 * rows * width,
            transcendentals=count * codes * rows * 2,
            bytes_accessed=2**23,
        )

    early = HEAD * SUBDIM

    def quantize(k, cb_k, y1, *head):
        n_keep, n_send = (p_rows + s_rows, p_rows) if k == 0 else (p_rows, p_rows + s_rows)
        out_shape = [
            rec_shape,
            rec_shape,
            jax.ShapeDtypeStruct((n_keep, lanes), F32),
            jax.ShapeDtypeStruct((n_send, lanes), BF16),
        ]
        first = 0 if k else HEAD
        return pl.pallas_call(
            functools.partial(quantize_kernel, k=k, per=per, first=first, last=per),
            in_specs=[vmem] * (5 + len(head)),
            out_specs=[vmem] * len(out_shape),
            out_shape=out_shape,
            scratch_shapes=[pltpu.VMEM(cnt_shape, F32)],
            compiler_params=params,
            cost_estimate=cost(per - first, 1),
            name="quantize_far" if k else "quantize_near",
        )(cb_k, y0, y1, v0, vec_far, *head)

    early_shape = jax.ShapeDtypeStruct((early, rows), BF16)
    *head, y1 = pl.pallas_call(
        functools.partial(quantize_kernel, k=0, per=per, first=0, last=HEAD),
        in_specs=[vmem] * 4,
        out_specs=[vmem] * 5,
        out_shape=[
            early_shape,
            early_shape,
            jax.ShapeDtypeStruct(((codes // lanes) * early, lanes), F32),
            jax.ShapeDtypeStruct(cnt_shape, F32),
            y_shape,
        ],
        compiler_params=params,
        cost_estimate=cost(HEAD, 0),
        name="quantize_head",
    )(cb, y0, vec_far, rott)

    cb_far, *head = lax.optimization_barrier((cb_far, *head))

    mine1, other1, keep1, send1 = quantize(1, cb_far, y1)
    got1 = lax.ppermute(send1, "sub", swap)
    theirs1 = lax.ppermute(other1, "rep", swap)
    mine0, other0, keep0, send0 = quantize(0, cb, y1, *head)
    got0 = lax.ppermute(send0, "sub", swap)
    other0, got1 = lax.optimization_barrier((other0, got1))
    theirs0 = lax.ppermute(other0, "rep", swap)

    reconstruction = pl.pallas_call(
        turn_kernel,
        out_shape=jax.ShapeDtypeStruct((rows, width), BF16),
        in_specs=[vmem] * 4,
        out_specs=vmem,
        scratch_shapes=[pltpu.VMEM((width, rows), BF16)],
        compiler_params=small,
        name="turn",
    )(mine0, mine1, theirs0, theirs1)

    def scatter(kept, got, order):
        size = (kept.shape[0] // rows_n, lanes)
        own, *sent = pl.pallas_call(
            functools.partial(pieces_kernel, n=rows_n, order=order),
            out_shape=[jax.ShapeDtypeStruct(size, F32)] + [jax.ShapeDtypeStruct(size, BF16)] * (rows_n - 1),
            in_specs=[vmem] * 2,
            out_specs=[vmem] * rows_n,
            scratch_shapes=[pltpu.VMEM(kept.shape, F32)],
            compiler_params=small,
            name="pieces",
        )(kept, got)
        return [own] + [exchange(x, rows_n, d) for x, d in zip(sent, order)]

    def add_up(parts):
        return functools.reduce(lambda a, b: a + b.astype(F32), parts[1:], parts[0]).astype(BF16)

    near = scatter(keep0, got1, SCATTER)
    near[0], got0, theirs1 = lax.optimization_barrier((near[0], got0, theirs1))
    summed = jnp.concatenate([add_up(near), add_up(scatter(keep1, got0, LATER))], axis=0)
    mine = [summed] + [exchange(summed, rows_n, d) for d in GATHER]
    mine[2], mine[3], reconstruction = lax.optimization_barrier((mine[2], mine[3], reconstruction))
    theirs = [lax.ppermute(x, "rep", swap) for x in mine]

    any_spec = pl.BlockSpec(memory_space=pl.ANY)
    cross, new = pl.pallas_call(
        functools.partial(final_kernel, n=rows_n, per=per, total=total),
        out_shape=(jax.ShapeDtypeStruct((part, width), F32), jax.ShapeDtypeStruct(cb.shape, F32)),
        in_specs=[vmem] * (2 * rows_n + 1),
        out_specs=(any_spec, any_spec),
        scratch_shapes=[
            pltpu.VMEM((2, 2 * p_rows + s_rows, lanes), F32),
            pltpu.VMEM((part, width), F32),
            pltpu.VMEM(cb.shape, F32),
            pltpu.SemaphoreType.DMA((part // lanes + 1,)),
        ],
        compiler_params=small,
        name="final",
    )(*mine, *theirs, cb)
    return reconstruction, new.transpose(0, 2, 1), cross


def solution(mesh):
    placed = (P(("dom", "row", "sub", "rep"), None), P("dom", None), P(("dom", "sub"), None, None))
    body = on_device if mesh.shape["sub"] == 2 and mesh.shape["row"] == 4 else any_mesh
    return jax.shard_map(
        body,
        mesh=mesh,
        in_specs=placed,
        out_specs=(
            P(("dom", "row", "sub", "rep"), None),
            P(("dom", "sub"), None, None),
            P(("dom", "sub"), None),
        ),
        check_vma=False,
    )
```
